32 devices in a mesh: facet: 4 (over z), pol: 4 (over y, x), tm: 2 (over core).
Axes of the slice: x: 2, y: 2, z: 4, core: 2. Of those that a mesh axis runs over, the one named last changes fastest.
Arguments:
- tile_spectral_lines: bfloat16 [64, 4, 2, 64, 4096], P('facet', 'pol', None, 'tm'), may hold values from -6 to 6
- taper_leading_axis: bfloat16 [4, 2, 128, 512], P('facet', 'tm'), may hold values from -0.25 to 0.25
- taper_trailing_axis: bfloat16 [4, 2, 128, 512], P('facet', 'tm'), may hold values from -0.25 to 0.25
- depth_layer_factors: bfloat16 [4, 2, 2, 128], P('facet', 'tm'), may hold values from -4 to 4
- measured_correlations: float32 [4, 8, 2, 128], P('facet', None, 'tm', 'pol'), may hold values from -6 to 6
- visibility_groups_table: int32 [4, 2, 3, 8], P('facet', 'tm'), may hold values from 0 to 130815, as said below
- antenna_links: int32 [2, 130816], replicated, may hold values from 0 to 511, as said below
- complex_receiver_factors: float32 [256, 4, 512], replicated, may hold values from -5 to 5
Outputs:
- residual: float32 [4, 8, 2, 128], P('facet', None, 'tm', 'pol')
- gain_grad: float32 [512, 1024], P(('facet', 'pol', 'tm'))
The draws below stay inside these ranges and needn't reach their ends.
Inputs may be any that keep to these rules, and one draw needn't show every extreme that they name: `visibility_groups_table`: for each subgrid and owner, every block has a channel below 256, a count of 1 or more, and baselines offset to offset + count - 1 below 130816; the counts of one owner sum to at most 128, and some owner reaches 128 in every draw. `antenna_links`: each baseline joins two different stations.
All inputs are finite; a program needn't handle non-finite values.
Results may differ from the reference program's by a relative error of at most 0.012.
Values may be sent and summed in bfloat16 or wider, within the bound.
A program may use at most 192 MiB of HBM per device.

```python
import math
import jax
import jax.numpy as jnp
import numpy as np
from jax import lax

FGRID = 8
NF = 64
FS = 4096
MC = 64
SG = 512
NPOL = 4
NW = 2
NSUB = 4
TMO = 2
VT = 128
NBLK = 8
NCH = 256
NST = 512
NBASE = 130816


def draw_visibility_groups_table(key, part):
    subkeys = jax.random.split(jax.random.fold_in(key, 4101), 5)
    owners_all = NSUB * TMO
    raw_draw = jax.random.randint(subkeys[0], (owners_all,), 0, VT + 1)
    base_load = VT // 16
    owner_loads = base_load + raw_draw * raw_draw * (VT - base_load) // (VT * VT)
    chosen = jax.random.randint(subkeys[1], (), 0, owners_all)
    owner_loads = jnp.where(jnp.arange(owners_all) == chosen, VT, owner_loads)
    weights = jax.random.randint(subkeys[2], (owners_all, NBLK), 1, 17)
    spare_load = owner_loads - NBLK
    amounts = 1 + spare_load[:, None] * weights // jnp.sum(weights, axis=1, keepdims=True)
    amounts = amounts.at[:, NBLK - 1].set(owner_loads - jnp.sum(amounts[:, :NBLK - 1], axis=1))
    channels = jax.random.randint(subkeys[3], (owners_all, NBLK), 0, NCH)
    offsets = jax.random.randint(subkeys[4], (owners_all, NBLK), 0, NBASE - VT + 1)
    block_table = jnp.stack([channels, offsets, amounts], axis=1)
    return block_table.reshape(NSUB, TMO, 3, NBLK).astype(jnp.int32)


def draw_antenna_links(key, part):
    subkeys = jax.random.split(jax.random.fold_in(key, 7723), 2)
    antenna_left = jax.random.randint(subkeys[0], (NBASE,), 0, NST)
    step_ahead = jax.random.randint(subkeys[1], (NBASE,), 1, NST)
    antenna_right = (antenna_left + step_ahead) % NST
    return jnp.stack([antenna_left, antenna_right]).astype(jnp.int32)


def levels(key, dims, cuts, low, high):
    factor_of, own = 1.0, jax.random.fold_in(key, 6)
    for dim, blocks in cuts:
        steps = jnp.exp(jax.random.uniform(jax.random.fold_in(own, dim), (blocks,), jnp.float32, low / len(cuts), high / len(cuts)))
        factor_of = factor_of * jnp.repeat(steps, dims[dim] // blocks).reshape([-1 if axis == dim else 1 for axis in range(len(dims))])
    return factor_of


def noise(own_key, extent, width, bound, cuts=(), held_as=jnp.bfloat16):
    gain = levels(own_key, extent, cuts, -0.22, 0.18) if cuts else 1.0
    drawn = jax.random.normal(own_key, extent, jnp.float32) * width * gain
    return jnp.minimum(jnp.maximum(drawn, -bound), bound).astype(held_as)


def setup_inputs(seed: int = 0) -> dict:
    keys = jax.random.split(jax.random.key(seed), 9)
    tile_spectral_lines = noise(keys[0], (NF, NPOL, 2, MC, FS), 1.0, 6.0, ((0, 4), (1, 4), (3, 2)))
    taper_leading_axis = noise(keys[1], (NSUB, TMO, VT, SG), SG ** -0.5, 0.25, ((0, 4), (1, 2)))
    taper_trailing_axis = noise(keys[2], (NSUB, TMO, VT, SG), SG ** -0.5, 0.25, ((0, 4), (1, 2)))
    depth_layer_factors = noise(keys[3], (NSUB, TMO, NW, VT), NW ** -0.5, 4.0, ((0, 4), (1, 2)))
    measured_correlations = noise(keys[4], (NSUB, 2 * NPOL, TMO, VT), 1.0, 6.0, ((0, 4), (2, 2), (3, 4)), jnp.float32)
    visibility_groups_table = draw_visibility_groups_table(jax.random.fold_in(keys[8], 71), 0)
    antenna_links = draw_antenna_links(jax.random.fold_in(keys[8], 71), 0)
    complex_receiver_factors = noise(keys[7], (NCH, 4, NST), 0.8, 5.0, (), jnp.float32)
    return dict(tile_spectral_lines=tile_spectral_lines, taper_leading_axis=taper_leading_axis, taper_trailing_axis=taper_trailing_axis, depth_layer_factors=depth_layer_factors, measured_correlations=measured_correlations, visibility_groups_table=visibility_groups_table, antenna_links=antenna_links, complex_receiver_factors=complex_receiver_factors)


w_chirp = 0.37
grad_scale = 0.1
feed_first = np.array([0, 0, 1, 1])
feed_second = np.array([0, 1, 0, 1])

def dft_table(length):
    indices = jnp.arange(length, dtype=jnp.int32)
    product = indices[:, None] * indices[None, :] % length
    angles = 2.0 * math.pi / length * product.astype(jnp.float32)
    factor = 1.0 / math.sqrt(length)
    return ((jnp.cos(angles) * factor).astype(jnp.bfloat16), (jnp.sin(angles) * factor).astype(jnp.bfloat16))

def chirp_phase(first_row, row_total, side_cells):
    across = (first_row + jnp.arange(row_total, dtype=jnp.int32) - side_cells // 2).astype(jnp.float32)
    downward = (jnp.arange(side_cells, dtype=jnp.int32) - side_cells // 2).astype(jnp.float32)
    return w_chirp * (across[:, None] * across[:, None] + downward[None, :] * downward[None, :]) / float(side_cells * side_cells)

def make_planes(sub_real, sub_imag, phase_grid, layers):
    planes_list = []
    for plane_index in range(layers):
        angles = 2.0 * math.pi * plane_index * phase_grid
        cosine = jnp.cos(angles)
        sine_part = jnp.sin(angles)
        planes_list.append(jnp.stack([sub_real * cosine - sub_imag * sine_part, sub_real * sine_part + sub_imag * cosine]).astype(jnp.bfloat16))
    return jnp.stack(planes_list)

def decode_slots(block_table, slot_index):
    channels = block_table[..., 0, :]
    offsets = block_table[..., 1, :]
    amounts = block_table[..., 2, :]
    starts = (jnp.cumsum(amounts, axis=-1) - amounts).astype(jnp.int32)
    relative = (slot_index[:, None] - starts[..., None, :]).astype(jnp.int32)
    member = ((relative >= 0) & (relative < amounts[..., None, :])).astype(jnp.int32)
    slot_live = lax.optimization_barrier(jnp.sum(member, axis=-1)).astype(jnp.int32)
    channel = lax.optimization_barrier(jnp.sum(member * channels[..., None, :], axis=-1)).astype(jnp.int32)
    antenna_couple = lax.optimization_barrier(jnp.sum(member * (offsets[..., None, :] + relative), axis=-1)).astype(jnp.int32)
    return (slot_live, channel, antenna_couple)

def model_terms(pred_re, pred_im, obs_re, obs_im, gain_first, gain_second, slot_live):
    first_re = gain_first[..., 2 * feed_first]
    first_im = gain_first[..., 2 * feed_first + 1]
    second_re = gain_second[..., 2 * feed_second]
    second_im = gain_second[..., 2 * feed_second + 1]
    both_re = first_re * second_re + first_im * second_im
    both_im = first_im * second_re - first_re * second_im
    model_re = both_re * pred_re - both_im * pred_im
    model_im = both_re * pred_im + both_im * pred_re
    alive_mask = slot_live.astype(jnp.float32)[..., None]
    resid_re = alive_mask * (obs_re - model_re)
    resid_im = alive_mask * (obs_im - model_im)
    cross_re = second_re * pred_re + second_im * pred_im
    cross_im = second_im * pred_re - second_re * pred_im
    lead_re = -(resid_re * cross_re - resid_im * cross_im)
    lead_im = -(resid_re * cross_im + resid_im * cross_re)
    along_re = first_re * pred_re - first_im * pred_im
    along_im = first_re * pred_im + first_im * pred_re
    trail_re = -(resid_re * along_re + resid_im * along_im)
    trail_im = -(resid_re * along_im - resid_im * along_re)
    leading = jnp.stack([lead_re[..., 0] + lead_re[..., 1], lead_im[..., 0] + lead_im[..., 1], lead_re[..., 2] + lead_re[..., 3], lead_im[..., 2] + lead_im[..., 3]], axis=-1)
    trailing = jnp.stack([trail_re[..., 0] + trail_re[..., 2], trail_im[..., 0] + trail_im[..., 2], trail_re[..., 1] + trail_re[..., 3], trail_im[..., 1] + trail_im[..., 3]], axis=-1)
    return (resid_re, resid_im, leading, trailing)

def real_dot(left_side, right_side):
    return jnp.dot(left_side.astype(jnp.float32), right_side.astype(jnp.float32), precision=lax.Precision.HIGHEST)

def degrid_reference(layers, rows_u, rows_v, weights_w):
    spread_v = jnp.einsum('wcuv,nv->wcun', layers.astype(jnp.float32), rows_v.astype(jnp.float32), precision=lax.Precision.HIGHEST)
    along_u = lax.optimization_barrier(jnp.sum(spread_v * jnp.transpose(rows_u).astype(jnp.float32)[None, None], axis=2))
    return lax.optimization_barrier(jnp.sum(along_u * weights_w.astype(jnp.float32)[:, None, :], axis=0))

def reference(tile_spectral_lines, taper_leading_axis, taper_trailing_axis, depth_layer_factors, measured_correlations, visibility_groups_table, antenna_links, complex_receiver_factors):
    source = tile_spectral_lines.astype(jnp.float32)
    spectrum = jnp.fft.fft(source[:, :, 0] + 1j * source[:, :, 1], axis=-1)[..., :NSUB * MC] / math.sqrt(FS)
    contrib_re = jnp.real(spectrum).astype(jnp.bfloat16)
    contrib_im = jnp.imag(spectrum).astype(jnp.bfloat16)

    def assemble(pieces):
        layout = pieces.reshape(FGRID, FGRID, NPOL, MC, NSUB, MC)
        return jnp.transpose(layout, (4, 2, 0, 3, 1, 5)).reshape(NSUB, NPOL, SG, SG)
    table_re, table_im = dft_table(SG)
    phase_grid = chirp_phase(0, SG, SG)

    def one_subgrid(inputs):
        layout_re, layout_im, rows_u, rows_v, weights_w = inputs
        flat_u = rows_u.reshape(TMO * VT, SG)
        flat_v = rows_v.reshape(TMO * VT, SG)
        flat_w = jnp.transpose(weights_w, (1, 0, 2)).reshape(NW, TMO * VT)
        results = []
        for polarisation in range(NPOL):
            half_re = (real_dot(layout_re[polarisation], table_re) - real_dot(layout_im[polarisation], table_im)).astype(jnp.bfloat16)
            half_im = (real_dot(layout_re[polarisation], table_im) + real_dot(layout_im[polarisation], table_re)).astype(jnp.bfloat16)
            sub_real = (real_dot(table_re, half_re) - real_dot(table_im, half_im)).astype(jnp.bfloat16)
            sub_imag = (real_dot(table_re, half_im) + real_dot(table_im, half_re)).astype(jnp.bfloat16)
            layers = make_planes(sub_real, sub_imag, phase_grid, NW)
            results.append(degrid_reference(layers, flat_u, flat_v, flat_w))
        return jnp.stack(results).reshape(NPOL, 2, TMO, VT)
    predicted = lax.map(one_subgrid, (assemble(contrib_re), assemble(contrib_im), taper_leading_axis, taper_trailing_axis, depth_layer_factors))
    slot_index = jnp.arange(VT, dtype=jnp.int32)
    slot_live, channel, antenna_couple = decode_slots(visibility_groups_table, slot_index)
    antenna_left = jnp.take(antenna_links[0], antenna_couple)
    antenna_right = jnp.take(antenna_links[1], antenna_couple)
    gains_turned = jnp.transpose(complex_receiver_factors, (0, 2, 1))
    gain_first = gains_turned[channel, antenna_left]
    gain_second = gains_turned[channel, antenna_right]
    pred_re = jnp.transpose(predicted[:, :, 0], (0, 2, 3, 1))
    pred_im = jnp.transpose(predicted[:, :, 1], (0, 2, 3, 1))
    obs_re = jnp.transpose(measured_correlations[:, 0::2], (0, 2, 3, 1))
    obs_im = jnp.transpose(measured_correlations[:, 1::2], (0, 2, 3, 1))
    resid_re, resid_im, leading, trailing = model_terms(pred_re, pred_im, obs_re, obs_im, gain_first, gain_second, slot_live)
    residual = jnp.transpose(jnp.stack([resid_re, resid_im], axis=-1), (0, 3, 4, 1, 2)).reshape(NSUB, 2 * NPOL, TMO, VT)
    segments_first = (antenna_left * NCH + channel).reshape(-1).astype(jnp.int32)
    segments_second = (antenna_right * NCH + channel).reshape(-1).astype(jnp.int32)
    summed = jax.ops.segment_sum(leading.reshape(-1, 4), segments_first, num_segments=NST * NCH)
    summed = summed + jax.ops.segment_sum(trailing.reshape(-1, 4), segments_second, num_segments=NST * NCH)
    gain_grad = grad_scale * summed.reshape(NST, NCH * 4)
    return (residual, gain_grad)
```

```python
import functools
import math

import jax
import jax.numpy as jnp
import numpy as np
from jax import lax
from jax.experimental import pallas as pl
from jax.experimental.pallas import tpu as pltpu
from jax.sharding import PartitionSpec as P

FGRID = 8
FS = 4096
MC = 64
SG = 512
NPOL = 4
NW = 2
NCH = 256
NST = 512
CHUNK = 1024
PIECES = 2

w_chirp = 0.37
grad_scale = 0.1


def unit_angles(left, right, length):
    product = np.outer(np.arange(left), np.arange(right)) % length
    return 2.0 * math.pi * product / length


def fourier_factors(subgrids):
    spread = FS // MC
    alpha = unit_angles(FS // spread, MC, MC)
    p = np.concatenate([np.cos(alpha), -np.sin(alpha)], axis=1) / math.sqrt(FS)
    q = np.concatenate([-np.sin(alpha), -np.cos(alpha)], axis=1) / math.sqrt(FS)
    beta = unit_angles(spread, subgrids * MC, FS).reshape(spread, subgrids, 1, MC)
    beta = np.broadcast_to(beta, (spread, subgrids, 2, MC)).reshape(spread, subgrids * 2 * MC)
    tile = lambda t: np.tile(t, (1, subgrids)).astype(np.float32)
    return (
        tile(p),
        tile(q),
        np.cos(beta).astype(np.float32),
        np.sin(beta).astype(np.float32),
    )


def fetch_lookups(block_ref, links_ref, gain_ref, window, channel_gain, window_sem, gain_sem):
    blocks, _, span = window.shape
    copies = []
    for b in range(blocks):
        first = jnp.minimum(block_ref[1, b] // 128 * 128, links_ref.shape[1] - span)
        first = pl.multiple_of(first, 128)
        copies.append(
            pltpu.make_async_copy(
                links_ref.at[:, pl.ds(first, span)], window.at[b], window_sem.at[b]
            )
        )
        copies.append(
            pltpu.make_async_copy(
                gain_ref.at[block_ref[0, b]], channel_gain.at[b], gain_sem.at[b]
            )
        )
    return copies


def use_lookups(block_ref, links_ref, window, channel_gain, gains_ref, idents_ref):
    blocks, _, span = window.shape
    slots = idents_ref.shape[1]
    lane = lax.broadcasted_iota(jnp.int32, (1, slots), 1)
    place = lax.broadcasted_iota(jnp.int32, (span, slots), 0)
    lane_tall = lax.broadcasted_iota(jnp.int32, (span, slots), 1)
    begin = jnp.int32(0)
    member, picks = [], []
    channel = jnp.zeros((1, slots), jnp.float32)
    alive = jnp.zeros((1, slots), jnp.float32)
    for b in range(blocks):
        offset, amount = block_ref[1, b], block_ref[2, b]
        first = jnp.minimum(offset // 128 * 128, links_ref.shape[1] - span)
        inside = jnp.where((lane >= begin) & (lane < begin + amount), 1.0, 0.0)
        member.append(inside)
        alive += inside
        channel += inside * block_ref[0, b].astype(jnp.float32)
        hit = place == lane_tall + (offset - first - begin)
        picks.append((jnp.where(hit, 1.0, 0.0) * inside).astype(jnp.bfloat16))
        begin = begin + amount
    links = jnp.concatenate([window[b] for b in range(blocks)], axis=1)
    upper = links // 16
    lower = links - 16 * upper
    pieces = jnp.concatenate([upper, lower], axis=0).astype(jnp.float32).astype(jnp.bfloat16)
    found = jnp.dot(
        pieces, jnp.concatenate(picks, axis=0), preferred_element_type=jnp.float32
    )
    stations = 16.0 * found[0:2] + found[2:4]
    table = channel_gain[...].reshape(blocks * 4, channel_gain.shape[2])
    high = table.astype(jnp.bfloat16)
    rest = table - high.astype(jnp.float32)
    middle = rest.astype(jnp.bfloat16)
    low = (rest - middle.astype(jnp.float32)).astype(jnp.bfloat16)
    names = lax.broadcasted_iota(jnp.int32, (table.shape[1], 1), 0).astype(jnp.float32)
    for side in range(2):
        pick = jnp.where(names == stations[side : side + 1], 1.0, 0.0).astype(jnp.bfloat16)
        rows = (
            jnp.dot(high, pick, preferred_element_type=jnp.float32)
            + jnp.dot(middle, pick, preferred_element_type=jnp.float32)
            + jnp.dot(low, pick, preferred_element_type=jnp.float32)
        )
        chosen = member[0] * rows[0:4]
        for b in range(1, blocks):
            chosen = chosen + member[b] * rows[4 * b : 4 * b + 4]
        gains_ref[4 * side : 4 * side + 4, :] = chosen
    idents_ref[0:2, :] = stations
    idents_ref[2:3, :] = channel
    idents_ref[3:4, :] = alive
    idents_ref[4:8, :] = jnp.zeros((4, slots), jnp.float32)


def fourier_kernel(
    block_ref,
    links_ref,
    gain_ref,
    p_ref,
    q_ref,
    c_ref,
    s_ref,
    x_ref,
    o_ref,
    gains_ref,
    idents_ref,
    table,
    total,
    window,
    channel_gain,
    window_sem,
    gain_sem,
):
    step = pl.program_id(0)
    copies = fetch_lookups(
        block_ref, links_ref, gain_ref, window, channel_gain, window_sem, gain_sem
    )

    @pl.when(step == 0)
    def _():
        for copy in copies:
            copy.start()

    @pl.when(step == pl.num_programs(0) - 1)
    def _():
        for copy in copies:
            copy.wait()
        use_lookups(block_ref, links_ref, window, channel_gain, gains_ref, idents_ref)

    facets, _, rows, chunk = x_ref.shape
    subgrids = o_ref.shape[0]
    spread = c_ref.shape[0]
    cosine, sine = c_ref[...], s_ref[...]
    for part in range(chunk // spread):
        lead = p_ref[part : part + 1, :]
        other = q_ref[part : part + 1, :]
        table[part * spread : (part + 1) * spread, :] = (lead * cosine + other * sine).astype(
            jnp.bfloat16
        )
    x = x_ref[...].reshape(facets * 2 * rows, chunk)
    product = jnp.dot(x, table[...], preferred_element_type=jnp.float32)

    @pl.when(step == 0)
    def _():
        total[...] = product

    @pl.when(step > 0)
    def _():
        total[...] += product

    @pl.when(step == pl.num_programs(0) - 1)
    def _():
        lane = lax.broadcasted_iota(jnp.int32, (rows, 2 * MC), 1)
        sign = jnp.where(lane < MC, -1.0, 1.0)
        packed = o_ref.shape[3] // (2 * MC)
        for f in range(facets):
            for s in range(subgrids):
                cut = slice(s * 2 * MC, (s + 1) * 2 * MC)
                first = total[2 * f * rows : (2 * f + 1) * rows, cut]
                second = total[(2 * f + 1) * rows : (2 * f + 2) * rows, cut]
                value = first + sign * pltpu.roll(second, MC, 1)
                j = f % packed
                o_ref[s, f // packed, :, j * 2 * MC : (j + 1) * 2 * MC] = value.astype(jnp.bfloat16)


def fourier(x, subgrids, slots, block_table, links, station_gains):
    facets, _, rows, length = x.shape
    width = subgrids * 2 * MC
    spread = FS // MC
    packed = FGRID if facets % FGRID == 0 else 1
    per_step = CHUNK // spread
    blocks = block_table.shape[1]
    span = slots + 128
    in_place = lambda array: pltpu.with_memory_space_constraint(array, pltpu.HBM)
    factors = [in_place(jnp.asarray(t)) for t in fourier_factors(subgrids)]
    out = (subgrids, facets // packed, rows, packed * 2 * MC)
    return pl.pallas_call(
        fourier_kernel,
        out_shape=(
            jax.ShapeDtypeStruct(out, jnp.bfloat16),
            jax.ShapeDtypeStruct((8, slots), jnp.float32),
            jax.ShapeDtypeStruct((8, slots), jnp.float32),
        ),
        grid=(length // CHUNK,),
        in_specs=[
            pl.BlockSpec(memory_space=pltpu.SMEM),
            pl.BlockSpec(memory_space=pltpu.HBM),
            pl.BlockSpec(memory_space=pltpu.HBM),
            pl.BlockSpec((per_step, width), lambda g: (g, 0)),
            pl.BlockSpec((per_step, width), lambda g: (g, 0)),
            pl.BlockSpec((spread, width), lambda g: (0, 0)),
            pl.BlockSpec((spread, width), lambda g: (0, 0)),
            pl.BlockSpec((facets, 2, rows, CHUNK), lambda g: (0, 0, 0, g)),
        ],
        out_specs=(
            pl.BlockSpec(out, lambda g: (0, 0, 0, 0)),
            pl.BlockSpec((8, slots), lambda g: (0, 0)),
            pl.BlockSpec((8, slots), lambda g: (0, 0)),
        ),
        scratch_shapes=[
            pltpu.VMEM((CHUNK, width), jnp.bfloat16),
            pltpu.VMEM((facets * 2 * rows, width), jnp.float32),
            pltpu.VMEM((blocks, 2, span), jnp.int32),
            pltpu.VMEM((blocks, 4, NST), jnp.float32),
            pltpu.SemaphoreType.DMA((blocks,)),
            pltpu.SemaphoreType.DMA((blocks,)),
        ],
        compiler_params=pltpu.CompilerParams(
            dimension_semantics=("arbitrary",), vmem_limit_bytes=48 << 20
        ),
    )(
        block_table,
        in_place(links),
        in_place(station_gains),
        *factors,
        x,
    )


def subgrid_tables():
    angle = unit_angles(SG, SG, SG)
    re = np.cos(angle) / math.sqrt(SG)
    im = np.sin(angle) / math.sqrt(SG)
    blocks = lambda t: t.reshape(SG, FGRID, MC)
    second = np.stack([blocks(re), -blocks(im)], axis=2).reshape(SG, 2 * SG)
    return [t.astype(jnp.bfloat16) for t in (re, im, second)]


def chirp_line():
    offset = np.arange(SG) - SG // 2
    angle = 2.0 * math.pi * w_chirp * (offset * offset) / float(SG * SG)
    return np.cos(angle).astype(np.float32), np.sin(angle).astype(np.float32)


def model_terms(pred, observed, first, second, alive):
    residual, lead, trail = [], [], []
    for p in range(NPOL):
        f1, f2 = p // 2, p % 2
        pred_re, pred_im = pred[p]
        first_re, first_im = first[2 * f1], first[2 * f1 + 1]
        second_re, second_im = second[2 * f2], second[2 * f2 + 1]
        both_re = first_re * second_re + first_im * second_im
        both_im = first_im * second_re - first_re * second_im
        resid_re = alive * (observed[2 * p] - (both_re * pred_re - both_im * pred_im))
        resid_im = alive * (observed[2 * p + 1] - (both_re * pred_im + both_im * pred_re))
        cross_re = second_re * pred_re + second_im * pred_im
        cross_im = second_im * pred_re - second_re * pred_im
        along_re = first_re * pred_re - first_im * pred_im
        along_im = first_re * pred_im + first_im * pred_re
        residual += [resid_re, resid_im]
        lead.append(
            (-(resid_re * cross_re - resid_im * cross_im), -(resid_re * cross_im + resid_im * cross_re))
        )
        trail.append(
            (-(resid_re * along_re + resid_im * along_im), -(resid_re * along_im - resid_im * along_re))
        )
    leading = [lead[2 * f][r] + lead[2 * f + 1][r] for f in range(2) for r in range(2)]
    trailing = [trail[f][r] + trail[f + 2][r] for f in range(2) for r in range(2)]
    return residual, leading, trailing


def nt_dot(left, right, **kw):
    return lax.dot_general(
        left, right, (((1,), (1,)), ((), ())), preferred_element_type=jnp.float32, **kw
    )


def chirped_rows(taper, chirp_ref):
    wide = taper.astype(jnp.float32)
    return jnp.concatenate(
        [
            taper,
            (wide * chirp_ref[0:1, :]).astype(jnp.bfloat16),
            (wide * chirp_ref[1:2, :]).astype(jnp.bfloat16),
        ],
        axis=0,
    )


def predict_kernel(
    sizes,
    contrib_ref,
    lead_ref,
    trail_ref,
    depth_ref,
    observed_ref,
    gains_ref,
    idents_ref,
    table_re_ref,
    table_im_ref,
    second_ref,
    chirp_ref,
    residual_ref,
    grad_ref,
    got,
    lines,
    tapers,
    right,
    left,
    part_out,
    part_in,
    observed_out,
    observed_in,
    record_out,
    record_in,
    got_send,
    got_recv,
    taper_send,
    taper_recv,
    observed_send,
    observed_recv,
    part_send,
    part_recv,
    record_send,
    record_recv,
):
    subgrids, pols, owners = sizes
    z, p, t = lax.axis_index("facet"), lax.axis_index("pol"), lax.axis_index("tm")
    slots = lead_ref.shape[0]
    _, groups, rows, width = contrib_ref.shape
    mesh_id = pl.DeviceIdType.MESH

    def remote(src, dst, send, recv, peer):
        return pltpu.make_async_remote_copy(
            src_ref=src,
            dst_ref=dst,
            send_sem=send,
            recv_sem=recv,
            device_id=peer,
            device_id_type=mesh_id,
        )

    across_total = subgrids * owners
    plane_total = pols * owners
    across = z * owners + t
    plane = p * owners + t

    def across_peer(d):
        other = lax.rem(across + d, across_total)
        return other, (other // owners, p, lax.rem(other, owners))

    def plane_peer(d):
        other = lax.rem(plane + d, plane_total)
        return other, (z, other // owners, lax.rem(other, owners))

    barrier = pltpu.get_barrier_semaphore()
    for d in range(1, across_total):
        pl.semaphore_signal(barrier, inc=1, device_id=across_peer(d)[1], device_id_type=mesh_id)
    for d in range(1, pols):
        q = lax.rem(p + d, pols)
        for o in range(owners):
            pl.semaphore_signal(barrier, inc=1, device_id=(z, q, o), device_id_type=mesh_id)
    pl.semaphore_wait(barrier, across_total - 1 + (pols - 1) * owners)

    quarter = observed_ref.shape[1]
    place = lax.broadcasted_iota(jnp.int32, (2 * NPOL, slots), 1)
    observed_out[...] = jnp.where(
        (place >= p * quarter) & (place < (p + 1) * quarter),
        jnp.concatenate([observed_ref[...]] * pols, axis=1),
        0.0,
    )
    copies = []
    for d in sorted(range(1, subgrids), key=lambda d: -min(d, subgrids - d)):
        other = lax.rem(z + d, subgrids)
        copies.append(
            remote(contrib_ref.at[other], got.at[z], got_send.at[d], got_recv.at[d], (other, p, t))
        )
    partner = lax.rem(t + 1, owners)
    taper_copies = [
        remote(ref, tapers.at[t, k], taper_send.at[k], taper_recv.at[k], (z, p, partner))
        for k, ref in enumerate((trail_ref, lead_ref))
    ]
    observed_copies = []
    for d in range(1, pols):
        q = lax.rem(p + d, pols)
        observed_copies.append(
            remote(
                observed_out, observed_in.at[p], observed_send.at[d], observed_recv.at[d], (z, q, t)
            )
        )
    for copy in copies + taper_copies + observed_copies:
        copy.start()

    table_re = jnp.concatenate([table_re_ref[i, t] for i in range(FGRID)], axis=0)
    table_im = jnp.concatenate([table_im_ref[i, t] for i in range(FGRID)], axis=0)

    turn = jnp.where(
        lax.broadcasted_iota(jnp.int32, (3 * slots, 2 * MC), 1) < MC, -1.0, 1.0
    )

    def prepare(owner, trail, lead):
        trail3 = chirped_rows(trail, chirp_ref)
        a = jnp.dot(trail3, second_ref[...], preferred_element_type=jnp.float32)
        b = jnp.concatenate(
            [
                turn * pltpu.roll(a[:, j * 2 * MC : (j + 1) * 2 * MC], MC, 1)
                for j in range(a.shape[1] // (2 * MC))
            ],
            axis=1,
        )
        n0, n1, n2 = slice(0, slots), slice(slots, 2 * slots), slice(2 * slots, 3 * slots)
        right[owner, 0:slots, :] = a[n0].astype(jnp.bfloat16)
        right[owner, slots : 2 * slots, :] = (a[n1] - b[n2]).astype(jnp.bfloat16)
        right[owner, 2 * slots : 3 * slots, :] = b[n0].astype(jnp.bfloat16)
        right[owner, 3 * slots : 4 * slots, :] = (b[n1] + a[n2]).astype(jnp.bfloat16)
        lead3 = chirped_rows(lead, chirp_ref)
        u = nt_dot(table_re, lead3)
        v = nt_dot(table_im, lead3)
        left[owner, 0] = u[:, n0]
        left[owner, 1] = v[:, n0]
        left[owner, 2] = u[:, n1] - v[:, n2]
        left[owner, 3] = u[:, n2] + v[:, n1]

    prepare(t, trail_ref[...], lead_ref[...])
    got[z] = contrib_ref[z]
    for copy in taper_copies:
        copy.wait()
    prepare(partner, tapers[partner, 0], tapers[partner, 1])
    for copy in copies:
        copy.wait()
    if width == 2 * SG:
        whole = got[...].reshape(subgrids * groups * rows, width)
    else:
        for f in range(subgrids * groups):
            i, j = f // FGRID, f % FGRID
            lines[i * rows : (i + 1) * rows, j * 2 * MC : (j + 1) * 2 * MC] = got[
                f // groups, f % groups
            ]
        whole = lines[...]
    for o in range(owners):
        spread = nt_dot(whole, right[o])
        for w in range(NW):
            g_re = spread[:, w * slots : (w + 1) * slots]
            g_im = spread[:, (NW + w) * slots : (NW + w + 1) * slots]
            l_re, l_im = left[o, 2 * w], left[o, 2 * w + 1]
            part_out[o, 2 * w : 2 * w + 1, :] = jnp.sum(l_re * g_re - l_im * g_im, axis=0, keepdims=True)
            part_out[o, 2 * w + 1 : 2 * w + 2, :] = jnp.sum(
                l_re * g_im + l_im * g_re, axis=0, keepdims=True
            )
        part_out[o, 2 * NW :, :] = jnp.zeros((8 - 2 * NW, slots), jnp.float32)

    part_copies = []
    for d in range(1, plane_total):
        other, peer = plane_peer(d)
        part_copies.append(
            remote(
                part_out.at[lax.rem(other, owners)],
                part_in.at[plane],
                part_send.at[d],
                part_recv.at[d],
                peer,
            )
        )
    for copy in part_copies:
        copy.start()
    part_in[plane] = part_out[t]
    observed_in[p] = observed_out[...]
    for copy in observed_copies:
        copy.wait()
    observed = observed_in[0]
    for q in range(1, pols):
        observed = observed + observed_in[q]
    depth = depth_ref[...].astype(jnp.float32)
    for copy in part_copies:
        copy.wait()

    pred = []
    per_pol = part_in.shape[0] // NPOL
    for q in range(NPOL):
        block = part_in[q * per_pol]
        for o in range(1, per_pol):
            block = block + part_in[q * per_pol + o]
        pred.append(
            tuple(
                sum(depth[w : w + 1] * block[2 * w + c : 2 * w + c + 1] for w in range(NW))
                for c in range(2)
            )
        )
    gains = gains_ref[...]
    idents = idents_ref[...]
    residual, leading, trailing = model_terms(
        pred,
        [observed[k : k + 1] for k in range(2 * NPOL)],
        [gains[k : k + 1] for k in range(4)],
        [gains[4 + k : 5 + k] for k in range(4)],
        idents[3:4],
    )
    for k in range(3):
        record_out[k : k + 1, :] = idents[k : k + 1]
    for k in range(4):
        record_out[3 + k : 4 + k, :] = leading[k]
        record_out[7 + k : 8 + k, :] = trailing[k]
    record_out[11:, :] = jnp.zeros((5, slots), jnp.float32)
    record_copies = []
    for d in range(1, across_total):
        other, peer = across_peer(d)
        record_copies.append(
            remote(record_out, record_in.at[across], record_send.at[d], record_recv.at[d], peer)
        )
    for copy in record_copies:
        copy.start()
    record_in[across] = record_out[...]
    rest = jnp.concatenate(residual, axis=0)
    own_rest = jnp.zeros((2 * NPOL, quarter), jnp.float32)
    for q in range(pols):
        own_rest = jnp.where(p == q, rest[:, q * quarter : (q + 1) * quarter], own_rest)
    residual_ref[...] = own_rest
    for copy in record_copies:
        copy.wait()

    piece = jnp.concatenate([record_in[d] for d in range(across_total)], axis=1)
    own_count = grad_ref.shape[1]
    index = (z * pols + p) * owners + t
    mine = (index * own_count + lax.broadcasted_iota(jnp.int32, (own_count, 1), 0)).astype(
        jnp.float32
    )
    match_first = mine == piece[0:1]
    match_second = mine == piece[1:2]
    weighted = jnp.concatenate(
        [
            jnp.where(match_first, piece[3 + k : 4 + k], 0.0)
            + jnp.where(match_second, piece[7 + k : 8 + k], 0.0)
            for k in range(4)
        ],
        axis=0,
    )
    high = weighted.astype(jnp.bfloat16)
    low = (weighted - high.astype(jnp.float32)).astype(jnp.bfloat16)
    channel_ids = lax.broadcasted_iota(jnp.int32, (NCH, 1), 0).astype(jnp.float32)
    onehot = jnp.where(channel_ids == piece[2:3], 1.0, 0.0).astype(jnp.bfloat16)
    summed = nt_dot(high, onehot) + nt_dot(low, onehot)
    for k in range(4):
        grad_ref[k] = grad_scale * summed[k * own_count : (k + 1) * own_count]


def predict(sizes, own_count, *operands):
    subgrids, pols, owners = sizes
    contrib, lead = operands[0], operands[1]
    _, groups, rows, width = contrib.shape
    slots = lead.shape[0]
    vmem = pl.BlockSpec(memory_space=pltpu.VMEM)
    dma = lambda n: pltpu.SemaphoreType.DMA((n,))
    across_total, plane_total = subgrids * owners, pols * owners
    return pl.pallas_call(
        functools.partial(predict_kernel, sizes),
        out_shape=(
            jax.ShapeDtypeStruct((2 * NPOL, slots // pols), jnp.float32),
            jax.ShapeDtypeStruct((4, own_count, NCH), jnp.float32),
        ),
        in_specs=[vmem] * len(operands),
        out_specs=(vmem, vmem),
        scratch_shapes=[
            pltpu.VMEM(contrib.shape, jnp.bfloat16),
            pltpu.VMEM((FGRID * rows, 2 * SG), jnp.bfloat16),
            pltpu.VMEM((owners, 2, slots, SG), jnp.bfloat16),
            pltpu.VMEM((owners, 2 * NW * slots, 2 * SG), jnp.bfloat16),
            pltpu.VMEM((owners, 4, FGRID * rows, slots), jnp.float32),
            pltpu.VMEM((owners, 8, slots), jnp.float32),
            pltpu.VMEM((plane_total, 8, slots), jnp.float32),
            pltpu.VMEM((8, slots), jnp.float32),
            pltpu.VMEM((pols, 8, slots), jnp.float32),
            pltpu.VMEM((16, slots), jnp.float32),
            pltpu.VMEM((across_total, 16, slots), jnp.float32),
            dma(subgrids),
            dma(subgrids),
            dma(2),
            dma(2),
            dma(pols),
            dma(pols),
            dma(plane_total),
            dma(plane_total),
            dma(across_total),
            dma(across_total),
        ],
        compiler_params=pltpu.CompilerParams(
            collective_id=0, has_side_effects=True, vmem_limit_bytes=48 << 20
        ),
    )(*operands)


def gather_lookups(block_ref, links_ref, gain_ref, gains_ref, idents_ref):
    blocks = block_ref.shape[2]
    slots = idents_ref.shape[1]
    span = slots + 128
    lane = lax.broadcasted_iota(jnp.int32, (1, slots), 1)
    place = lax.broadcasted_iota(jnp.int32, (span, slots), 0)
    lane_tall = lax.broadcasted_iota(jnp.int32, (span, slots), 1)
    begin = jnp.int32(0)
    member, picks, windows, tables = [], [], [], []
    channel = jnp.zeros((1, slots), jnp.float32)
    alive = jnp.zeros((1, slots), jnp.float32)
    for b in range(blocks):
        chosen, offset, amount = [block_ref[k, 0, b] for k in range(3)]
        row = jnp.minimum(lax.div(offset, 128), links_ref.shape[0] - span // 128)
        first = row * 128
        windows += [links_ref[row + k] for k in range(span // 128)]
        tables.append(gain_ref[chosen])
        inside = jnp.where((lane >= begin) & (lane < begin + amount), 1.0, 0.0)
        member.append(inside)
        alive += inside
        channel += inside * chosen.astype(jnp.float32)
        hit = place == lane_tall + (offset - first - begin)
        picks.append((jnp.where(hit, 1.0, 0.0) * inside).astype(jnp.bfloat16))
        begin = begin + amount
    links = jnp.concatenate(windows, axis=1)
    upper = links // 16
    lower = links - 16 * upper
    pieces = jnp.concatenate([upper, lower], axis=0).astype(jnp.float32).astype(jnp.bfloat16)
    found = jnp.dot(
        pieces, jnp.concatenate(picks, axis=0), preferred_element_type=jnp.float32
    )
    stations = 16.0 * found[0:2] + found[2:4]
    table = jnp.concatenate(tables, axis=0)
    high = table.astype(jnp.bfloat16)
    rest = table - high.astype(jnp.float32)
    middle = rest.astype(jnp.bfloat16)
    low = (rest - middle.astype(jnp.float32)).astype(jnp.bfloat16)
    split = jnp.concatenate([high, middle, low], axis=0)
    size = table.shape[0]
    names = lax.broadcasted_iota(jnp.int32, (table.shape[1], 1), 0).astype(jnp.float32)
    for side in range(2):
        pick = jnp.where(names == stations[side : side + 1], 1.0, 0.0).astype(jnp.bfloat16)
        three = jnp.dot(split, pick, preferred_element_type=jnp.float32)
        rows = three[:size] + three[size : 2 * size] + three[2 * size :]
        chosen = member[0] * rows[0:4]
        for b in range(1, blocks):
            chosen = chosen + member[b] * rows[4 * b : 4 * b + 4]
        gains_ref[4 * side : 4 * side + 4, :] = chosen
    idents_ref[0:2, :] = stations
    idents_ref[2:3, :] = channel
    idents_ref[3:4, :] = alive
    idents_ref[4:8, :] = jnp.zeros((4, slots), jnp.float32)


def fused_kernel(
    sizes,
    block_hbm,
    links_hbm,
    gain_hbm,
    p_hbm,
    q_hbm,
    c_hbm,
    s_hbm,
    x_hbm,
    lead_hbm,
    trail_hbm,
    depth_hbm,
    observed_hbm,
    table_re_hbm,
    table_im_hbm,
    second_hbm,
    chirp_hbm,
    residual_ref,
    grad_ref,
    block_ref,
    links_ref,
    gain_ref,
    p_ref,
    q_ref,
    c_ref,
    s_ref,
    x_ref,
    lead_ref,
    trail_ref,
    depth_ref,
    observed_ref,
    table_ref,
    second_ref,
    chirp_ref,
    factors,
    contrib,
    got,
    tapers,
    right,
    left,
    gains_ref,
    idents,
    part_out,
    part_in,
    observed_out,
    observed_in,
    record_out,
    record_in,
    load_sem,
    chunk_sem,
    got_send,
    got_recv,
    taper_send,
    taper_recv,
    observed_send,
    observed_recv,
    part_send,
    part_recv,
    ident_send,
    ident_recv,
    record_send,
    record_recv,
):
    subgrids, pols, owners = sizes
    z, p, t = lax.axis_index("facet"), lax.axis_index("pol"), lax.axis_index("tm")
    slots = lead_ref.shape[0]
    facets, _, rows, length = x_ref.shape
    _, groups, _, width = contrib.shape
    mesh_id = pl.DeviceIdType.MESH

    def remote(src, dst, send, recv, peer):
        return pltpu.make_async_remote_copy(
            src_ref=src,
            dst_ref=dst,
            send_sem=send,
            recv_sem=recv,
            device_id=peer,
            device_id_type=mesh_id,
        )

    across_total = subgrids * owners
    plane_total = pols * owners
    across = z * owners + t
    plane = p * owners + t

    def across_peer(d):
        other = lax.rem(across + d, across_total)
        return other, (other // owners, p, lax.rem(other, owners))

    def plane_peer(d):
        other = lax.rem(plane + d, plane_total)
        return other, (z, other // owners, lax.rem(other, owners))

    barrier = pltpu.get_barrier_semaphore()
    for d in range(1, across_total):
        pl.semaphore_signal(barrier, inc=1, device_id=across_peer(d)[1], device_id_type=mesh_id)
    for d in range(1, pols):
        q = lax.rem(p + d, pols)
        for o in range(owners):
            pl.semaphore_signal(barrier, inc=1, device_id=(z, q, o), device_id_type=mesh_id)

    per_chunk = FGRID // PIECES
    chunks = facets // per_chunk
    x_loads = [
        pltpu.make_async_copy(
            x_hbm.at[pl.ds(c * per_chunk, per_chunk)],
            x_ref.at[pl.ds(c * per_chunk, per_chunk)],
            chunk_sem.at[c],
        )
        for c in range(chunks)
    ]
    pairs = [
        (c_hbm, c_ref),
        (s_hbm, s_ref),
        (p_hbm, p_ref),
        (q_hbm, q_ref),
        (lead_hbm, lead_ref),
        (trail_hbm, trail_ref),
        (depth_hbm, depth_ref),
        (observed_hbm, observed_ref),
        (chirp_hbm, chirp_ref),
        (second_hbm, second_ref),
        (table_re_hbm.at[:, t], table_ref.at[0]),
        (table_im_hbm.at[:, t], table_ref.at[1]),
        (block_hbm, block_ref),
        (links_hbm, links_ref),
        (gain_hbm, gain_ref),
    ]
    loads = [
        pltpu.make_async_copy(src, dst, load_sem.at[k]) for k, (src, dst) in enumerate(pairs)
    ]
    for copy in loads[:4]:
        copy.start()
    x_loads[0].start()
    for copy in loads[4:9]:
        copy.start()
    for copy in x_loads[1:]:
        copy.start()
    for copy in loads[9:]:
        copy.start()

    for copy in loads[:4]:
        copy.wait()
    spread = c_ref.shape[0]
    cosine, sine = c_ref[...], s_ref[...]
    for part in range(length // spread):
        factors[part * spread : (part + 1) * spread, :] = (
            p_ref[part : part + 1, :] * cosine + q_ref[part : part + 1, :] * sine
        ).astype(jnp.bfloat16)

    lane = lax.broadcasted_iota(jnp.int32, (rows, 2 * MC), 1)
    sign = jnp.where(lane < MC, -1.0, 1.0)
    part_width = width // PIECES
    partner = lax.rem(t + 1, owners)
    copies, taper_copies, observed_copies = [], [], []
    for c in range(chunks):
        x_loads[c].wait()
        x = x_ref[c * per_chunk : (c + 1) * per_chunk].reshape(per_chunk * 2 * rows, length)
        total = jnp.dot(x, factors[...], preferred_element_type=jnp.float32)
        group, piece = c // PIECES, c % PIECES
        for s in range(subgrids):
            cut = slice(s * 2 * MC, (s + 1) * 2 * MC)
            for f in range(per_chunk):
                first = total[2 * f * rows : (2 * f + 1) * rows, cut]
                second = total[(2 * f + 1) * rows : (2 * f + 2) * rows, cut]
                j = piece * per_chunk + f
                contrib[s, group, :, j * 2 * MC : (j + 1) * 2 * MC] = (
                    first + sign * pltpu.roll(second, MC, 1)
                ).astype(jnp.bfloat16)
        if c == 0:
            pl.semaphore_wait(barrier, across_total - 1 + (pols - 1) * owners)
        lanes = pl.ds(piece * part_width, part_width)
        for d in sorted(range(1, subgrids), key=lambda d: -min(d, subgrids - d)):
            other = lax.rem(z + d, subgrids)
            copy = remote(
                contrib.at[other, group, :, lanes],
                got.at[z, group, :, lanes],
                got_send.at[c * subgrids + d],
                got_recv.at[c * subgrids + d],
                (other, p, t),
            )
            copy.start()
            copies.append(copy)
        if c == 0:
            for copy in loads[4:9]:
                copy.wait()
            taper_copies = [
                remote(ref, tapers.at[k], taper_send.at[k], taper_recv.at[k], (z, p, partner))
                for k, ref in enumerate((trail_ref, lead_ref))
            ]
            quarter = observed_ref.shape[1]
            place = lax.broadcasted_iota(jnp.int32, (2 * NPOL, slots), 1)
            observed_out[...] = jnp.where(
                (place >= p * quarter) & (place < (p + 1) * quarter),
                jnp.concatenate([observed_ref[...]] * pols, axis=1),
                0.0,
            )
            for d in range(1, pols):
                q = lax.rem(p + d, pols)
                observed_copies.append(
                    remote(
                        observed_out,
                        observed_in.at[p],
                        observed_send.at[d],
                        observed_recv.at[d],
                        (z, q, t),
                    )
                )
            for copy in taper_copies + observed_copies:
                copy.start()

    got[z] = contrib[z]
    for copy in loads[9:]:
        copy.wait()
    gather_lookups(block_ref, links_ref, gain_ref, gains_ref, idents.at[across])
    ident_copies = []
    for d in range(1, across_total):
        other, peer = across_peer(d)
        ident_copies.append(
            remote(idents.at[across], idents.at[across], ident_send.at[d], ident_recv.at[d], peer)
        )
    for copy in ident_copies:
        copy.start()

    table_re = jnp.concatenate([table_ref[0, i] for i in range(FGRID)], axis=0)
    table_im = jnp.concatenate([table_ref[1, i] for i in range(FGRID)], axis=0)
    turn = jnp.where(
        lax.broadcasted_iota(jnp.int32, (3 * slots, 2 * MC), 1) < MC, -1.0, 1.0
    )

    def prepare(owner, trail, lead):
        trail3 = chirped_rows(trail, chirp_ref)
        a = jnp.dot(trail3, second_ref[...], preferred_element_type=jnp.float32)
        b = jnp.concatenate(
            [
                turn * pltpu.roll(a[:, j * 2 * MC : (j + 1) * 2 * MC], MC, 1)
                for j in range(a.shape[1] // (2 * MC))
            ],
            axis=1,
        )
        n0, n1, n2 = slice(0, slots), slice(slots, 2 * slots), slice(2 * slots, 3 * slots)
        right[owner, 0:slots, :] = a[n0].astype(jnp.bfloat16)
        right[owner, slots : 2 * slots, :] = (a[n1] - b[n2]).astype(jnp.bfloat16)
        right[owner, 2 * slots : 3 * slots, :] = b[n0].astype(jnp.bfloat16)
        right[owner, 3 * slots : 4 * slots, :] = (b[n1] + a[n2]).astype(jnp.bfloat16)
        lead3 = chirped_rows(lead, chirp_ref)
        u = nt_dot(table_re, lead3)
        v = nt_dot(table_im, lead3)
        left[owner, 0] = u[:, n0]
        left[owner, 1] = v[:, n0]
        left[owner, 2] = u[:, n1] - v[:, n2]
        left[owner, 3] = u[:, n2] + v[:, n1]

    prepare(t, trail_ref[...], lead_ref[...])
    for copy in taper_copies:
        copy.wait()
    prepare(partner, tapers[0], tapers[1])
    for copy in copies:
        copy.wait()
    whole = got[...].reshape(subgrids * groups * rows, width)
    for o in range(owners):
        across_v = nt_dot(whole, right[o])
        for w in range(NW):
            g_re = across_v[:, w * slots : (w + 1) * slots]
            g_im = across_v[:, (NW + w) * slots : (NW + w + 1) * slots]
            l_re, l_im = left[o, 2 * w], left[o, 2 * w + 1]
            part_out[o, 2 * w : 2 * w + 1, :] = jnp.sum(l_re * g_re - l_im * g_im, axis=0, keepdims=True)
            part_out[o, 2 * w + 1 : 2 * w + 2, :] = jnp.sum(
                l_re * g_im + l_im * g_re, axis=0, keepdims=True
            )
        part_out[o, 2 * NW :, :] = jnp.zeros((8 - 2 * NW, slots), jnp.float32)

    part_copies = []
    for d in range(1, plane_total):
        other, peer = plane_peer(d)
        part_copies.append(
            remote(
                part_out.at[lax.rem(other, owners)],
                part_in.at[plane],
                part_send.at[d],
                part_recv.at[d],
                peer,
            )
        )
    for copy in part_copies:
        copy.start()
    part_in[plane] = part_out[t]
    observed_in[p] = observed_out[...]
    for copy in observed_copies:
        copy.wait()
    observed = observed_in[0]
    for q in range(1, pols):
        observed = observed + observed_in[q]
    depth = depth_ref[...].astype(jnp.float32)
    own_idents = idents[across]
    gains = gains_ref[...]
    for copy in ident_copies:
        copy.wait()
    names = jnp.concatenate([idents[d, 0:3] for d in range(across_total)], axis=1)
    own_count = grad_ref.shape[0]
    index = (z * pols + p) * owners + t
    mine = (index * own_count + lax.broadcasted_iota(jnp.int32, (own_count, 1), 0)).astype(
        jnp.float32
    )
    first_here = jnp.where(mine == names[0:1], 1.0, 0.0)
    second_here = jnp.where(mine == names[1:2], 1.0, 0.0)
    channel_ids = lax.broadcasted_iota(jnp.int32, (NCH, 1), 0).astype(jnp.float32)
    onehot = jnp.where(channel_ids == names[2:3], 1.0, 0.0).astype(jnp.bfloat16)
    for copy in part_copies:
        copy.wait()

    pred = []
    per_pol = part_in.shape[0] // NPOL
    for q in range(NPOL):
        block = part_in[q * per_pol]
        for o in range(1, per_pol):
            block = block + part_in[q * per_pol + o]
        pred.append(
            tuple(
                sum(depth[w : w + 1] * block[2 * w + c : 2 * w + c + 1] for w in range(NW))
                for c in range(2)
            )
        )
    residual, leading, trailing = model_terms(
        pred,
        [observed[k : k + 1] for k in range(2 * NPOL)],
        [gains[k : k + 1] for k in range(4)],
        [gains[4 + k : 5 + k] for k in range(4)],
        own_idents[3:4],
    )
    record_out[...] = jnp.concatenate(leading + trailing, axis=0)
    record_copies = []
    for d in range(1, across_total):
        other, peer = across_peer(d)
        record_copies.append(
            remote(record_out, record_in.at[across], record_send.at[d], record_recv.at[d], peer)
        )
    for copy in record_copies:
        copy.start()
    record_in[across] = record_out[...]
    rest = jnp.concatenate(residual, axis=0)
    quarter = observed_ref.shape[1]
    own_rest = jnp.zeros((2 * NPOL, quarter), jnp.float32)
    for q in range(pols):
        own_rest = jnp.where(p == q, rest[:, q * quarter : (q + 1) * quarter], own_rest)
    residual_ref[...] = own_rest
    for copy in record_copies:
        copy.wait()

    piece = jnp.concatenate([record_in[d] for d in range(across_total)], axis=1)
    weighted = jnp.concatenate(
        [
            first_here * piece[k : k + 1] + second_here * piece[4 + k : 5 + k]
            for k in range(4)
        ],
        axis=0,
    )
    high = weighted.astype(jnp.bfloat16)
    low = (weighted - high.astype(jnp.float32)).astype(jnp.bfloat16)
    summed = nt_dot(high, onehot) + nt_dot(low, onehot)
    lane_group = lax.broadcasted_iota(jnp.int32, (own_count, 128), 1) // 32
    mixed = []
    for g in range(NCH // 32):
        base = g // 4 * 128
        built = None
        for k in range(4):
            block = summed[k * own_count : (k + 1) * own_count, base : base + 128]
            shift = 32 * (k - g % 4) % 128
            block = pltpu.roll(block, shift, 1) if shift else block
            built = block if built is None else jnp.where(lane_group == k, block, built)
        mixed.append(grad_scale * built)
    mixed = jnp.concatenate(mixed, axis=0)
    high = mixed.astype(jnp.bfloat16)
    low = (mixed - high.astype(jnp.float32)).astype(jnp.bfloat16)
    came = lax.broadcasted_iota(jnp.int32, (128, 128), 0)
    goes = lax.broadcasted_iota(jnp.int32, (128, 128), 1)
    order = jnp.where(goes == came % 32 * 4 + came // 32, 1.0, 0.0).astype(jnp.bfloat16)
    placed = jnp.dot(
        jnp.concatenate([high, low], axis=0), order, preferred_element_type=jnp.float32
    )
    placed = placed[: mixed.shape[0]] + placed[mixed.shape[0] :]
    for g in range(NCH // 32):
        grad_ref[:, g * 128 : (g + 1) * 128] = placed[g * own_count : (g + 1) * own_count]


def emit_kernel(residual_ref, grad_ref, residual_out, grad_out, sems):
    copies = [
        pltpu.make_async_copy(residual_ref, residual_out, sems.at[0]),
        pltpu.make_async_copy(grad_ref, grad_out, sems.at[1]),
    ]
    for copy in copies:
        copy.start()
    for copy in copies:
        copy.wait()


def fused(sizes, own_count, *operands):
    subgrids, pols, owners = sizes
    block_table, links, gains = operands[0:3]
    x, lead, trail, depth, observed = operands[7:12]
    facets, _, rows, length = x.shape
    slots = lead.shape[0]
    width = subgrids * 2 * MC
    spread = FS // MC
    groups = facets // FGRID
    chunks = facets // (FGRID // PIECES)
    hbm = pl.BlockSpec(memory_space=pltpu.HBM)
    vmem = pl.BlockSpec(memory_space=pltpu.VMEM)
    dma = lambda n: pltpu.SemaphoreType.DMA((n,))
    held = lambda a: pltpu.VMEM(a.shape, a.dtype)
    across_total, plane_total = subgrids * owners, pols * owners
    f32, bf16 = jnp.float32, jnp.bfloat16
    residual, grad = pl.pallas_call(
        functools.partial(fused_kernel, sizes),
        out_shape=(
            jax.ShapeDtypeStruct(observed.shape, f32),
            jax.ShapeDtypeStruct((own_count, 4 * NCH), f32),
        ),
        in_specs=[hbm] * len(operands),
        out_specs=(vmem, vmem),
        scratch_shapes=[
            pltpu.SMEM(block_table.shape, jnp.int32),
            held(links),
            held(gains),
            pltpu.VMEM((length // spread, width), f32),
            pltpu.VMEM((length // spread, width), f32),
            pltpu.VMEM((spread, width), f32),
            pltpu.VMEM((spread, width), f32),
            held(x),
            held(lead),
            held(trail),
            held(depth),
            held(observed),
            pltpu.VMEM((2, FGRID, rows, SG), bf16),
            pltpu.VMEM((SG, 2 * SG), bf16),
            pltpu.VMEM((2, SG), f32),
            pltpu.VMEM((length, width), bf16),
            pltpu.VMEM((subgrids, groups, rows, 2 * SG), bf16),
            pltpu.VMEM((subgrids, groups, rows, 2 * SG), bf16),
            pltpu.VMEM((2, slots, SG), bf16),
            pltpu.VMEM((owners, 2 * NW * slots, 2 * SG), bf16),
            pltpu.VMEM((owners, 4, FGRID * rows, slots), f32),
            pltpu.VMEM((8, slots), f32),
            pltpu.VMEM((across_total, 8, slots), f32),
            pltpu.VMEM((owners, 8, slots), f32),
            pltpu.VMEM((plane_total, 8, slots), f32),
            pltpu.VMEM((8, slots), f32),
            pltpu.VMEM((pols, 8, slots), f32),
            pltpu.VMEM((8, slots), f32),
            pltpu.VMEM((across_total, 8, slots), f32),
            dma(15),
            dma(chunks),
            dma(chunks * subgrids),
            dma(chunks * subgrids),
            dma(2),
            dma(2),
            dma(pols),
            dma(pols),
            dma(plane_total),
            dma(plane_total),
            dma(across_total),
            dma(across_total),
            dma(across_total),
            dma(across_total),
        ],
        compiler_params=pltpu.CompilerParams(
            collective_id=0, has_side_effects=True, vmem_limit_bytes=56 << 20
        ),
    )(*[pltpu.with_memory_space_constraint(a, pltpu.HBM) for a in operands])
    return pl.pallas_call(
        emit_kernel,
        out_shape=(
            jax.ShapeDtypeStruct(residual.shape, f32),
            jax.ShapeDtypeStruct(grad.shape, f32),
        ),
        in_specs=[vmem] * 2,
        out_specs=[hbm] * 2,
        scratch_shapes=[dma(2)],
    )(residual, grad)


def on_device(
    tile_spectral_lines,
    taper_leading_axis,
    taper_trailing_axis,
    depth_layer_factors,
    measured_correlations,
    visibility_groups_table,
    antenna_links,
    complex_receiver_factors,
):
    sizes = tuple(lax.axis_size(name) for name in ("facet", "pol", "tm"))
    subgrids, pols, owners = sizes
    slots = taper_leading_axis.shape[2]
    quarter = measured_correlations.shape[3]
    rows = tile_spectral_lines.shape[3]

    block_table = visibility_groups_table.reshape(3, visibility_groups_table.shape[3])
    observed = measured_correlations.reshape(2 * NPOL, quarter)

    if tile_spectral_lines.shape[0] % FGRID == 0:
        table_re, table_im, second = [jnp.asarray(t) for t in subgrid_tables()]
        own_count = NST // (subgrids * pols * owners)
        residual, gain_grad = fused(
            sizes,
            own_count,
            visibility_groups_table.reshape(3, 1, visibility_groups_table.shape[3]),
            jnp.transpose(antenna_links.reshape(2, -1, 128), (1, 0, 2)),
            complex_receiver_factors,
            *[jnp.asarray(t) for t in fourier_factors(subgrids)],
            tile_spectral_lines[:, 0],
            taper_leading_axis.reshape(slots, SG),
            taper_trailing_axis.reshape(slots, SG),
            depth_layer_factors.reshape(NW, slots),
            observed,
            table_re.reshape(FGRID, owners, rows, SG),
            table_im.reshape(FGRID, owners, rows, SG),
            second,
            jnp.asarray(np.stack(chirp_line())),
        )
        return residual.reshape(1, 2 * NPOL, 1, quarter), gain_grad

    contrib, gains, idents = fourier(
        tile_spectral_lines[:, 0],
        subgrids,
        slots,
        block_table,
        antenna_links,
        complex_receiver_factors,
    )
    table_re, table_im, second = [jnp.asarray(t) for t in subgrid_tables()]
    cosine, sine = chirp_line()
    own_count = NST // (subgrids * pols * owners)
    residual, grad = predict(
        sizes,
        own_count,
        contrib,
        taper_leading_axis.reshape(slots, SG),
        taper_trailing_axis.reshape(slots, SG),
        depth_layer_factors.reshape(NW, slots),
        observed,
        gains,
        idents,
        table_re.reshape(FGRID, owners, rows, SG),
        table_im.reshape(FGRID, owners, rows, SG),
        second,
        jnp.asarray(np.stack([cosine, sine])),
    )
    gain_grad = jnp.transpose(grad, (1, 2, 0)).reshape(own_count, 4 * NCH)
    return residual.reshape(1, 2 * NPOL, 1, quarter), gain_grad


def solution(mesh):
    return jax.shard_map(
        on_device,
        mesh=mesh,
        in_specs=(
            P("facet", "pol", None, "tm", None),
            P("facet", "tm", None, None),
            P("facet", "tm", None, None),
            P("facet", "tm", None, None),
            P("facet", None, "tm", "pol"),
            P("facet", "tm", None, None),
            P(),
            P(),
        ),
        out_specs=(P("facet", None, "tm", "pol"), P(("facet", "pol", "tm"), None)),
        check_vma=False,
    )
```

```python
import functools
import math

import jax
import jax.numpy as jnp
import numpy as np
from jax import lax
from jax.experimental import pallas as pl
from jax.experimental.pallas import tpu as pltpu
from jax.sharding import PartitionSpec as P

FGRID = 8
FS = 4096
MC = 64
SG = 512
NPOL = 4
NW = 2
NCH = 256
NST = 512
CHUNK = 1024
PIECES = 2

w_chirp = 0.37
grad_scale = 0.1


def unit_angles(left, right, length):
    product = np.outer(np.arange(left), np.arange(right)) % length
    return 2.0 * math.pi * product / length


def fourier_factors(subgrids):
    spread = FS // MC
    alpha = unit_angles(FS // spread, MC, MC)
    p = np.concatenate([np.cos(alpha), -np.sin(alpha)], axis=1) / math.sqrt(FS)
    q = np.concatenate([-np.sin(alpha), -np.cos(alpha)], axis=1) / math.sqrt(FS)
    beta = unit_angles(spread, subgrids * MC, FS).reshape(spread, subgrids, 1, MC)
    beta = np.broadcast_to(beta, (spread, subgrids, 2, MC)).reshape(spread, subgrids * 2 * MC)
    tile = lambda t: np.tile(t, (1, subgrids)).astype(np.float32)
    return (
        tile(p),
        tile(q),
        np.cos(beta).astype(np.float32),
        np.sin(beta).astype(np.float32),
    )


def fetch_lookups(block_ref, links_ref, gain_ref, window, channel_gain, window_sem, gain_sem):
    blocks, _, span = window.shape
    copies = []
    for b in range(blocks):
        first = jnp.minimum(block_ref[1, b] // 128 * 128, links_ref.shape[1] - span)
        first = pl.multiple_of(first, 128)
        copies.append(
            pltpu.make_async_copy(
                links_ref.at[:, pl.ds(first, span)], window.at[b], window_sem.at[b]
            )
        )
        copies.append(
            pltpu.make_async_copy(
                gain_ref.at[block_ref[0, b]], channel_gain.at[b], gain_sem.at[b]
            )
        )
    return copies


def use_lookups(block_ref, links_ref, window, channel_gain, gains_ref, idents_ref):
    blocks, _, span = window.shape
    slots = idents_ref.shape[1]
    lane = lax.broadcasted_iota(jnp.int32, (1, slots), 1)
    place = lax.broadcasted_iota(jnp.int32, (span, slots), 0)
    lane_tall = lax.broadcasted_iota(jnp.int32, (span, slots), 1)
    begin = jnp.int32(0)
    member, picks = [], []
    channel = jnp.zeros((1, slots), jnp.float32)
    alive = jnp.zeros((1, slots), jnp.float32)
    for b in range(blocks):
        offset, amount = block_ref[1, b], block_ref[2, b]
        first = jnp.minimum(offset // 128 * 128, links_ref.shape[1] - span)
        inside = jnp.where((lane >= begin) & (lane < begin + amount), 1.0, 0.0)
        member.append(inside)
        alive += inside
        channel += inside * block_ref[0, b].astype(jnp.float32)
        hit = place == lane_tall + (offset - first - begin)
        picks.append((jnp.where(hit, 1.0, 0.0) * inside).astype(jnp.bfloat16))
        begin = begin + amount
    links = jnp.concatenate([window[b] for b in range(blocks)], axis=1)
    upper = links // 16
    lower = links - 16 * upper
    pieces = jnp.concatenate([upper, lower], axis=0).astype(jnp.float32).astype(jnp.bfloat16)
    found = jnp.dot(
        pieces, jnp.concatenate(picks, axis=0), preferred_element_type=jnp.float32
    )
    stations = 16.0 * found[0:2] + found[2:4]
    table = channel_gain[...].reshape(blocks * 4, channel_gain.shape[2])
    high = table.astype(jnp.bfloat16)
    rest = table - high.astype(jnp.float32)
    middle = rest.astype(jnp.bfloat16)
    low = (rest - middle.astype(jnp.float32)).astype(jnp.bfloat16)
    names = lax.broadcasted_iota(jnp.int32, (table.shape[1], 1), 0).astype(jnp.float32)
    for side in range(2):
        pick = jnp.where(names == stations[side : side + 1], 1.0, 0.0).astype(jnp.bfloat16)
        rows = (
            jnp.dot(high, pick, preferred_element_type=jnp.float32)
            + jnp.dot(middle, pick, preferred_element_type=jnp.float32)
            + jnp.dot(low, pick, preferred_element_type=jnp.float32)
        )
        chosen = member[0] * rows[0:4]
        for b in range(1, blocks):
            chosen = chosen + member[b] * rows[4 * b : 4 * b + 4]
        gains_ref[4 * side : 4 * side + 4, :] = chosen
    idents_ref[0:2, :] = stations
    idents_ref[2:3, :] = channel
    idents_ref[3:4, :] = alive
    idents_ref[4:8, :] = jnp.zeros((4, slots), jnp.float32)


def fourier_kernel(
    block_ref,
    links_ref,
    gain_ref,
    p_ref,
    q_ref,
    c_ref,
    s_ref,
    x_ref,
    o_ref,
    gains_ref,
    idents_ref,
    table,
    total,
    window,
    channel_gain,
    window_sem,
    gain_sem,
):
    step = pl.program_id(0)
    copies = fetch_lookups(
        block_ref, links_ref, gain_ref, window, channel_gain, window_sem, gain_sem
    )

    @pl.when(step == 0)
    def _():
        for copy in copies:
            copy.start()

    @pl.when(step == pl.num_programs(0) - 1)
    def _():
        for copy in copies:
            copy.wait()
        use_lookups(block_ref, links_ref, window, channel_gain, gains_ref, idents_ref)

    facets, _, rows, chunk = x_ref.shape
    subgrids = o_ref.shape[0]
    spread = c_ref.shape[0]
    cosine, sine = c_ref[...], s_ref[...]
    for part in range(chunk // spread):
        lead = p_ref[part : part + 1, :]
        other = q_ref[part : part + 1, :]
        table[part * spread : (part + 1) * spread, :] = (lead * cosine + other * sine).astype(
            jnp.bfloat16
        )
    x = x_ref[...].reshape(facets * 2 * rows, chunk)
    product = jnp.dot(x, table[...], preferred_element_type=jnp.float32)

    @pl.when(step == 0)
    def _():
        total[...] = product

    @pl.when(step > 0)
    def _():
        total[...] += product

    @pl.when(step == pl.num_programs(0) - 1)
    def _():
        lane = lax.broadcasted_iota(jnp.int32, (rows, 2 * MC), 1)
        sign = jnp.where(lane < MC, -1.0, 1.0)
        packed = o_ref.shape[3] // (2 * MC)
        for f in range(facets):
            for s in range(subgrids):
                cut = slice(s * 2 * MC, (s + 1) * 2 * MC)
                first = total[2 * f * rows : (2 * f + 1) * rows, cut]
                second = total[(2 * f + 1) * rows : (2 * f + 2) * rows, cut]
                value = first + sign * pltpu.roll(second, MC, 1)
                j = f % packed
                o_ref[s, f // packed, :, j * 2 * MC : (j + 1) * 2 * MC] = value.astype(jnp.bfloat16)


def fourier(x, subgrids, slots, block_table, links, station_gains):
    facets, _, rows, length = x.shape
    width = subgrids * 2 * MC
    spread = FS // MC
    packed = FGRID if facets % FGRID == 0 else 1
    per_step = CHUNK // spread
    blocks = block_table.shape[1]
    span = slots + 128
    in_place = lambda array: pltpu.with_memory_space_constraint(array, pltpu.HBM)
    factors = [in_place(jnp.asarray(t)) for t in fourier_factors(subgrids)]
    out = (subgrids, facets // packed, rows, packed * 2 * MC)
    return pl.pallas_call(
        fourier_kernel,
        out_shape=(
            jax.ShapeDtypeStruct(out, jnp.bfloat16),
            jax.ShapeDtypeStruct((8, slots), jnp.float32),
            jax.ShapeDtypeStruct((8, slots), jnp.float32),
        ),
        grid=(length // CHUNK,),
        in_specs=[
            pl.BlockSpec(memory_space=pltpu.SMEM),
            pl.BlockSpec(memory_space=pltpu.HBM),
            pl.BlockSpec(memory_space=pltpu.HBM),
            pl.BlockSpec((per_step, width), lambda g: (g, 0)),
            pl.BlockSpec((per_step, width), lambda g: (g, 0)),
            pl.BlockSpec((spread, width), lambda g: (0, 0)),
            pl.BlockSpec((spread, width), lambda g: (0, 0)),
            pl.BlockSpec((facets, 2, rows, CHUNK), lambda g: (0, 0, 0, g)),
        ],
        out_specs=(
            pl.BlockSpec(out, lambda g: (0, 0, 0, 0)),
            pl.BlockSpec((8, slots), lambda g: (0, 0)),
            pl.BlockSpec((8, slots), lambda g: (0, 0)),
        ),
        scratch_shapes=[
            pltpu.VMEM((CHUNK, width), jnp.bfloat16),
            pltpu.VMEM((facets * 2 * rows, width), jnp.float32),
            pltpu.VMEM((blocks, 2, span), jnp.int32),
            pltpu.VMEM((blocks, 4, NST), jnp.float32),
            pltpu.SemaphoreType.DMA((blocks,)),
            pltpu.SemaphoreType.DMA((blocks,)),
        ],
        compiler_params=pltpu.CompilerParams(
            dimension_semantics=("arbitrary",), vmem_limit_bytes=48 << 20
        ),
    )(
        block_table,
        in_place(links),
        in_place(station_gains),
        *factors,
        x,
    )


def subgrid_tables():
    angle = unit_angles(SG, SG, SG)
    re = np.cos(angle) / math.sqrt(SG)
    im = np.sin(angle) / math.sqrt(SG)
    blocks = lambda t: t.reshape(SG, FGRID, MC)
    second = np.stack([blocks(re), -blocks(im)], axis=2).reshape(SG, 2 * SG)
    return [t.astype(jnp.bfloat16) for t in (re, im, second)]


def chirp_line():
    offset = np.arange(SG) - SG // 2
    angle = 2.0 * math.pi * w_chirp * (offset * offset) / float(SG * SG)
    return np.cos(angle).astype(np.float32), np.sin(angle).astype(np.float32)


def model_terms(pred, observed, first, second, alive):
    residual, lead, trail = [], [], []
    for p in range(NPOL):
        f1, f2 = p // 2, p % 2
        pred_re, pred_im = pred[p]
        first_re, first_im = first[2 * f1], first[2 * f1 + 1]
        second_re, second_im = second[2 * f2], second[2 * f2 + 1]
        both_re = first_re * second_re + first_im * second_im
        both_im = first_im * second_re - first_re * second_im
        resid_re = alive * (observed[2 * p] - (both_re * pred_re - both_im * pred_im))
        resid_im = alive * (observed[2 * p + 1] - (both_re * pred_im + both_im * pred_re))
        cross_re = second_re * pred_re + second_im * pred_im
        cross_im = second_im * pred_re - second_re * pred_im
        along_re = first_re * pred_re - first_im * pred_im
        along_im = first_re * pred_im + first_im * pred_re
        residual += [resid_re, resid_im]
        lead.append(
            (-(resid_re * cross_re - resid_im * cross_im), -(resid_re * cross_im + resid_im * cross_re))
        )
        trail.append(
            (-(resid_re * along_re + resid_im * along_im), -(resid_re * along_im - resid_im * along_re))
        )
    leading = [lead[2 * f][r] + lead[2 * f + 1][r] for f in range(2) for r in range(2)]
    trailing = [trail[f][r] + trail[f + 2][r] for f in range(2) for r in range(2)]
    return residual, leading, trailing


def nt_dot(left, right, **kw):
    return lax.dot_general(
        left, right, (((1,), (1,)), ((), ())), preferred_element_type=jnp.float32, **kw
    )


def chirped_rows(taper, chirp_ref):
    wide = taper.astype(jnp.float32)
    return jnp.concatenate(
        [
            taper,
            (wide * chirp_ref[0:1, :]).astype(jnp.bfloat16),
            (wide * chirp_ref[1:2, :]).astype(jnp.bfloat16),
        ],
        axis=0,
    )


def predict_kernel(
    sizes,
    contrib_ref,
    lead_ref,
    trail_ref,
    depth_ref,
    observed_ref,
    gains_ref,
    idents_ref,
    table_re_ref,
    table_im_ref,
    second_ref,
    chirp_ref,
    residual_ref,
    grad_ref,
    got,
    lines,
    tapers,
    right,
    left,
    part_out,
    part_in,
    observed_out,
    observed_in,
    record_out,
    record_in,
    got_send,
    got_recv,
    taper_send,
    taper_recv,
    observed_send,
    observed_recv,
    part_send,
    part_recv,
    record_send,
    record_recv,
):
    subgrids, pols, owners = sizes
    z, p, t = lax.axis_index("facet"), lax.axis_index("pol"), lax.axis_index("tm")
    slots = lead_ref.shape[0]
    _, groups, rows, width = contrib_ref.shape
    mesh_id = pl.DeviceIdType.MESH

    def remote(src, dst, send, recv, peer):
        return pltpu.make_async_remote_copy(
            src_ref=src,
            dst_ref=dst,
            send_sem=send,
            recv_sem=recv,
            device_id=peer,
            device_id_type=mesh_id,
        )

    across_total = subgrids * owners
    plane_total = pols * owners
    across = z * owners + t
    plane = p * owners + t

    def across_peer(d):
        other = lax.rem(across + d, across_total)
        return other, (other // owners, p, lax.rem(other, owners))

    def plane_peer(d):
        other = lax.rem(plane + d, plane_total)
        return other, (z, other // owners, lax.rem(other, owners))

    barrier = pltpu.get_barrier_semaphore()
    for d in range(1, across_total):
        pl.semaphore_signal(barrier, inc=1, device_id=across_peer(d)[1], device_id_type=mesh_id)
    for d in range(1, pols):
        q = lax.rem(p + d, pols)
        for o in range(owners):
            pl.semaphore_signal(barrier, inc=1, device_id=(z, q, o), device_id_type=mesh_id)
    pl.semaphore_wait(barrier, across_total - 1 + (pols - 1) * owners)

    quarter = observed_ref.shape[1]
    place = lax.broadcasted_iota(jnp.int32, (2 * NPOL, slots), 1)
    observed_out[...] = jnp.where(
        (place >= p * quarter) & (place < (p + 1) * quarter),
        jnp.concatenate([observed_ref[...]] * pols, axis=1),
        0.0,
    )
    copies = []
    for d in sorted(range(1, subgrids), key=lambda d: -min(d, subgrids - d)):
        other = lax.rem(z + d, subgrids)
        copies.append(
            remote(contrib_ref.at[other], got.at[z], got_send.at[d], got_recv.at[d], (other, p, t))
        )
    partner = lax.rem(t + 1, owners)
    taper_copies = [
        remote(ref, tapers.at[t, k], taper_send.at[k], taper_recv.at[k], (z, p, partner))
        for k, ref in enumerate((trail_ref, lead_ref))
    ]
    observed_copies = []
    for d in range(1, pols):
        q = lax.rem(p + d, pols)
        observed_copies.append(
            remote(
                observed_out, observed_in.at[p], observed_send.at[d], observed_recv.at[d], (z, q, t)
            )
        )
    for copy in copies + taper_copies + observed_copies:
        copy.start()

    table_re = jnp.concatenate([table_re_ref[i, t] for i in range(FGRID)], axis=0)
    table_im = jnp.concatenate([table_im_ref[i, t] for i in range(FGRID)], axis=0)

    turn = jnp.where(
        lax.broadcasted_iota(jnp.int32, (3 * slots, 2 * MC), 1) < MC, -1.0, 1.0
    )

    def prepare(owner, trail, lead):
        trail3 = chirped_rows(trail, chirp_ref)
        a = jnp.dot(trail3, second_ref[...], preferred_element_type=jnp.float32)
        b = jnp.concatenate(
            [
                turn * pltpu.roll(a[:, j * 2 * MC : (j + 1) * 2 * MC], MC, 1)
                for j in range(a.shape[1] // (2 * MC))
            ],
            axis=1,
        )
        n0, n1, n2 = slice(0, slots), slice(slots, 2 * slots), slice(2 * slots, 3 * slots)
        right[owner, 0:slots, :] = a[n0].astype(jnp.bfloat16)
        right[owner, slots : 2 * slots, :] = (a[n1] - b[n2]).astype(jnp.bfloat16)
        right[owner, 2 * slots : 3 * slots, :] = b[n0].astype(jnp.bfloat16)
        right[owner, 3 * slots : 4 * slots, :] = (b[n1] + a[n2]).astype(jnp.bfloat16)
        lead3 = chirped_rows(lead, chirp_ref)
        u = nt_dot(table_re, lead3)
        v = nt_dot(table_im, lead3)
        left[owner, 0] = u[:, n0]
        left[owner, 1] = v[:, n0]
        left[owner, 2] = u[:, n1] - v[:, n2]
        left[owner, 3] = u[:, n2] + v[:, n1]

    prepare(t, trail_ref[...], lead_ref[...])
    got[z] = contrib_ref[z]
    for copy in taper_copies:
        copy.wait()
    prepare(partner, tapers[partner, 0], tapers[partner, 1])
    for copy in copies:
        copy.wait()
    if width == 2 * SG:
        whole = got[...].reshape(subgrids * groups * rows, width)
    else:
        for f in range(subgrids * groups):
            i, j = f // FGRID, f % FGRID
            lines[i * rows : (i + 1) * rows, j * 2 * MC : (j + 1) * 2 * MC] = got[
                f // groups, f % groups
            ]
        whole = lines[...]
    for o in range(owners):
        spread = nt_dot(whole, right[o])
        for w in range(NW):
            g_re = spread[:, w * slots : (w + 1) * slots]
            g_im = spread[:, (NW + w) * slots : (NW + w + 1) * slots]
            l_re, l_im = left[o, 2 * w], left[o, 2 * w + 1]
            part_out[o, 2 * w : 2 * w + 1, :] = jnp.sum(l_re * g_re - l_im * g_im, axis=0, keepdims=True)
            part_out[o, 2 * w + 1 : 2 * w + 2, :] = jnp.sum(
                l_re * g_im + l_im * g_re, axis=0, keepdims=True
            )
        part_out[o, 2 * NW :, :] = jnp.zeros((8 - 2 * NW, slots), jnp.float32)

    part_copies = []
    for d in range(1, plane_total):
        other, peer = plane_peer(d)
        part_copies.append(
            remote(
                part_out.at[lax.rem(other, owners)],
                part_in.at[plane],
                part_send.at[d],
                part_recv.at[d],
                peer,
            )
        )
    for copy in part_copies:
        copy.start()
    part_in[plane] = part_out[t]
    observed_in[p] = observed_out[...]
    for copy in observed_copies:
        copy.wait()
    observed = observed_in[0]
    for q in range(1, pols):
        observed = observed + observed_in[q]
    depth = depth_ref[...].astype(jnp.float32)
    for copy in part_copies:
        copy.wait()

    pred = []
    per_pol = part_in.shape[0] // NPOL
    for q in range(NPOL):
        block = part_in[q * per_pol]
        for o in range(1, per_pol):
            block = block + part_in[q * per_pol + o]
        pred.append(
            tuple(
                sum(depth[w : w + 1] * block[2 * w + c : 2 * w + c + 1] for w in range(NW))
                for c in range(2)
            )
        )
    gains = gains_ref[...]
    idents = idents_ref[...]
    residual, leading, trailing = model_terms(
        pred,
        [observed[k : k + 1] for k in range(2 * NPOL)],
        [gains[k : k + 1] for k in range(4)],
        [gains[4 + k : 5 + k] for k in range(4)],
        idents[3:4],
    )
    for k in range(3):
        record_out[k : k + 1, :] = idents[k : k + 1]
    for k in range(4):
        record_out[3 + k : 4 + k, :] = leading[k]
        record_out[7 + k : 8 + k, :] = trailing[k]
    record_out[11:, :] = jnp.zeros((5, slots), jnp.float32)
    record_copies = []
    for d in range(1, across_total):
        other, peer = across_peer(d)
        record_copies.append(
            remote(record_out, record_in.at[across], record_send.at[d], record_recv.at[d], peer)
        )
    for copy in record_copies:
        copy.start()
    record_in[across] = record_out[...]
    rest = jnp.concatenate(residual, axis=0)
    own_rest = jnp.zeros((2 * NPOL, quarter), jnp.float32)
    for q in range(pols):
        own_rest = jnp.where(p == q, rest[:, q * quarter : (q + 1) * quarter], own_rest)
    residual_ref[...] = own_rest
    for copy in record_copies:
        copy.wait()

    piece = jnp.concatenate([record_in[d] for d in range(across_total)], axis=1)
    own_count = grad_ref.shape[1]
    index = (z * pols + p) * owners + t
    mine = (index * own_count + lax.broadcasted_iota(jnp.int32, (own_count, 1), 0)).astype(
        jnp.float32
    )
    match_first = mine == piece[0:1]
    match_second = mine == piece[1:2]
    weighted = jnp.concatenate(
        [
            jnp.where(match_first, piece[3 + k : 4 + k], 0.0)
            + jnp.where(match_second, piece[7 + k : 8 + k], 0.0)
            for k in range(4)
        ],
        axis=0,
    )
    high = weighted.astype(jnp.bfloat16)
    low = (weighted - high.astype(jnp.float32)).astype(jnp.bfloat16)
    channel_ids = lax.broadcasted_iota(jnp.int32, (NCH, 1), 0).astype(jnp.float32)
    onehot = jnp.where(channel_ids == piece[2:3], 1.0, 0.0).astype(jnp.bfloat16)
    summed = nt_dot(high, onehot) + nt_dot(low, onehot)
    for k in range(4):
        grad_ref[k] = grad_scale * summed[k * own_count : (k + 1) * own_count]


def predict(sizes, own_count, *operands):
    subgrids, pols, owners = sizes
    contrib, lead = operands[0], operands[1]
    _, groups, rows, width = contrib.shape
    slots = lead.shape[0]
    vmem = pl.BlockSpec(memory_space=pltpu.VMEM)
    dma = lambda n: pltpu.SemaphoreType.DMA((n,))
    across_total, plane_total = subgrids * owners, pols * owners
    return pl.pallas_call(
        functools.partial(predict_kernel, sizes),
        out_shape=(
            jax.ShapeDtypeStruct((2 * NPOL, slots // pols), jnp.float32),
            jax.ShapeDtypeStruct((4, own_count, NCH), jnp.float32),
        ),
        in_specs=[vmem] * len(operands),
        out_specs=(vmem, vmem),
        scratch_shapes=[
            pltpu.VMEM(contrib.shape, jnp.bfloat16),
            pltpu.VMEM((FGRID * rows, 2 * SG), jnp.bfloat16),
            pltpu.VMEM((owners, 2, slots, SG), jnp.bfloat16),
            pltpu.VMEM((owners, 2 * NW * slots, 2 * SG), jnp.bfloat16),
            pltpu.VMEM((owners, 4, FGRID * rows, slots), jnp.float32),
            pltpu.VMEM((owners, 8, slots), jnp.float32),
            pltpu.VMEM((plane_total, 8, slots), jnp.float32),
            pltpu.VMEM((8, slots), jnp.float32),
            pltpu.VMEM((pols, 8, slots), jnp.float32),
            pltpu.VMEM((16, slots), jnp.float32),
            pltpu.VMEM((across_total, 16, slots), jnp.float32),
            dma(subgrids),
            dma(subgrids),
            dma(2),
            dma(2),
            dma(pols),
            dma(pols),
            dma(plane_total),
            dma(plane_total),
            dma(across_total),
            dma(across_total),
        ],
        compiler_params=pltpu.CompilerParams(
            collective_id=0, has_side_effects=True, vmem_limit_bytes=48 << 20
        ),
    )(*operands)


def gather_lookups(block_ref, links_ref, gain_ref, gains_ref, idents_ref):
    blocks = block_ref.shape[2]
    slots = idents_ref.shape[1]
    span = slots + 128
    lane = lax.broadcasted_iota(jnp.int32, (1, slots), 1)
    place = lax.broadcasted_iota(jnp.int32, (span, slots), 0)
    lane_tall = lax.broadcasted_iota(jnp.int32, (span, slots), 1)
    begin = jnp.int32(0)
    member, picks, windows, tables = [], [], [], []
    channel = jnp.zeros((1, slots), jnp.float32)
    alive = jnp.zeros((1, slots), jnp.float32)
    for b in range(blocks):
        chosen, offset, amount = [block_ref[k, 0, b] for k in range(3)]
        row = jnp.minimum(lax.div(offset, 128), links_ref.shape[0] - span // 128)
        first = row * 128
        windows += [links_ref[row + k] for k in range(span // 128)]
        tables.append(gain_ref[chosen])
        inside = jnp.where((lane >= begin) & (lane < begin + amount), 1.0, 0.0)
        member.append(inside)
        alive += inside
        channel += inside * chosen.astype(jnp.float32)
        hit = place == lane_tall + (offset - first - begin)
        picks.append((jnp.where(hit, 1.0, 0.0) * inside).astype(jnp.bfloat16))
        begin = begin + amount
    links = jnp.concatenate(windows, axis=1)
    upper = links // 16
    lower = links - 16 * upper
    pieces = jnp.concatenate([upper, lower], axis=0).astype(jnp.float32).astype(jnp.bfloat16)
    found = jnp.dot(
        pieces, jnp.concatenate(picks, axis=0), preferred_element_type=jnp.float32
    )
    stations = 16.0 * found[0:2] + found[2:4]
    table = jnp.concatenate(tables, axis=0)
    high = table.astype(jnp.bfloat16)
    rest = table - high.astype(jnp.float32)
    middle = rest.astype(jnp.bfloat16)
    low = (rest - middle.astype(jnp.float32)).astype(jnp.bfloat16)
    split = jnp.concatenate([high, middle, low], axis=0)
    size = table.shape[0]
    names = lax.broadcasted_iota(jnp.int32, (table.shape[1], 1), 0).astype(jnp.float32)
    for side in range(2):
        pick = jnp.where(names == stations[side : side + 1], 1.0, 0.0).astype(jnp.bfloat16)
        three = jnp.dot(split, pick, preferred_element_type=jnp.float32)
        rows = three[:size] + three[size : 2 * size] + three[2 * size :]
        chosen = member[0] * rows[0:4]
        for b in range(1, blocks):
            chosen = chosen + member[b] * rows[4 * b : 4 * b + 4]
        gains_ref[4 * side : 4 * side + 4, :] = chosen
    idents_ref[0:2, :] = stations
    idents_ref[2:3, :] = channel
    idents_ref[3:4, :] = alive
    idents_ref[4:8, :] = jnp.zeros((4, slots), jnp.float32)


def fused_kernel(
    sizes,
    block_hbm,
    links_hbm,
    gain_hbm,
    p_hbm,
    q_hbm,
    c_hbm,
    s_hbm,
    x_hbm,
    lead_hbm,
    trail_hbm,
    depth_hbm,
    observed_hbm,
    table_re_hbm,
    table_im_hbm,
    second_hbm,
    chirp_hbm,
    residual_ref,
    grad_ref,
    block_ref,
    links_ref,
    gain_ref,
    p_ref,
    q_ref,
    c_ref,
    s_ref,
    x_ref,
    lead_ref,
    trail_ref,
    depth_ref,
    observed_ref,
    table_ref,
    second_ref,
    chirp_ref,
    factors,
    contrib,
    got,
    tapers,
    right,
    left,
    gains_ref,
    idents_ref,
    depths,
    side,
    part_out,
    part_in,
    observed_out,
    observed_in,
    rests,
    load_sem,
    chunk_sem,
    got_send,
    got_recv,
    taper_send,
    taper_recv,
    observed_send,
    observed_recv,
    side_send,
    side_recv,
    part_send,
    part_recv,
):
    subgrids, pols, owners = sizes
    z, p, t = lax.axis_index("facet"), lax.axis_index("pol"), lax.axis_index("tm")
    slots = lead_ref.shape[0]
    facets, _, rows, length = x_ref.shape
    _, groups, _, width = contrib.shape
    mesh_id = pl.DeviceIdType.MESH

    def remote(src, dst, send, recv, peer):
        return pltpu.make_async_remote_copy(
            src_ref=src,
            dst_ref=dst,
            send_sem=send,
            recv_sem=recv,
            device_id=peer,
            device_id_type=mesh_id,
        )

    across_total = subgrids * owners
    across = z * owners + t

    def across_peer(d):
        other = lax.rem(across + d, across_total)
        return other, (other // owners, p, lax.rem(other, owners))

    barrier = pltpu.get_barrier_semaphore()
    for d in range(1, across_total):
        pl.semaphore_signal(barrier, inc=1, device_id=across_peer(d)[1], device_id_type=mesh_id)
    for d in range(1, pols):
        q = lax.rem(p + d, pols)
        for o in range(owners):
            pl.semaphore_signal(barrier, inc=1, device_id=(z, q, o), device_id_type=mesh_id)

    offsets = [
        (dz, dp, dt)
        for dz in sorted(range(subgrids), key=lambda d: -min(d, subgrids - d))
        for dp in reversed(range(pols))
        for dt in range(owners)
    ]
    offsets.remove((0, 0, 0))
    per_chunk = FGRID // PIECES
    chunks = facets // per_chunk
    x_loads = [
        pltpu.make_async_copy(
            x_hbm.at[pl.ds(c * per_chunk, per_chunk)],
            x_ref.at[pl.ds(c * per_chunk, per_chunk)],
            chunk_sem.at[c],
        )
        for c in range(chunks)
    ]
    pairs = [
        (c_hbm, c_ref),
        (s_hbm, s_ref),
        (p_hbm, p_ref),
        (q_hbm, q_ref),
        (lead_hbm, lead_ref),
        (trail_hbm, trail_ref),
        (depth_hbm, depth_ref),
        (observed_hbm, observed_ref),
        (chirp_hbm, chirp_ref),
        (second_hbm, second_ref),
        (table_re_hbm.at[:, t], table_ref.at[0]),
        (table_im_hbm.at[:, t], table_ref.at[1]),
        (block_hbm, block_ref),
        (links_hbm, links_ref),
        (gain_hbm, gain_ref),
    ]
    loads = [
        pltpu.make_async_copy(src, dst, load_sem.at[k]) for k, (src, dst) in enumerate(pairs)
    ]
    for copy in loads[:4]:
        copy.start()
    x_loads[0].start()
    for copy in loads[4:9]:
        copy.start()
    for copy in x_loads[1:]:
        copy.start()
    for copy in loads[9:]:
        copy.start()

    for copy in loads[:4]:
        copy.wait()
    spread = c_ref.shape[0]
    cosine, sine = c_ref[...], s_ref[...]
    for part in range(length // spread):
        factors[part * spread : (part + 1) * spread, :] = (
            p_ref[part : part + 1, :] * cosine + q_ref[part : part + 1, :] * sine
        ).astype(jnp.bfloat16)

    lane = lax.broadcasted_iota(jnp.int32, (rows, 2 * MC), 1)
    sign = jnp.where(lane < MC, -1.0, 1.0)
    part_width = width // PIECES
    partner = lax.rem(t + 1, owners)
    copies, taper_copies, observed_copies = [], [], []
    for c in range(chunks):
        x_loads[c].wait()
        x = x_ref[c * per_chunk : (c + 1) * per_chunk].reshape(per_chunk * 2 * rows, length)
        total = jnp.dot(x, factors[...], preferred_element_type=jnp.float32)
        group, piece = c // PIECES, c % PIECES
        for s in range(subgrids):
            cut = slice(s * 2 * MC, (s + 1) * 2 * MC)
            for f in range(per_chunk):
                first = total[2 * f * rows : (2 * f + 1) * rows, cut]
                second = total[(2 * f + 1) * rows : (2 * f + 2) * rows, cut]
                j = piece * per_chunk + f
                contrib[s, group, :, j * 2 * MC : (j + 1) * 2 * MC] = (
                    first + sign * pltpu.roll(second, MC, 1)
                ).astype(jnp.bfloat16)
        if c == 0:
            pl.semaphore_wait(barrier, across_total - 1 + (pols - 1) * owners)
        lanes = pl.ds(piece * part_width, part_width)
        for d in sorted(range(1, subgrids), key=lambda d: -min(d, subgrids - d)):
            other = lax.rem(z + d, subgrids)
            copy = remote(
                contrib.at[other, group, :, lanes],
                got.at[z, group, :, lanes],
                got_send.at[c * subgrids + d],
                got_recv.at[c * subgrids + d],
                (other, p, t),
            )
            copy.start()
            copies.append(copy)
        if c == 0:
            for copy in loads[4:9]:
                copy.wait()
            taper_copies = [
                remote(src, dst, taper_send.at[k], taper_recv.at[k], (z, p, partner))
                for k, (src, dst) in enumerate(
                    [
                        (trail_ref, tapers.at[0]),
                        (lead_ref, tapers.at[1]),
                        (depth_ref, depths),
                    ]
                )
            ]
            quarter = observed_ref.shape[1]
            place = lax.broadcasted_iota(jnp.int32, (2 * NPOL, slots), 1)
            observed_out[...] = jnp.where(
                (place >= p * quarter) & (place < (p + 1) * quarter),
                jnp.concatenate([observed_ref[...]] * pols, axis=1),
                0.0,
            )
            for d in range(1, pols):
                q = lax.rem(p + d, pols)
                observed_copies.append(
                    remote(
                        observed_out,
                        observed_in.at[p],
                        observed_send.at[d],
                        observed_recv.at[d],
                        (z, q, t),
                    )
                )
            for copy in taper_copies + observed_copies:
                copy.start()

    got[z] = contrib[z]
    for copy in loads[9:]:
        copy.wait()
    gather_lookups(block_ref, links_ref, gain_ref, gains_ref, idents_ref)
    observed_in[p] = observed_out[...]
    for copy in observed_copies:
        copy.wait()
    observed = observed_in[0]
    for q in range(1, pols):
        observed = observed + observed_in[q]
    side[across, 0:8] = gains_ref[...]
    side[across, 8:16] = observed
    side[across, 16:20] = idents_ref[0:4]
    side_copies = []
    for d in range(1, across_total):
        other, peer = across_peer(d)
        side_copies.append(
            remote(side.at[across], side.at[across], side_send.at[d], side_recv.at[d], peer)
        )
    for copy in side_copies:
        copy.start()

    table_re = jnp.concatenate([table_ref[0, i] for i in range(FGRID)], axis=0)
    table_im = jnp.concatenate([table_ref[1, i] for i in range(FGRID)], axis=0)
    turn = jnp.where(
        lax.broadcasted_iota(jnp.int32, (3 * slots, 2 * MC), 1) < MC, -1.0, 1.0
    )

    def prepare(owner, trail, lead):
        trail3 = chirped_rows(trail, chirp_ref)
        a = jnp.dot(trail3, second_ref[...], preferred_element_type=jnp.float32)
        b = jnp.concatenate(
            [
                turn * pltpu.roll(a[:, j * 2 * MC : (j + 1) * 2 * MC], MC, 1)
                for j in range(a.shape[1] // (2 * MC))
            ],
            axis=1,
        )
        n0, n1, n2 = slice(0, slots), slice(slots, 2 * slots), slice(2 * slots, 3 * slots)
        right[owner, 0:slots, :] = a[n0].astype(jnp.bfloat16)
        right[owner, slots : 2 * slots, :] = (a[n1] - b[n2]).astype(jnp.bfloat16)
        right[owner, 2 * slots : 3 * slots, :] = b[n0].astype(jnp.bfloat16)
        right[owner, 3 * slots : 4 * slots, :] = (b[n1] + a[n2]).astype(jnp.bfloat16)
        lead3 = chirped_rows(lead, chirp_ref)
        u = nt_dot(table_re, lead3)
        v = nt_dot(table_im, lead3)
        left[owner, 0] = u[:, n0]
        left[owner, 1] = v[:, n0]
        left[owner, 2] = u[:, n1] - v[:, n2]
        left[owner, 3] = u[:, n2] + v[:, n1]

    prepare(t, trail_ref[...], lead_ref[...])
    for copy in taper_copies:
        copy.wait()
    prepare(partner, tapers[0], tapers[1])
    for copy in copies:
        copy.wait()
    whole = got[...].reshape(subgrids * groups * rows, width)
    for o in range(owners):
        across_v = nt_dot(whole, right[o])
        sums = [0.0, 0.0]
        weights = jnp.where(o == t, depth_ref[...].astype(jnp.float32), depths[...].astype(jnp.float32))
        for w in range(NW):
            g_re = across_v[:, w * slots : (w + 1) * slots]
            g_im = across_v[:, (NW + w) * slots : (NW + w + 1) * slots]
            l_re, l_im = left[o, 2 * w], left[o, 2 * w + 1]
            weight = weights[w : w + 1]
            sums[0] += weight * jnp.sum(l_re * g_re - l_im * g_im, axis=0, keepdims=True)
            sums[1] += weight * jnp.sum(l_re * g_im + l_im * g_re, axis=0, keepdims=True)
        for c in range(2):
            part_out[owners * c + o : owners * c + o + 1, :] = sums[c]

    part_copies = []
    for dz, dp, dt in offsets:
        peer = (lax.rem(z + dz, subgrids), lax.rem(p + dp, pols), lax.rem(t + dt, owners))
        k = (dz * pols + dp) * owners + dt
        part_copies.append(
            remote(part_out, part_in.at[z, p, t], part_send.at[k], part_recv.at[k], peer)
        )
    for copy in part_copies:
        copy.start()
    part_in[z, p, t] = part_out[...]

    for copy in side_copies:
        copy.wait()
    own_count = grad_ref.shape[0]
    index = (z * pols + p) * owners + t
    mine = (index * own_count + lax.broadcasted_iota(jnp.int32, (own_count, 1), 0)).astype(
        jnp.float32
    )
    channel_ids = lax.broadcasted_iota(jnp.int32, (NCH, 1), 0).astype(jnp.float32)
    first_here = [jnp.where(mine == side[d, 16:17], 1.0, 0.0) for d in range(across_total)]
    second_here = [jnp.where(mine == side[d, 17:18], 1.0, 0.0) for d in range(across_total)]
    onehot = jnp.concatenate(
        [
            jnp.where(channel_ids == side[d, 18:19], 1.0, 0.0).astype(jnp.bfloat16)
            for d in range(across_total)
        ],
        axis=1,
    )
    column = lambda k: jnp.concatenate([side[d, k : k + 1] for d in range(across_total)], axis=0)
    gains = [column(k) for k in range(8)]
    observed = [column(8 + k) for k in range(8)]
    alive = column(19)
    for copy in part_copies:
        copy.wait()

    pred = [
        tuple(
            sum(
                jnp.concatenate(
                    [
                        part_in[y, q, o, owners * c : owners * (c + 1)]
                        for y in range(subgrids)
                    ],
                    axis=0,
                )
                for o in range(owners)
            )
            for c in range(2)
        )
        for q in range(NPOL)
    ]
    residual, leading, trailing = model_terms(pred, observed, gains[:4], gains[4:], alive)
    for k in range(2 * NPOL):
        rests[:, k : k + 1, :] = residual[k][:, None, :]
    rest = rests[across]
    quarter = observed_ref.shape[1]
    own_rest = jnp.zeros((2 * NPOL, quarter), jnp.float32)
    for q in range(pols):
        own_rest = jnp.where(p == q, rest[:, q * quarter : (q + 1) * quarter], own_rest)
    residual_ref[...] = own_rest

    weighted = jnp.concatenate(
        [
            jnp.concatenate(
                [
                    first_here[d] * leading[k][d : d + 1]
                    + second_here[d] * trailing[k][d : d + 1]
                    for d in range(across_total)
                ],
                axis=1,
            )
            for k in range(4)
        ],
        axis=0,
    )
    high = weighted.astype(jnp.bfloat16)
    low = (weighted - high.astype(jnp.float32)).astype(jnp.bfloat16)
    summed = nt_dot(high, onehot) + nt_dot(low, onehot)
    lane_group = lax.broadcasted_iota(jnp.int32, (own_count, 128), 1) // 32
    mixed = []
    for g in range(NCH // 32):
        base = g // 4 * 128
        built = None
        for k in range(4):
            block = summed[k * own_count : (k + 1) * own_count, base : base + 128]
            shift = 32 * (k - g % 4) % 128
            block = pltpu.roll(block, shift, 1) if shift else block
            built = block if built is None else jnp.where(lane_group == k, block, built)
        mixed.append(grad_scale * built)
    mixed = jnp.concatenate(mixed, axis=0)
    high = mixed.astype(jnp.bfloat16)
    low = (mixed - high.astype(jnp.float32)).astype(jnp.bfloat16)
    came = lax.broadcasted_iota(jnp.int32, (128, 128), 0)
    goes = lax.broadcasted_iota(jnp.int32, (128, 128), 1)
    order = jnp.where(goes == came % 32 * 4 + came // 32, 1.0, 0.0).astype(jnp.bfloat16)
    placed = jnp.dot(
        jnp.concatenate([high, low], axis=0), order, preferred_element_type=jnp.float32
    )
    placed = placed[: mixed.shape[0]] + placed[mixed.shape[0] :]
    for g in range(NCH // 32):
        grad_ref[:, g * 128 : (g + 1) * 128] = placed[g * own_count : (g + 1) * own_count]


def emit_kernel(residual_ref, grad_ref, residual_out, grad_out, sems):
    copies = [
        pltpu.make_async_copy(residual_ref, residual_out, sems.at[0]),
        pltpu.make_async_copy(grad_ref, grad_out, sems.at[1]),
    ]
    for copy in copies:
        copy.start()
    for copy in copies:
        copy.wait()


def fused(sizes, own_count, *operands):
    subgrids, pols, owners = sizes
    block_table, links, gains = operands[0:3]
    x, lead, trail, depth, observed = operands[7:12]
    facets, _, rows, length = x.shape
    slots = lead.shape[0]
    width = subgrids * 2 * MC
    spread = FS // MC
    groups = facets // FGRID
    chunks = facets // (FGRID // PIECES)
    hbm = pl.BlockSpec(memory_space=pltpu.HBM)
    vmem = pl.BlockSpec(memory_space=pltpu.VMEM)
    dma = lambda n: pltpu.SemaphoreType.DMA((n,))
    held = lambda a: pltpu.VMEM(a.shape, a.dtype)
    across_total, all_total = subgrids * owners, subgrids * pols * owners
    f32, bf16 = jnp.float32, jnp.bfloat16
    residual, grad = pl.pallas_call(
        functools.partial(fused_kernel, sizes),
        out_shape=(
            jax.ShapeDtypeStruct(observed.shape, f32),
            jax.ShapeDtypeStruct((own_count, 4 * NCH), f32),
        ),
        in_specs=[hbm] * len(operands),
        out_specs=(vmem, vmem),
        scratch_shapes=[
            pltpu.SMEM(block_table.shape, jnp.int32),
            held(links),
            held(gains),
            pltpu.VMEM((length // spread, width), f32),
            pltpu.VMEM((length // spread, width), f32),
            pltpu.VMEM((spread, width), f32),
            pltpu.VMEM((spread, width), f32),
            held(x),
            held(lead),
            held(trail),
            held(depth),
            held(observed),
            pltpu.VMEM((2, FGRID, rows, SG), bf16),
            pltpu.VMEM((SG, 2 * SG), bf16),
            pltpu.VMEM((2, SG), f32),
            pltpu.VMEM((length, width), bf16),
            pltpu.VMEM((subgrids, groups, rows, 2 * SG), bf16),
            pltpu.VMEM((subgrids, groups, rows, 2 * SG), bf16),
            pltpu.VMEM((2, slots, SG), bf16),
            pltpu.VMEM((owners, 2 * NW * slots, 2 * SG), bf16),
            pltpu.VMEM((owners, 4, FGRID * rows, slots), f32),
            pltpu.VMEM((8, slots), f32),
            pltpu.VMEM((8, slots), f32),
            held(depth),
            pltpu.VMEM((across_total, 20, slots), f32),
            pltpu.VMEM((2 * owners, slots), f32),
            pltpu.VMEM((subgrids, pols, owners, 2 * owners, slots), f32),
            pltpu.VMEM((8, slots), f32),
            pltpu.VMEM((pols, 8, slots), f32),
            pltpu.VMEM((across_total, 8, slots), f32),
            dma(15),
            dma(chunks),
            dma(chunks * subgrids),
            dma(chunks * subgrids),
            dma(3),
            dma(3),
            dma(pols),
            dma(pols),
            dma(across_total),
            dma(across_total),
            dma(all_total),
            dma(all_total),
        ],
        compiler_params=pltpu.CompilerParams(
            collective_id=0, has_side_effects=True, vmem_limit_bytes=36 << 20
        ),
    )(*[pltpu.with_memory_space_constraint(a, pltpu.HBM) for a in operands])
    return pl.pallas_call(
        emit_kernel,
        out_shape=(
            jax.ShapeDtypeStruct(residual.shape, f32),
            jax.ShapeDtypeStruct(grad.shape, f32),
        ),
        in_specs=[vmem] * 2,
        out_specs=[hbm] * 2,
        scratch_shapes=[dma(2)],
        compiler_params=pltpu.CompilerParams(vmem_limit_bytes=1 << 20),
    )(residual, grad)


def on_device(
    tile_spectral_lines,
    taper_leading_axis,
    taper_trailing_axis,
    depth_layer_factors,
    measured_correlations,
    visibility_groups_table,
    antenna_links,
    complex_receiver_factors,
):
    sizes = tuple(lax.axis_size(name) for name in ("facet", "pol", "tm"))
    subgrids, pols, owners = sizes
    slots = taper_leading_axis.shape[2]
    quarter = measured_correlations.shape[3]
    rows = tile_spectral_lines.shape[3]

    block_table = visibility_groups_table.reshape(3, visibility_groups_table.shape[3])
    observed = measured_correlations.reshape(2 * NPOL, quarter)

    if tile_spectral_lines.shape[0] % FGRID == 0:
        table_re, table_im, second = [jnp.asarray(t) for t in subgrid_tables()]
        own_count = NST // (subgrids * pols * owners)
        residual, gain_grad = fused(
            sizes,
            own_count,
            visibility_groups_table.reshape(3, 1, visibility_groups_table.shape[3]),
            jnp.transpose(antenna_links.reshape(2, -1, 128), (1, 0, 2)),
            complex_receiver_factors,
            *[jnp.asarray(t) for t in fourier_factors(subgrids)],
            tile_spectral_lines[:, 0],
            taper_leading_axis.reshape(slots, SG),
            taper_trailing_axis.reshape(slots, SG),
            depth_layer_factors.reshape(NW, slots),
            observed,
            table_re.reshape(FGRID, owners, rows, SG),
            table_im.reshape(FGRID, owners, rows, SG),
            second,
            jnp.asarray(np.stack(chirp_line())),
        )
        return residual.reshape(1, 2 * NPOL, 1, quarter), gain_grad

    contrib, gains, idents = fourier(
        tile_spectral_lines[:, 0],
        subgrids,
        slots,
        block_table,
        antenna_links,
        complex_receiver_factors,
    )
    table_re, table_im, second = [jnp.asarray(t) for t in subgrid_tables()]
    cosine, sine = chirp_line()
    own_count = NST // (subgrids * pols * owners)
    residual, grad = predict(
        sizes,
        own_count,
        contrib,
        taper_leading_axis.reshape(slots, SG),
        taper_trailing_axis.reshape(slots, SG),
        depth_layer_factors.reshape(NW, slots),
        observed,
        gains,
        idents,
        table_re.reshape(FGRID, owners, rows, SG),
        table_im.reshape(FGRID, owners, rows, SG),
        second,
        jnp.asarray(np.stack([cosine, sine])),
    )
    gain_grad = jnp.transpose(grad, (1, 2, 0)).reshape(own_count, 4 * NCH)
    return residual.reshape(1, 2 * NPOL, 1, quarter), gain_grad


def solution(mesh):
    return jax.shard_map(
        on_device,
        mesh=mesh,
        in_specs=(
            P("facet", "pol", None, "tm", None),
            P("facet", "tm", None, None),
            P("facet", "tm", None, None),
            P("facet", "tm", None, None),
            P("facet", None, "tm", "pol"),
            P("facet", "tm", None, None),
            P(),
            P(),
        ),
        out_specs=(P("facet", None, "tm", "pol"), P(("facet", "pol", "tm"), None)),
        check_vma=False,
    )
```

```python
import functools
import math

import jax
import jax.numpy as jnp
import numpy as np
from jax import lax
from jax.experimental import pallas as pl
from jax.experimental.pallas import tpu as pltpu
from jax.sharding import PartitionSpec as P

FGRID = 8
FS = 4096
MC = 64
SG = 512
NPOL = 4
NW = 2
NCH = 256
NST = 512
CHUNK = 1024
PIECES = 2
FORWARD = 2

w_chirp = 0.37
grad_scale = 0.1


def unit_angles(left, right, length):
    product = np.outer(np.arange(left), np.arange(right)) % length
    return 2.0 * math.pi * product / length


def fourier_factors(subgrids):
    spread = FS // MC
    alpha = unit_angles(FS // spread, MC, MC)
    p = np.concatenate([np.cos(alpha), -np.sin(alpha)], axis=1) / math.sqrt(FS)
    q = np.concatenate([-np.sin(alpha), -np.cos(alpha)], axis=1) / math.sqrt(FS)
    beta = unit_angles(spread, subgrids * MC, FS).reshape(spread, subgrids, 1, MC)
    beta = np.broadcast_to(beta, (spread, subgrids, 2, MC)).reshape(spread, subgrids * 2 * MC)
    tile = lambda t: np.tile(t, (1, subgrids)).astype(np.float32)
    return (
        tile(p),
        tile(q),
        np.cos(beta).astype(np.float32),
        np.sin(beta).astype(np.float32),
    )


def fetch_lookups(block_ref, links_ref, gain_ref, window, channel_gain, window_sem, gain_sem):
    blocks, _, span = window.shape
    copies = []
    for b in range(blocks):
        first = jnp.minimum(block_ref[1, b] // 128 * 128, links_ref.shape[1] - span)
        first = pl.multiple_of(first, 128)
        copies.append(
            pltpu.make_async_copy(
                links_ref.at[:, pl.ds(first, span)], window.at[b], window_sem.at[b]
            )
        )
        copies.append(
            pltpu.make_async_copy(
                gain_ref.at[block_ref[0, b]], channel_gain.at[b], gain_sem.at[b]
            )
        )
    return copies


def use_lookups(block_ref, links_ref, window, channel_gain, gains_ref, idents_ref):
    blocks, _, span = window.shape
    slots = idents_ref.shape[1]
    lane = lax.broadcasted_iota(jnp.int32, (1, slots), 1)
    place = lax.broadcasted_iota(jnp.int32, (span, slots), 0)
    lane_tall = lax.broadcasted_iota(jnp.int32, (span, slots), 1)
    begin = jnp.int32(0)
    member, picks = [], []
    channel = jnp.zeros((1, slots), jnp.float32)
    alive = jnp.zeros((1, slots), jnp.float32)
    for b in range(blocks):
        offset, amount = block_ref[1, b], block_ref[2, b]
        first = jnp.minimum(offset // 128 * 128, links_ref.shape[1] - span)
        inside = jnp.where((lane >= begin) & (lane < begin + amount), 1.0, 0.0)
        member.append(inside)
        alive += inside
        channel += inside * block_ref[0, b].astype(jnp.float32)
        hit = place == lane_tall + (offset - first - begin)
        picks.append((jnp.where(hit, 1.0, 0.0) * inside).astype(jnp.bfloat16))
        begin = begin + amount
    links = jnp.concatenate([window[b] for b in range(blocks)], axis=1)
    upper = links // 16
    lower = links - 16 * upper
    pieces = jnp.concatenate([upper, lower], axis=0).astype(jnp.float32).astype(jnp.bfloat16)
    found = jnp.dot(
        pieces, jnp.concatenate(picks, axis=0), preferred_element_type=jnp.float32
    )
    stations = 16.0 * found[0:2] + found[2:4]
    table = channel_gain[...].reshape(blocks * 4, channel_gain.shape[2])
    high = table.astype(jnp.bfloat16)
    rest = table - high.astype(jnp.float32)
    middle = rest.astype(jnp.bfloat16)
    low = (rest - middle.astype(jnp.float32)).astype(jnp.bfloat16)
    names = lax.broadcasted_iota(jnp.int32, (table.shape[1], 1), 0).astype(jnp.float32)
    for side in range(2):
        pick = jnp.where(names == stations[side : side + 1], 1.0, 0.0).astype(jnp.bfloat16)
        rows = (
            jnp.dot(high, pick, preferred_element_type=jnp.float32)
            + jnp.dot(middle, pick, preferred_element_type=jnp.float32)
            + jnp.dot(low, pick, preferred_element_type=jnp.float32)
        )
        chosen = member[0] * rows[0:4]
        for b in range(1, blocks):
            chosen = chosen + member[b] * rows[4 * b : 4 * b + 4]
        gains_ref[4 * side : 4 * side + 4, :] = chosen
    idents_ref[0:2, :] = stations
    idents_ref[2:3, :] = channel
    idents_ref[3:4, :] = alive
    idents_ref[4:8, :] = jnp.zeros((4, slots), jnp.float32)


def fourier_kernel(
    block_ref,
    links_ref,
    gain_ref,
    p_ref,
    q_ref,
    c_ref,
    s_ref,
    x_ref,
    o_ref,
    gains_ref,
    idents_ref,
    table,
    total,
    window,
    channel_gain,
    window_sem,
    gain_sem,
):
    step = pl.program_id(0)
    copies = fetch_lookups(
        block_ref, links_ref, gain_ref, window, channel_gain, window_sem, gain_sem
    )

    @pl.when(step == 0)
    def _():
        for copy in copies:
            copy.start()

    @pl.when(step == pl.num_programs(0) - 1)
    def _():
        for copy in copies:
            copy.wait()
        use_lookups(block_ref, links_ref, window, channel_gain, gains_ref, idents_ref)

    facets, _, rows, chunk = x_ref.shape
    subgrids = o_ref.shape[0]
    spread = c_ref.shape[0]
    cosine, sine = c_ref[...], s_ref[...]
    for part in range(chunk // spread):
        lead = p_ref[part : part + 1, :]
        other = q_ref[part : part + 1, :]
        table[part * spread : (part + 1) * spread, :] = (lead * cosine + other * sine).astype(
            jnp.bfloat16
        )
    x = x_ref[...].reshape(facets * 2 * rows, chunk)
    product = jnp.dot(x, table[...], preferred_element_type=jnp.float32)

    @pl.when(step == 0)
    def _():
        total[...] = product

    @pl.when(step > 0)
    def _():
        total[...] += product

    @pl.when(step == pl.num_programs(0) - 1)
    def _():
        lane = lax.broadcasted_iota(jnp.int32, (rows, 2 * MC), 1)
        sign = jnp.where(lane < MC, -1.0, 1.0)
        packed = o_ref.shape[3] // (2 * MC)
        for f in range(facets):
            for s in range(subgrids):
                cut = slice(s * 2 * MC, (s + 1) * 2 * MC)
                first = total[2 * f * rows : (2 * f + 1) * rows, cut]
                second = total[(2 * f + 1) * rows : (2 * f + 2) * rows, cut]
                value = first + sign * pltpu.roll(second, MC, 1)
                j = f % packed
                o_ref[s, f // packed, :, j * 2 * MC : (j + 1) * 2 * MC] = value.astype(jnp.bfloat16)


def fourier(x, subgrids, slots, block_table, links, station_gains):
    facets, _, rows, length = x.shape
    width = subgrids * 2 * MC
    spread = FS // MC
    packed = FGRID if facets % FGRID == 0 else 1
    per_step = CHUNK // spread
    blocks = block_table.shape[1]
    span = slots + 128
    in_place = lambda array: pltpu.with_memory_space_constraint(array, pltpu.HBM)
    factors = [in_place(jnp.asarray(t)) for t in fourier_factors(subgrids)]
    out = (subgrids, facets // packed, rows, packed * 2 * MC)
    return pl.pallas_call(
        fourier_kernel,
        out_shape=(
            jax.ShapeDtypeStruct(out, jnp.bfloat16),
            jax.ShapeDtypeStruct((8, slots), jnp.float32),
            jax.ShapeDtypeStruct((8, slots), jnp.float32),
        ),
        grid=(length // CHUNK,),
        in_specs=[
            pl.BlockSpec(memory_space=pltpu.SMEM),
            pl.BlockSpec(memory_space=pltpu.HBM),
            pl.BlockSpec(memory_space=pltpu.HBM),
            pl.BlockSpec((per_step, width), lambda g: (g, 0)),
            pl.BlockSpec((per_step, width), lambda g: (g, 0)),
            pl.BlockSpec((spread, width), lambda g: (0, 0)),
            pl.BlockSpec((spread, width), lambda g: (0, 0)),
            pl.BlockSpec((facets, 2, rows, CHUNK), lambda g: (0, 0, 0, g)),
        ],
        out_specs=(
            pl.BlockSpec(out, lambda g: (0, 0, 0, 0)),
            pl.BlockSpec((8, slots), lambda g: (0, 0)),
            pl.BlockSpec((8, slots), lambda g: (0, 0)),
        ),
        scratch_shapes=[
            pltpu.VMEM((CHUNK, width), jnp.bfloat16),
            pltpu.VMEM((facets * 2 * rows, width), jnp.float32),
            pltpu.VMEM((blocks, 2, span), jnp.int32),
            pltpu.VMEM((blocks, 4, NST), jnp.float32),
            pltpu.SemaphoreType.DMA((blocks,)),
            pltpu.SemaphoreType.DMA((blocks,)),
        ],
        compiler_params=pltpu.CompilerParams(
            dimension_semantics=("arbitrary",), vmem_limit_bytes=48 << 20
        ),
    )(
        block_table,
        in_place(links),
        in_place(station_gains),
        *factors,
        x,
    )


def subgrid_tables():
    angle = unit_angles(SG, SG, SG)
    re = np.cos(angle) / math.sqrt(SG)
    im = np.sin(angle) / math.sqrt(SG)
    blocks = lambda t: t.reshape(SG, FGRID, MC)
    second = np.stack([blocks(re), -blocks(im)], axis=2).reshape(SG, 2 * SG)
    return [t.astype(jnp.bfloat16) for t in (re, im, second)]


def chirp_line():
    offset = np.arange(SG) - SG // 2
    angle = 2.0 * math.pi * w_chirp * (offset * offset) / float(SG * SG)
    return np.cos(angle).astype(np.float32), np.sin(angle).astype(np.float32)


def model_terms(pred, observed, first, second, alive):
    residual, lead, trail = [], [], []
    for p in range(NPOL):
        f1, f2 = p // 2, p % 2
        pred_re, pred_im = pred[p]
        first_re, first_im = first[2 * f1], first[2 * f1 + 1]
        second_re, second_im = second[2 * f2], second[2 * f2 + 1]
        both_re = first_re * second_re + first_im * second_im
        both_im = first_im * second_re - first_re * second_im
        resid_re = alive * (observed[2 * p] - (both_re * pred_re - both_im * pred_im))
        resid_im = alive * (observed[2 * p + 1] - (both_re * pred_im + both_im * pred_re))
        cross_re = second_re * pred_re + second_im * pred_im
        cross_im = second_im * pred_re - second_re * pred_im
        along_re = first_re * pred_re - first_im * pred_im
        along_im = first_re * pred_im + first_im * pred_re
        residual += [resid_re, resid_im]
        lead.append(
            (-(resid_re * cross_re - resid_im * cross_im), -(resid_re * cross_im + resid_im * cross_re))
        )
        trail.append(
            (-(resid_re * along_re + resid_im * along_im), -(resid_re * along_im - resid_im * along_re))
        )
    leading = [lead[2 * f][r] + lead[2 * f + 1][r] for f in range(2) for r in range(2)]
    trailing = [trail[f][r] + trail[f + 2][r] for f in range(2) for r in range(2)]
    return residual, leading, trailing


def nt_dot(left, right, **kw):
    return lax.dot_general(
        left, right, (((1,), (1,)), ((), ())), preferred_element_type=jnp.float32, **kw
    )


def chirped_rows(taper, chirp_ref):
    wide = taper.astype(jnp.float32)
    return jnp.concatenate(
        [
            taper,
            (wide * chirp_ref[0:1, :]).astype(jnp.bfloat16),
            (wide * chirp_ref[1:2, :]).astype(jnp.bfloat16),
        ],
        axis=0,
    )


def predict_kernel(
    sizes,
    contrib_ref,
    lead_ref,
    trail_ref,
    depth_ref,
    observed_ref,
    gains_ref,
    idents_ref,
    table_re_ref,
    table_im_ref,
    second_ref,
    chirp_ref,
    residual_ref,
    grad_ref,
    got,
    lines,
    tapers,
    right,
    left,
    part_out,
    part_in,
    observed_out,
    observed_in,
    record_out,
    record_in,
    got_send,
    got_recv,
    taper_send,
    taper_recv,
    observed_send,
    observed_recv,
    part_send,
    part_recv,
    record_send,
    record_recv,
):
    subgrids, pols, owners = sizes
    z, p, t = lax.axis_index("facet"), lax.axis_index("pol"), lax.axis_index("tm")
    slots = lead_ref.shape[0]
    _, groups, rows, width = contrib_ref.shape
    mesh_id = pl.DeviceIdType.MESH

    def remote(src, dst, send, recv, peer):
        return pltpu.make_async_remote_copy(
            src_ref=src,
            dst_ref=dst,
            send_sem=send,
            recv_sem=recv,
            device_id=peer,
            device_id_type=mesh_id,
        )

    across_total = subgrids * owners
    plane_total = pols * owners
    across = z * owners + t
    plane = p * owners + t

    def across_peer(d):
        other = lax.rem(across + d, across_total)
        return other, (other // owners, p, lax.rem(other, owners))

    def plane_peer(d):
        other = lax.rem(plane + d, plane_total)
        return other, (z, other // owners, lax.rem(other, owners))

    barrier = pltpu.get_barrier_semaphore()
    for d in range(1, across_total):
        pl.semaphore_signal(barrier, inc=1, device_id=across_peer(d)[1], device_id_type=mesh_id)
    for d in range(1, pols):
        q = lax.rem(p + d, pols)
        for o in range(owners):
            pl.semaphore_signal(barrier, inc=1, device_id=(z, q, o), device_id_type=mesh_id)
    pl.semaphore_wait(barrier, across_total - 1 + (pols - 1) * owners)

    quarter = observed_ref.shape[1]
    place = lax.broadcasted_iota(jnp.int32, (2 * NPOL, slots), 1)
    observed_out[...] = jnp.where(
        (place >= p * quarter) & (place < (p + 1) * quarter),
        jnp.concatenate([observed_ref[...]] * pols, axis=1),
        0.0,
    )
    copies = []
    for d in sorted(range(1, subgrids), key=lambda d: -min(d, subgrids - d)):
        other = lax.rem(z + d, subgrids)
        copies.append(
            remote(contrib_ref.at[other], got.at[z], got_send.at[d], got_recv.at[d], (other, p, t))
        )
    partner = lax.rem(t + 1, owners)
    taper_copies = [
        remote(ref, tapers.at[t, k], taper_send.at[k], taper_recv.at[k], (z, p, partner))
        for k, ref in enumerate((trail_ref, lead_ref))
    ]
    observed_copies = []
    for d in range(1, pols):
        q = lax.rem(p + d, pols)
        observed_copies.append(
            remote(
                observed_out, observed_in.at[p], observed_send.at[d], observed_recv.at[d], (z, q, t)
            )
        )
    for copy in copies + taper_copies + observed_copies:
        copy.start()

    table_re = jnp.concatenate([table_re_ref[i, t] for i in range(FGRID)], axis=0)
    table_im = jnp.concatenate([table_im_ref[i, t] for i in range(FGRID)], axis=0)

    turn = jnp.where(
        lax.broadcasted_iota(jnp.int32, (3 * slots, 2 * MC), 1) < MC, -1.0, 1.0
    )

    def prepare(owner, trail, lead):
        trail3 = chirped_rows(trail, chirp_ref)
        a = jnp.dot(trail3, second_ref[...], preferred_element_type=jnp.float32)
        b = jnp.concatenate(
            [
                turn * pltpu.roll(a[:, j * 2 * MC : (j + 1) * 2 * MC], MC, 1)
                for j in range(a.shape[1] // (2 * MC))
            ],
            axis=1,
        )
        n0, n1, n2 = slice(0, slots), slice(slots, 2 * slots), slice(2 * slots, 3 * slots)
        right[owner, 0:slots, :] = a[n0].astype(jnp.bfloat16)
        right[owner, slots : 2 * slots, :] = (a[n1] - b[n2]).astype(jnp.bfloat16)
        right[owner, 2 * slots : 3 * slots, :] = b[n0].astype(jnp.bfloat16)
        right[owner, 3 * slots : 4 * slots, :] = (b[n1] + a[n2]).astype(jnp.bfloat16)
        lead3 = chirped_rows(lead, chirp_ref)
        u = nt_dot(table_re, lead3)
        v = nt_dot(table_im, lead3)
        left[owner, 0] = u[:, n0]
        left[owner, 1] = v[:, n0]
        left[owner, 2] = u[:, n1] - v[:, n2]
        left[owner, 3] = u[:, n2] + v[:, n1]

    prepare(t, trail_ref[...], lead_ref[...])
    got[z] = contrib_ref[z]
    for copy in taper_copies:
        copy.wait()
    prepare(partner, tapers[partner, 0], tapers[partner, 1])
    for copy in copies:
        copy.wait()
    if width == 2 * SG:
        whole = got[...].reshape(subgrids * groups * rows, width)
    else:
        for f in range(subgrids * groups):
            i, j = f // FGRID, f % FGRID
            lines[i * rows : (i + 1) * rows, j * 2 * MC : (j + 1) * 2 * MC] = got[
                f // groups, f % groups
            ]
        whole = lines[...]
    for o in range(owners):
        spread = nt_dot(whole, right[o])
        for w in range(NW):
            g_re = spread[:, w * slots : (w + 1) * slots]
            g_im = spread[:, (NW + w) * slots : (NW + w + 1) * slots]
            l_re, l_im = left[o, 2 * w], left[o, 2 * w + 1]
            part_out[o, 2 * w : 2 * w + 1, :] = jnp.sum(l_re * g_re - l_im * g_im, axis=0, keepdims=True)
            part_out[o, 2 * w + 1 : 2 * w + 2, :] = jnp.sum(
                l_re * g_im + l_im * g_re, axis=0, keepdims=True
            )
        part_out[o, 2 * NW :, :] = jnp.zeros((8 - 2 * NW, slots), jnp.float32)

    part_copies = []
    for d in range(1, plane_total):
        other, peer = plane_peer(d)
        part_copies.append(
            remote(
                part_out.at[lax.rem(other, owners)],
                part_in.at[plane],
                part_send.at[d],
                part_recv.at[d],
                peer,
            )
        )
    for copy in part_copies:
        copy.start()
    part_in[plane] = part_out[t]
    observed_in[p] = observed_out[...]
    for copy in observed_copies:
        copy.wait()
    observed = observed_in[0]
    for q in range(1, pols):
        observed = observed + observed_in[q]
    depth = depth_ref[...].astype(jnp.float32)
    for copy in part_copies:
        copy.wait()

    pred = []
    per_pol = part_in.shape[0] // NPOL
    for q in range(NPOL):
        block = part_in[q * per_pol]
        for o in range(1, per_pol):
            block = block + part_in[q * per_pol + o]
        pred.append(
            tuple(
                sum(depth[w : w + 1] * block[2 * w + c : 2 * w + c + 1] for w in range(NW))
                for c in range(2)
            )
        )
    gains = gains_ref[...]
    idents = idents_ref[...]
    residual, leading, trailing = model_terms(
        pred,
        [observed[k : k + 1] for k in range(2 * NPOL)],
        [gains[k : k + 1] for k in range(4)],
        [gains[4 + k : 5 + k] for k in range(4)],
        idents[3:4],
    )
    for k in range(3):
        record_out[k : k + 1, :] = idents[k : k + 1]
    for k in range(4):
        record_out[3 + k : 4 + k, :] = leading[k]
        record_out[7 + k : 8 + k, :] = trailing[k]
    record_out[11:, :] = jnp.zeros((5, slots), jnp.float32)
    record_copies = []
    for d in range(1, across_total):
        other, peer = across_peer(d)
        record_copies.append(
            remote(record_out, record_in.at[across], record_send.at[d], record_recv.at[d], peer)
        )
    for copy in record_copies:
        copy.start()
    record_in[across] = record_out[...]
    rest = jnp.concatenate(residual, axis=0)
    own_rest = jnp.zeros((2 * NPOL, quarter), jnp.float32)
    for q in range(pols):
        own_rest = jnp.where(p == q, rest[:, q * quarter : (q + 1) * quarter], own_rest)
    residual_ref[...] = own_rest
    for copy in record_copies:
        copy.wait()

    piece = jnp.concatenate([record_in[d] for d in range(across_total)], axis=1)
    own_count = grad_ref.shape[1]
    index = (z * pols + p) * owners + t
    mine = (index * own_count + lax.broadcasted_iota(jnp.int32, (own_count, 1), 0)).astype(
        jnp.float32
    )
    match_first = mine == piece[0:1]
    match_second = mine == piece[1:2]
    weighted = jnp.concatenate(
        [
            jnp.where(match_first, piece[3 + k : 4 + k], 0.0)
            + jnp.where(match_second, piece[7 + k : 8 + k], 0.0)
            for k in range(4)
        ],
        axis=0,
    )
    high = weighted.astype(jnp.bfloat16)
    low = (weighted - high.astype(jnp.float32)).astype(jnp.bfloat16)
    channel_ids = lax.broadcasted_iota(jnp.int32, (NCH, 1), 0).astype(jnp.float32)
    onehot = jnp.where(channel_ids == piece[2:3], 1.0, 0.0).astype(jnp.bfloat16)
    summed = nt_dot(high, onehot) + nt_dot(low, onehot)
    for k in range(4):
        grad_ref[k] = grad_scale * summed[k * own_count : (k + 1) * own_count]


def predict(sizes, own_count, *operands):
    subgrids, pols, owners = sizes
    contrib, lead = operands[0], operands[1]
    _, groups, rows, width = contrib.shape
    slots = lead.shape[0]
    vmem = pl.BlockSpec(memory_space=pltpu.VMEM)
    dma = lambda n: pltpu.SemaphoreType.DMA((n,))
    across_total, plane_total = subgrids * owners, pols * owners
    return pl.pallas_call(
        functools.partial(predict_kernel, sizes),
        out_shape=(
            jax.ShapeDtypeStruct((2 * NPOL, slots // pols), jnp.float32),
            jax.ShapeDtypeStruct((4, own_count, NCH), jnp.float32),
        ),
        in_specs=[vmem] * len(operands),
        out_specs=(vmem, vmem),
        scratch_shapes=[
            pltpu.VMEM(contrib.shape, jnp.bfloat16),
            pltpu.VMEM((FGRID * rows, 2 * SG), jnp.bfloat16),
            pltpu.VMEM((owners, 2, slots, SG), jnp.bfloat16),
            pltpu.VMEM((owners, 2 * NW * slots, 2 * SG), jnp.bfloat16),
            pltpu.VMEM((owners, 4, FGRID * rows, slots), jnp.float32),
            pltpu.VMEM((owners, 8, slots), jnp.float32),
            pltpu.VMEM((plane_total, 8, slots), jnp.float32),
            pltpu.VMEM((8, slots), jnp.float32),
            pltpu.VMEM((pols, 8, slots), jnp.float32),
            pltpu.VMEM((16, slots), jnp.float32),
            pltpu.VMEM((across_total, 16, slots), jnp.float32),
            dma(subgrids),
            dma(subgrids),
            dma(2),
            dma(2),
            dma(pols),
            dma(pols),
            dma(plane_total),
            dma(plane_total),
            dma(across_total),
            dma(across_total),
        ],
        compiler_params=pltpu.CompilerParams(
            collective_id=0, has_side_effects=True, vmem_limit_bytes=48 << 20
        ),
    )(*operands)


def gather_lookups(block_ref, links_ref, gain_ref, gains_ref, idents_ref):
    blocks = block_ref.shape[2]
    slots = idents_ref.shape[1]
    span = slots + 128
    lane = lax.broadcasted_iota(jnp.int32, (1, slots), 1)
    place = lax.broadcasted_iota(jnp.int32, (span, slots), 0)
    lane_tall = lax.broadcasted_iota(jnp.int32, (span, slots), 1)
    begin = jnp.int32(0)
    member, picks, windows, tables = [], [], [], []
    channel = jnp.zeros((1, slots), jnp.float32)
    alive = jnp.zeros((1, slots), jnp.float32)
    for b in range(blocks):
        chosen, offset, amount = [block_ref[k, 0, b] for k in range(3)]
        row = jnp.minimum(lax.div(offset, 128), links_ref.shape[0] - span // 128)
        first = row * 128
        windows += [links_ref[row + k] for k in range(span // 128)]
        tables.append(gain_ref[chosen])
        inside = jnp.where((lane >= begin) & (lane < begin + amount), 1.0, 0.0)
        member.append(inside)
        alive += inside
        channel += inside * chosen.astype(jnp.float32)
        hit = place == lane_tall + (offset - first - begin)
        picks.append((jnp.where(hit, 1.0, 0.0) * inside).astype(jnp.bfloat16))
        begin = begin + amount
    links = jnp.concatenate(windows, axis=1)
    upper = links // 16
    lower = links - 16 * upper
    pieces = jnp.concatenate([upper, lower], axis=0).astype(jnp.float32).astype(jnp.bfloat16)
    found = jnp.dot(
        pieces, jnp.concatenate(picks, axis=0), preferred_element_type=jnp.float32
    )
    stations = 16.0 * found[0:2] + found[2:4]
    table = jnp.concatenate(tables, axis=0)
    high = table.astype(jnp.bfloat16)
    rest = table - high.astype(jnp.float32)
    middle = rest.astype(jnp.bfloat16)
    low = (rest - middle.astype(jnp.float32)).astype(jnp.bfloat16)
    split = jnp.concatenate([high, middle, low], axis=0)
    size = table.shape[0]
    names = lax.broadcasted_iota(jnp.int32, (table.shape[1], 1), 0).astype(jnp.float32)
    for side in range(2):
        pick = jnp.where(names == stations[side : side + 1], 1.0, 0.0).astype(jnp.bfloat16)
        three = jnp.dot(split, pick, preferred_element_type=jnp.float32)
        rows = three[:size] + three[size : 2 * size] + three[2 * size :]
        chosen = member[0] * rows[0:4]
        for b in range(1, blocks):
            chosen = chosen + member[b] * rows[4 * b : 4 * b + 4]
        gains_ref[4 * side : 4 * side + 4, :] = chosen
    idents_ref[0:2, :] = stations
    idents_ref[2:3, :] = channel
    idents_ref[3:4, :] = alive
    idents_ref[4:8, :] = jnp.zeros((4, slots), jnp.float32)


def fused_kernel(
    sizes,
    block_hbm,
    links_hbm,
    gain_hbm,
    p_hbm,
    q_hbm,
    c_hbm,
    s_hbm,
    x_hbm,
    lead_hbm,
    trail_hbm,
    depth_hbm,
    observed_hbm,
    table_re_hbm,
    table_im_hbm,
    second_hbm,
    chirp_hbm,
    residual_ref,
    grad_ref,
    block_ref,
    links_ref,
    gain_ref,
    p_ref,
    q_ref,
    c_ref,
    s_ref,
    x_ref,
    tapers,
    depths,
    observed_ref,
    table_ref,
    second_ref,
    chirp_ref,
    factors,
    contrib,
    got,
    right,
    left,
    gains_ref,
    idents_ref,
    side,
    part_out,
    part_in,
    observed_out,
    observed_in,
    rests,
    load_sem,
    chunk_sem,
    pair_send,
    pair_recv,
    chip_send,
    chip_recv,
    relay_send,
    relay_recv,
    far_send,
    far_recv,
    near_send,
    near_recv,
    observed_send,
    observed_recv,
    side_send,
    side_recv,
    part_send,
    part_recv,
):
    subgrids, pols, owners = sizes
    z, p, t = lax.axis_index("facet"), lax.axis_index("pol"), lax.axis_index("tm")
    _, _, slots, _ = tapers.shape
    facets, _, rows, length = x_ref.shape
    _, _, groups, _, width = contrib.shape
    side_z, own = lax.rem(z, 2), z // 2
    far = 1 - own
    pair_z = z + 1 - 2 * side_z
    far_z = z + 2 - 4 * own
    partner = lax.rem(t + 1, owners)
    mesh_id = pl.DeviceIdType.MESH

    def remote(src, dst, send, recv, peer):
        return pltpu.make_async_remote_copy(
            src_ref=src,
            dst_ref=dst,
            send_sem=send,
            recv_sem=recv,
            device_id=peer,
            device_id_type=mesh_id,
        )

    across_total = subgrids * owners
    across = z * owners + t

    def across_peer(d):
        other = lax.rem(across + d, across_total)
        return other, (other // owners, p, lax.rem(other, owners))

    barrier = pltpu.get_barrier_semaphore()
    for d in range(1, across_total):
        pl.semaphore_signal(barrier, inc=1, device_id=across_peer(d)[1], device_id_type=mesh_id)
    for d in range(1, pols):
        q = lax.rem(p + d, pols)
        for o in range(owners):
            pl.semaphore_signal(barrier, inc=1, device_id=(z, q, o), device_id_type=mesh_id)

    offsets = [
        (dz, dp, dt)
        for dz in sorted(range(subgrids), key=lambda d: -min(d, subgrids - d))
        for dp in reversed(range(pols))
        for dt in range(owners)
    ]
    offsets.remove((0, 0, 0))
    per_chunk = FGRID // PIECES
    chunks = facets // per_chunk
    x_loads = [
        pltpu.make_async_copy(
            x_hbm.at[pl.ds(c * per_chunk, per_chunk)],
            x_ref.at[pl.ds(c * per_chunk, per_chunk)],
            chunk_sem.at[c],
        )
        for c in range(chunks)
    ]
    pairs = [
        (c_hbm, c_ref),
        (s_hbm, s_ref),
        (p_hbm, p_ref),
        (q_hbm, q_ref),
        (trail_hbm, tapers.at[own, 0]),
        (lead_hbm, tapers.at[own, 1]),
        (depth_hbm, depths.at[own]),
        (observed_hbm, observed_ref),
        (chirp_hbm, chirp_ref),
        (second_hbm, second_ref),
        (table_re_hbm.at[pl.ds(own * 2 * groups, 2 * groups)], table_ref.at[0]),
        (table_im_hbm.at[pl.ds(own * 2 * groups, 2 * groups)], table_ref.at[1]),
        (block_hbm, block_ref),
        (links_hbm, links_ref),
        (gain_hbm, gain_ref),
    ]
    loads = [
        pltpu.make_async_copy(src, dst, load_sem.at[k]) for k, (src, dst) in enumerate(pairs)
    ]
    for copy in loads[:4]:
        copy.start()
    x_loads[0].start()
    for copy in loads[4:9]:
        copy.start()
    for copy in x_loads[1:]:
        copy.start()
    for copy in loads[9:]:
        copy.start()

    for copy in loads[:4]:
        copy.wait()
    spread = c_ref.shape[0]
    cosine, sine = c_ref[...], s_ref[...]
    for part in range(length // spread):
        factors[part * spread : (part + 1) * spread, :] = (
            p_ref[part : part + 1, :] * cosine + q_ref[part : part + 1, :] * sine
        ).astype(jnp.bfloat16)

    for copy in loads[4:9]:
        copy.wait()
    quarter = observed_ref.shape[1]
    place = lax.broadcasted_iota(jnp.int32, (2 * NPOL, slots), 1)
    observed_out[...] = jnp.where(
        (place >= p * quarter) & (place < (p + 1) * quarter),
        jnp.concatenate([observed_ref[...]] * pols, axis=1),
        0.0,
    )
    pl.semaphore_wait(barrier, across_total - 1 + (pols - 1) * owners)
    share = lambda q: pl.ds(pl.multiple_of(q * quarter, quarter), quarter)
    far_copies = [
        remote(
            tapers.at[own, :, share(q)],
            tapers.at[own, :, share(q)],
            far_send.at[k],
            far_recv.at[k],
            (far_z, p, t),
        )
        for k, q in enumerate((p, pols - 1 - p))
    ]
    far_copies.append(
        remote(depths.at[own], depths.at[own], far_send.at[2], far_recv.at[2], (far_z, p, t))
    )
    observed_copies = []
    for d in range(1, pols):
        q = lax.rem(p + d, pols)
        observed_copies.append(
            remote(
                observed_out, observed_in.at[p], observed_send.at[d], observed_recv.at[d], (z, q, t)
            )
        )
    for copy in far_copies + observed_copies:
        copy.start()
    across_x = p + 1 - 2 * lax.rem(p, 2)
    near_copies = [
        remote(
            tapers.at[far, :, share(p)],
            tapers.at[far, :, share(p)],
            near_send.at[k],
            near_recv.at[k],
            (z, q, t),
        )
        for k, q in enumerate((across_x, pols - 1 - across_x))
    ]

    lane = lax.broadcasted_iota(jnp.int32, (rows, 2 * MC), 1)
    sign = jnp.where(lane < MC, -1.0, 1.0)
    part_width = width // PIECES
    pair_copies, chip_copies, relay_copies = [], [], []
    for c in range(chunks):
        x_loads[c].wait()
        x = x_ref[c * per_chunk : (c + 1) * per_chunk].reshape(per_chunk * 2 * rows, length)
        total = jnp.dot(x, factors[...], preferred_element_type=jnp.float32)
        group, piece = c // PIECES, c % PIECES
        for s in range(subgrids):
            cut = slice(s * 2 * MC, (s + 1) * 2 * MC)
            for f in range(per_chunk):
                first = total[2 * f * rows : (2 * f + 1) * rows, cut]
                second = total[(2 * f + 1) * rows : (2 * f + 2) * rows, cut]
                j = piece * per_chunk + f
                contrib[s % 2, s // 2, group, :, j * 2 * MC : (j + 1) * 2 * MC] = (
                    first + sign * pltpu.roll(second, MC, 1)
                ).astype(jnp.bfloat16)
        lanes = pl.ds(piece * part_width, part_width)
        pair_copies.append(
            remote(
                contrib.at[1 - side_z, :, group, :, lanes],
                got.at[:, side_z, group, t, :, lanes],
                pair_send.at[c],
                pair_recv.at[c],
                (pair_z, p, t),
            )
        )
        chip_copies.append(
            remote(
                contrib.at[side_z, :, group, :, lanes],
                got.at[:, side_z, group, t, :, lanes],
                chip_send.at[c],
                chip_recv.at[c],
                (z, p, partner),
            )
        )
        relay_copies.append(
            remote(
                got.at[:, 1 - side_z, group, t, :, lanes],
                got.at[:, 1 - side_z, group, t, :, lanes],
                relay_send.at[c],
                relay_recv.at[c],
                (z, p, partner),
            )
        )
        pair_copies[c].start()
        chip_copies[c].start()
        if c == chunks - FORWARD:
            far_copies[0].wait_recv()
            for copy in near_copies:
                copy.start()

    for k in range(2):
        for group in range(groups):
            got[k, side_z, group, t] = contrib[side_z, k, group]
    for copy in loads[9:]:
        copy.wait()
    gather_lookups(block_ref, links_ref, gain_ref, gains_ref, idents_ref)
    observed_in[p] = observed_out[...]
    for copy in observed_copies:
        copy.wait()
    observed = observed_in[0]
    for q in range(1, pols):
        observed = observed + observed_in[q]
    side[across, 0:8] = gains_ref[...]
    side[across, 8:16] = observed
    side[across, 16:20] = idents_ref[0:4]
    side_copies = []
    for d in range(1, across_total):
        other, peer = across_peer(d)
        side_copies.append(
            remote(side.at[across], side.at[across], side_send.at[d], side_recv.at[d], peer)
        )
    for copy in side_copies:
        copy.start()

    span = 2 * groups * owners * rows
    table_re = table_ref[0].reshape(span, SG)
    table_im = table_ref[1].reshape(span, SG)
    turn = jnp.where(
        lax.broadcasted_iota(jnp.int32, (3 * slots, 2 * MC), 1) < MC, -1.0, 1.0
    )

    def prepare(k):
        trail3 = chirped_rows(tapers[k, 0], chirp_ref)
        a = jnp.dot(trail3, second_ref[...], preferred_element_type=jnp.float32)
        b = jnp.concatenate(
            [
                turn * pltpu.roll(a[:, j * 2 * MC : (j + 1) * 2 * MC], MC, 1)
                for j in range(a.shape[1] // (2 * MC))
            ],
            axis=1,
        )
        n0, n1, n2 = slice(0, slots), slice(slots, 2 * slots), slice(2 * slots, 3 * slots)
        right[k, 0:slots, :] = a[n0].astype(jnp.bfloat16)
        right[k, slots : 2 * slots, :] = (a[n1] - b[n2]).astype(jnp.bfloat16)
        right[k, 2 * slots : 3 * slots, :] = b[n0].astype(jnp.bfloat16)
        right[k, 3 * slots : 4 * slots, :] = (b[n1] + a[n2]).astype(jnp.bfloat16)
        lead3 = chirped_rows(tapers[k, 1], chirp_ref)
        u = nt_dot(table_re, lead3)
        v = nt_dot(table_im, lead3)
        left[k, 0] = u[:, n0]
        left[k, 1] = v[:, n0]
        left[k, 2] = u[:, n1] - v[:, n2]
        left[k, 3] = u[:, n2] + v[:, n1]

    prepare(own)
    for pair, relay in zip(pair_copies, relay_copies):
        pair.wait_recv()
        relay.start()
    for copy in far_copies[1:] + near_copies:
        copy.wait_recv()
    prepare(far)
    for copy in side_copies + chip_copies + relay_copies:
        copy.wait()
    for copy in pair_copies + far_copies + near_copies:
        copy.wait_send()
    for k in range(2):
        spread_v = nt_dot(got[k].reshape(span, width), right[k])
        weights = depths[k].astype(jnp.float32)
        sums = [0.0, 0.0]
        for w in range(NW):
            g_re = spread_v[:, w * slots : (w + 1) * slots]
            g_im = spread_v[:, (NW + w) * slots : (NW + w + 1) * slots]
            l_re, l_im = left[k, 2 * w], left[k, 2 * w + 1]
            weight = weights[w : w + 1]
            sums[0] += weight * jnp.sum(l_re * g_re - l_im * g_im, axis=0, keepdims=True)
            sums[1] += weight * jnp.sum(l_re * g_im + l_im * g_re, axis=0, keepdims=True)
        for c in range(2):
            part_out[2 * c + k : 2 * c + k + 1, :] = sums[c]

    part_copies = []
    for dz, dp, dt in offsets:
        peer = (lax.rem(z + dz, subgrids), lax.rem(p + dp, pols), lax.rem(t + dt, owners))
        k = (dz * pols + dp) * owners + dt
        part_copies.append(
            remote(part_out, part_in.at[z, p, t], part_send.at[k], part_recv.at[k], peer)
        )
    for copy in part_copies:
        copy.start()
    part_in[z, p, t] = part_out[...]

    own_count = grad_ref.shape[0]
    index = (z * pols + p) * owners + t
    mine = (index * own_count + lax.broadcasted_iota(jnp.int32, (own_count, 1), 0)).astype(
        jnp.float32
    )
    channel_ids = lax.broadcasted_iota(jnp.int32, (NCH, 1), 0).astype(jnp.float32)
    first_here = [jnp.where(mine == side[d, 16:17], 1.0, 0.0) for d in range(across_total)]
    second_here = [jnp.where(mine == side[d, 17:18], 1.0, 0.0) for d in range(across_total)]
    onehot = jnp.concatenate(
        [
            jnp.where(channel_ids == side[d, 18:19], 1.0, 0.0).astype(jnp.bfloat16)
            for d in range(across_total)
        ],
        axis=1,
    )
    column = lambda k: jnp.concatenate([side[d, k : k + 1] for d in range(across_total)], axis=0)
    gains = [column(k) for k in range(8)]
    observed = [column(8 + k) for k in range(8)]
    alive = column(19)
    for copy in part_copies:
        copy.wait()

    pred = []
    for q in range(NPOL):
        both = [[part_in[y, q, o] + part_in[y + 2, q, o] for o in range(owners)] for y in range(2)]
        pred.append(
            tuple(
                jnp.concatenate(
                    [
                        both[s % 2][o][2 * c + s // 2 : 2 * c + s // 2 + 1]
                        for s in range(subgrids)
                        for o in range(owners)
                    ],
                    axis=0,
                )
                for c in range(2)
            )
        )
    residual, leading, trailing = model_terms(pred, observed, gains[:4], gains[4:], alive)
    for k in range(2 * NPOL):
        rests[:, k : k + 1, :] = residual[k][:, None, :]
    rest = rests[across]
    own_rest = jnp.zeros((2 * NPOL, quarter), jnp.float32)
    for q in range(pols):
        own_rest = jnp.where(p == q, rest[:, q * quarter : (q + 1) * quarter], own_rest)
    residual_ref[...] = own_rest

    weighted = jnp.concatenate(
        [
            jnp.concatenate(
                [
                    first_here[d] * leading[k][d : d + 1]
                    + second_here[d] * trailing[k][d : d + 1]
                    for d in range(across_total)
                ],
                axis=1,
            )
            for k in range(4)
        ],
        axis=0,
    )
    high = weighted.astype(jnp.bfloat16)
    low = (weighted - high.astype(jnp.float32)).astype(jnp.bfloat16)
    summed = nt_dot(high, onehot) + nt_dot(low, onehot)
    lane_group = lax.broadcasted_iota(jnp.int32, (own_count, 128), 1) // 32
    mixed = []
    for g in range(NCH // 32):
        base = g // 4 * 128
        built = None
        for k in range(4):
            block = summed[k * own_count : (k + 1) * own_count, base : base + 128]
            shift = 32 * (k - g % 4) % 128
            block = pltpu.roll(block, shift, 1) if shift else block
            built = block if built is None else jnp.where(lane_group == k, block, built)
        mixed.append(grad_scale * built)
    mixed = jnp.concatenate(mixed, axis=0)
    high = mixed.astype(jnp.bfloat16)
    low = (mixed - high.astype(jnp.float32)).astype(jnp.bfloat16)
    came = lax.broadcasted_iota(jnp.int32, (128, 128), 0)
    goes = lax.broadcasted_iota(jnp.int32, (128, 128), 1)
    order = jnp.where(goes == came % 32 * 4 + came // 32, 1.0, 0.0).astype(jnp.bfloat16)
    placed = jnp.dot(
        jnp.concatenate([high, low], axis=0), order, preferred_element_type=jnp.float32
    )
    placed = placed[: mixed.shape[0]] + placed[mixed.shape[0] :]
    for g in range(NCH // 32):
        grad_ref[:, g * 128 : (g + 1) * 128] = placed[g * own_count : (g + 1) * own_count]


def emit_kernel(residual_ref, grad_ref, residual_out, grad_out, sems):
    copies = [
        pltpu.make_async_copy(residual_ref, residual_out, sems.at[0]),
        pltpu.make_async_copy(grad_ref, grad_out, sems.at[1]),
    ]
    for copy in copies:
        copy.start()
    for copy in copies:
        copy.wait()


def fused(sizes, own_count, *operands):
    subgrids, pols, owners = sizes
    block_table, links, gains = operands[0:3]
    x, lead, trail, depth, observed = operands[7:12]
    facets, _, rows, length = x.shape
    slots = lead.shape[0]
    width = subgrids * 2 * MC
    spread = FS // MC
    groups = facets // FGRID
    chunks = facets // (FGRID // PIECES)
    hbm = pl.BlockSpec(memory_space=pltpu.HBM)
    vmem = pl.BlockSpec(memory_space=pltpu.VMEM)
    dma = lambda n: pltpu.SemaphoreType.DMA((n,))
    held = lambda a: pltpu.VMEM(a.shape, a.dtype)
    across_total, all_total = subgrids * owners, subgrids * pols * owners
    f32, bf16 = jnp.float32, jnp.bfloat16
    residual, grad = pl.pallas_call(
        functools.partial(fused_kernel, sizes),
        out_shape=(
            jax.ShapeDtypeStruct(observed.shape, f32),
            jax.ShapeDtypeStruct((own_count, 4 * NCH), f32),
        ),
        in_specs=[hbm] * len(operands),
        out_specs=(vmem, vmem),
        scratch_shapes=[
            pltpu.SMEM(block_table.shape, jnp.int32),
            held(links),
            held(gains),
            pltpu.VMEM((length // spread, width), f32),
            pltpu.VMEM((length // spread, width), f32),
            pltpu.VMEM((spread, width), f32),
            pltpu.VMEM((spread, width), f32),
            held(x),
            pltpu.VMEM((2, 2, slots, SG), bf16),
            pltpu.VMEM((2,) + depth.shape, bf16),
            held(observed),
            pltpu.VMEM((2, 2 * groups, owners, rows, SG), bf16),
            pltpu.VMEM((SG, 2 * SG), bf16),
            pltpu.VMEM((2, SG), f32),
            pltpu.VMEM((length, width), bf16),
            pltpu.VMEM((2, 2, groups, rows, 2 * SG), bf16),
            pltpu.VMEM((2, 2, groups, owners, rows, 2 * SG), bf16),
            pltpu.VMEM((2, 2 * NW * slots, 2 * SG), bf16),
            pltpu.VMEM((2, 4, 2 * groups * owners * rows, slots), f32),
            pltpu.VMEM((8, slots), f32),
            pltpu.VMEM((8, slots), f32),
            pltpu.VMEM((across_total, 20, slots), f32),
            pltpu.VMEM((4, slots), f32),
            pltpu.VMEM((subgrids, pols, owners, 4, slots), f32),
            pltpu.VMEM((8, slots), f32),
            pltpu.VMEM((pols, 8, slots), f32),
            pltpu.VMEM((across_total, 8, slots), f32),
            dma(15),
            dma(chunks),
            dma(chunks),
            dma(chunks),
            dma(chunks),
            dma(chunks),
            dma(chunks),
            dma(chunks),
            dma(3),
            dma(3),
            dma(2),
            dma(2),
            dma(pols),
            dma(pols),
            dma(across_total),
            dma(across_total),
            dma(all_total),
            dma(all_total),
        ],
        compiler_params=pltpu.CompilerParams(
            collective_id=0, has_side_effects=True, vmem_limit_bytes=36 << 20
        ),
    )(*[pltpu.with_memory_space_constraint(a, pltpu.HBM) for a in operands])
    return pl.pallas_call(
        emit_kernel,
        out_shape=(
            jax.ShapeDtypeStruct(residual.shape, f32),
            jax.ShapeDtypeStruct(grad.shape, f32),
        ),
        in_specs=[vmem] * 2,
        out_specs=[hbm] * 2,
        scratch_shapes=[dma(2)],
        compiler_params=pltpu.CompilerParams(vmem_limit_bytes=1 << 20),
    )(residual, grad)


def on_device(
    tile_spectral_lines,
    taper_leading_axis,
    taper_trailing_axis,
    depth_layer_factors,
    measured_correlations,
    visibility_groups_table,
    antenna_links,
    complex_receiver_factors,
):
    sizes = tuple(lax.axis_size(name) for name in ("facet", "pol", "tm"))
    subgrids, pols, owners = sizes
    slots = taper_leading_axis.shape[2]
    quarter = measured_correlations.shape[3]
    rows = tile_spectral_lines.shape[3]

    block_table = visibility_groups_table.reshape(3, visibility_groups_table.shape[3])
    observed = measured_correlations.reshape(2 * NPOL, quarter)

    if tile_spectral_lines.shape[0] % FGRID == 0 and sizes == (4, NPOL, 2):
        table_re, table_im, second = [jnp.asarray(t) for t in subgrid_tables()]
        own_count = NST // (subgrids * pols * owners)
        residual, gain_grad = fused(
            sizes,
            own_count,
            visibility_groups_table.reshape(3, 1, visibility_groups_table.shape[3]),
            jnp.transpose(antenna_links.reshape(2, -1, 128), (1, 0, 2)),
            complex_receiver_factors,
            *[jnp.asarray(t) for t in fourier_factors(subgrids)],
            tile_spectral_lines[:, 0],
            taper_leading_axis.reshape(slots, SG),
            taper_trailing_axis.reshape(slots, SG),
            depth_layer_factors.reshape(NW, slots),
            observed,
            table_re.reshape(FGRID, owners, rows, SG),
            table_im.reshape(FGRID, owners, rows, SG),
            second,
            jnp.asarray(np.stack(chirp_line())),
        )
        return residual.reshape(1, 2 * NPOL, 1, quarter), gain_grad

    contrib, gains, idents = fourier(
        tile_spectral_lines[:, 0],
        subgrids,
        slots,
        block_table,
        antenna_links,
        complex_receiver_factors,
    )
    table_re, table_im, second = [jnp.asarray(t) for t in subgrid_tables()]
    cosine, sine = chirp_line()
    own_count = NST // (subgrids * pols * owners)
    residual, grad = predict(
        sizes,
        own_count,
        contrib,
        taper_leading_axis.reshape(slots, SG),
        taper_trailing_axis.reshape(slots, SG),
        depth_layer_factors.reshape(NW, slots),
        observed,
        gains,
        idents,
        table_re.reshape(FGRID, owners, rows, SG),
        table_im.reshape(FGRID, owners, rows, SG),
        second,
        jnp.asarray(np.stack([cosine, sine])),
    )
    gain_grad = jnp.transpose(grad, (1, 2, 0)).reshape(own_count, 4 * NCH)
    return residual.reshape(1, 2 * NPOL, 1, quarter), gain_grad


def solution(mesh):
    return jax.shard_map(
        on_device,
        mesh=mesh,
        in_specs=(
            P("facet", "pol", None, "tm", None),
            P("facet", "tm", None, None),
            P("facet", "tm", None, None),
            P("facet", "tm", None, None),
            P("facet", None, "tm", "pol"),
            P("facet", "tm", None, None),
            P(),
            P(),
        ),
        out_specs=(P("facet", None, "tm", "pol"), P(("facet", "pol", "tm"), None)),
        check_vma=False,
    )
```

```python
import functools
import math

import jax
import jax.numpy as jnp
import numpy as np
from jax import lax
from jax.experimental import pallas as pl
from jax.experimental.pallas import tpu as pltpu
from jax.sharding import PartitionSpec as P

FGRID = 8
FS = 4096
MC = 64
SG = 512
NPOL = 4
NW = 2
NCH = 256
NST = 512
CHUNK = 1024
PIECES = 2
FORWARD = 1

w_chirp = 0.37
grad_scale = 0.1


def unit_angles(left, right, length):
    product = np.outer(np.arange(left), np.arange(right)) % length
    return 2.0 * math.pi * product / length


def fourier_factors(subgrids):
    spread = FS // MC
    alpha = unit_angles(FS // spread, MC, MC)
    p = np.concatenate([np.cos(alpha), -np.sin(alpha)], axis=1) / math.sqrt(FS)
    q = np.concatenate([-np.sin(alpha), -np.cos(alpha)], axis=1) / math.sqrt(FS)
    beta = unit_angles(spread, subgrids * MC, FS).reshape(spread, subgrids, 1, MC)
    beta = np.broadcast_to(beta, (spread, subgrids, 2, MC)).reshape(spread, subgrids * 2 * MC)
    tile = lambda t: np.tile(t, (1, subgrids)).astype(np.float32)
    return (
        tile(p),
        tile(q),
        np.cos(beta).astype(np.float32),
        np.sin(beta).astype(np.float32),
    )


def fetch_lookups(block_ref, links_ref, gain_ref, window, channel_gain, window_sem, gain_sem):
    blocks, _, span = window.shape
    copies = []
    for b in range(blocks):
        first = jnp.minimum(block_ref[1, b] // 128 * 128, links_ref.shape[1] - span)
        first = pl.multiple_of(first, 128)
        copies.append(
            pltpu.make_async_copy(
                links_ref.at[:, pl.ds(first, span)], window.at[b], window_sem.at[b]
            )
        )
        copies.append(
            pltpu.make_async_copy(
                gain_ref.at[block_ref[0, b]], channel_gain.at[b], gain_sem.at[b]
            )
        )
    return copies


def use_lookups(block_ref, links_ref, window, channel_gain, gains_ref, idents_ref):
    blocks, _, span = window.shape
    slots = idents_ref.shape[1]
    lane = lax.broadcasted_iota(jnp.int32, (1, slots), 1)
    place = lax.broadcasted_iota(jnp.int32, (span, slots), 0)
    lane_tall = lax.broadcasted_iota(jnp.int32, (span, slots), 1)
    begin = jnp.int32(0)
    member, picks = [], []
    channel = jnp.zeros((1, slots), jnp.float32)
    alive = jnp.zeros((1, slots), jnp.float32)
    for b in range(blocks):
        offset, amount = block_ref[1, b], block_ref[2, b]
        first = jnp.minimum(offset // 128 * 128, links_ref.shape[1] - span)
        inside = jnp.where((lane >= begin) & (lane < begin + amount), 1.0, 0.0)
        member.append(inside)
        alive += inside
        channel += inside * block_ref[0, b].astype(jnp.float32)
        hit = place == lane_tall + (offset - first - begin)
        picks.append((jnp.where(hit, 1.0, 0.0) * inside).astype(jnp.bfloat16))
        begin = begin + amount
    links = jnp.concatenate([window[b] for b in range(blocks)], axis=1)
    upper = links // 16
    lower = links - 16 * upper
    pieces = jnp.concatenate([upper, lower], axis=0).astype(jnp.float32).astype(jnp.bfloat16)
    found = jnp.dot(
        pieces, jnp.concatenate(picks, axis=0), preferred_element_type=jnp.float32
    )
    stations = 16.0 * found[0:2] + found[2:4]
    table = channel_gain[...].reshape(blocks * 4, channel_gain.shape[2])
    high = table.astype(jnp.bfloat16)
    rest = table - high.astype(jnp.float32)
    middle = rest.astype(jnp.bfloat16)
    low = (rest - middle.astype(jnp.float32)).astype(jnp.bfloat16)
    names = lax.broadcasted_iota(jnp.int32, (table.shape[1], 1), 0).astype(jnp.float32)
    for side in range(2):
        pick = jnp.where(names == stations[side : side + 1], 1.0, 0.0).astype(jnp.bfloat16)
        rows = (
            jnp.dot(high, pick, preferred_element_type=jnp.float32)
            + jnp.dot(middle, pick, preferred_element_type=jnp.float32)
            + jnp.dot(low, pick, preferred_element_type=jnp.float32)
        )
        chosen = member[0] * rows[0:4]
        for b in range(1, blocks):
            chosen = chosen + member[b] * rows[4 * b : 4 * b + 4]
        gains_ref[4 * side : 4 * side + 4, :] = chosen
    idents_ref[0:2, :] = stations
    idents_ref[2:3, :] = channel
    idents_ref[3:4, :] = alive
    idents_ref[4:8, :] = jnp.zeros((4, slots), jnp.float32)


def fourier_kernel(
    block_ref,
    links_ref,
    gain_ref,
    p_ref,
    q_ref,
    c_ref,
    s_ref,
    x_ref,
    o_ref,
    gains_ref,
    idents_ref,
    table,
    total,
    window,
    channel_gain,
    window_sem,
    gain_sem,
):
    step = pl.program_id(0)
    copies = fetch_lookups(
        block_ref, links_ref, gain_ref, window, channel_gain, window_sem, gain_sem
    )

    @pl.when(step == 0)
    def _():
        for copy in copies:
            copy.start()

    @pl.when(step == pl.num_programs(0) - 1)
    def _():
        for copy in copies:
            copy.wait()
        use_lookups(block_ref, links_ref, window, channel_gain, gains_ref, idents_ref)

    facets, _, rows, chunk = x_ref.shape
    subgrids = o_ref.shape[0]
    spread = c_ref.shape[0]
    cosine, sine = c_ref[...], s_ref[...]
    for part in range(chunk // spread):
        lead = p_ref[part : part + 1, :]
        other = q_ref[part : part + 1, :]
        table[part * spread : (part + 1) * spread, :] = (lead * cosine + other * sine).astype(
            jnp.bfloat16
        )
    x = x_ref[...].reshape(facets * 2 * rows, chunk)
    product = jnp.dot(x, table[...], preferred_element_type=jnp.float32)

    @pl.when(step == 0)
    def _():
        total[...] = product

    @pl.when(step > 0)
    def _():
        total[...] += product

    @pl.when(step == pl.num_programs(0) - 1)
    def _():
        lane = lax.broadcasted_iota(jnp.int32, (rows, 2 * MC), 1)
        sign = jnp.where(lane < MC, -1.0, 1.0)
        packed = o_ref.shape[3] // (2 * MC)
        for f in range(facets):
            for s in range(subgrids):
                cut = slice(s * 2 * MC, (s + 1) * 2 * MC)
                first = total[2 * f * rows : (2 * f + 1) * rows, cut]
                second = total[(2 * f + 1) * rows : (2 * f + 2) * rows, cut]
                value = first + sign * pltpu.roll(second, MC, 1)
                j = f % packed
                o_ref[s, f // packed, :, j * 2 * MC : (j + 1) * 2 * MC] = value.astype(jnp.bfloat16)


def fourier(x, subgrids, slots, block_table, links, station_gains):
    facets, _, rows, length = x.shape
    width = subgrids * 2 * MC
    spread = FS // MC
    packed = FGRID if facets % FGRID == 0 else 1
    per_step = CHUNK // spread
    blocks = block_table.shape[1]
    span = slots + 128
    in_place = lambda array: pltpu.with_memory_space_constraint(array, pltpu.HBM)
    factors = [in_place(jnp.asarray(t)) for t in fourier_factors(subgrids)]
    out = (subgrids, facets // packed, rows, packed * 2 * MC)
    return pl.pallas_call(
        fourier_kernel,
        out_shape=(
            jax.ShapeDtypeStruct(out, jnp.bfloat16),
            jax.ShapeDtypeStruct((8, slots), jnp.float32),
            jax.ShapeDtypeStruct((8, slots), jnp.float32),
        ),
        grid=(length // CHUNK,),
        in_specs=[
            pl.BlockSpec(memory_space=pltpu.SMEM),
            pl.BlockSpec(memory_space=pltpu.HBM),
            pl.BlockSpec(memory_space=pltpu.HBM),
            pl.BlockSpec((per_step, width), lambda g: (g, 0)),
            pl.BlockSpec((per_step, width), lambda g: (g, 0)),
            pl.BlockSpec((spread, width), lambda g: (0, 0)),
            pl.BlockSpec((spread, width), lambda g: (0, 0)),
            pl.BlockSpec((facets, 2, rows, CHUNK), lambda g: (0, 0, 0, g)),
        ],
        out_specs=(
            pl.BlockSpec(out, lambda g: (0, 0, 0, 0)),
            pl.BlockSpec((8, slots), lambda g: (0, 0)),
            pl.BlockSpec((8, slots), lambda g: (0, 0)),
        ),
        scratch_shapes=[
            pltpu.VMEM((CHUNK, width), jnp.bfloat16),
            pltpu.VMEM((facets * 2 * rows, width), jnp.float32),
            pltpu.VMEM((blocks, 2, span), jnp.int32),
            pltpu.VMEM((blocks, 4, NST), jnp.float32),
            pltpu.SemaphoreType.DMA((blocks,)),
            pltpu.SemaphoreType.DMA((blocks,)),
        ],
        compiler_params=pltpu.CompilerParams(
            dimension_semantics=("arbitrary",), vmem_limit_bytes=48 << 20
        ),
    )(
        block_table,
        in_place(links),
        in_place(station_gains),
        *factors,
        x,
    )


def subgrid_tables():
    angle = unit_angles(SG, SG, SG)
    re = np.cos(angle) / math.sqrt(SG)
    im = np.sin(angle) / math.sqrt(SG)
    blocks = lambda t: t.reshape(SG, FGRID, MC)
    second = np.stack([blocks(re), -blocks(im)], axis=2).reshape(SG, 2 * SG)
    return [t.astype(jnp.bfloat16) for t in (re, im, second)]


def chirp_line():
    offset = np.arange(SG) - SG // 2
    angle = 2.0 * math.pi * w_chirp * (offset * offset) / float(SG * SG)
    return np.cos(angle).astype(np.float32), np.sin(angle).astype(np.float32)


def model_terms(pred, observed, first, second, alive):
    residual, lead, trail = [], [], []
    for p in range(NPOL):
        f1, f2 = p // 2, p % 2
        pred_re, pred_im = pred[p]
        first_re, first_im = first[2 * f1], first[2 * f1 + 1]
        second_re, second_im = second[2 * f2], second[2 * f2 + 1]
        both_re = first_re * second_re + first_im * second_im
        both_im = first_im * second_re - first_re * second_im
        resid_re = alive * (observed[2 * p] - (both_re * pred_re - both_im * pred_im))
        resid_im = alive * (observed[2 * p + 1] - (both_re * pred_im + both_im * pred_re))
        cross_re = second_re * pred_re + second_im * pred_im
        cross_im = second_im * pred_re - second_re * pred_im
        along_re = first_re * pred_re - first_im * pred_im
        along_im = first_re * pred_im + first_im * pred_re
        residual += [resid_re, resid_im]
        lead.append(
            (-(resid_re * cross_re - resid_im * cross_im), -(resid_re * cross_im + resid_im * cross_re))
        )
        trail.append(
            (-(resid_re * along_re + resid_im * along_im), -(resid_re * along_im - resid_im * along_re))
        )
    leading = [lead[2 * f][r] + lead[2 * f + 1][r] for f in range(2) for r in range(2)]
    trailing = [trail[f][r] + trail[f + 2][r] for f in range(2) for r in range(2)]
    return residual, leading, trailing


def nt_dot(left, right, **kw):
    return lax.dot_general(
        left, right, (((1,), (1,)), ((), ())), preferred_element_type=jnp.float32, **kw
    )


def chirped_rows(taper, chirp_ref):
    wide = taper.astype(jnp.float32)
    return jnp.concatenate(
        [
            taper,
            (wide * chirp_ref[0:1, :]).astype(jnp.bfloat16),
            (wide * chirp_ref[1:2, :]).astype(jnp.bfloat16),
        ],
        axis=0,
    )


def predict_kernel(
    sizes,
    contrib_ref,
    lead_ref,
    trail_ref,
    depth_ref,
    observed_ref,
    gains_ref,
    idents_ref,
    table_re_ref,
    table_im_ref,
    second_ref,
    chirp_ref,
    residual_ref,
    grad_ref,
    got,
    lines,
    tapers,
    right,
    left,
    part_out,
    part_in,
    observed_out,
    observed_in,
    record_out,
    record_in,
    got_send,
    got_recv,
    taper_send,
    taper_recv,
    observed_send,
    observed_recv,
    part_send,
    part_recv,
    record_send,
    record_recv,
):
    subgrids, pols, owners = sizes
    z, p, t = lax.axis_index("facet"), lax.axis_index("pol"), lax.axis_index("tm")
    slots = lead_ref.shape[0]
    _, groups, rows, width = contrib_ref.shape
    mesh_id = pl.DeviceIdType.MESH

    def remote(src, dst, send, recv, peer):
        return pltpu.make_async_remote_copy(
            src_ref=src,
            dst_ref=dst,
            send_sem=send,
            recv_sem=recv,
            device_id=peer,
            device_id_type=mesh_id,
        )

    across_total = subgrids * owners
    plane_total = pols * owners
    across = z * owners + t
    plane = p * owners + t

    def across_peer(d):
        other = lax.rem(across + d, across_total)
        return other, (other // owners, p, lax.rem(other, owners))

    def plane_peer(d):
        other = lax.rem(plane + d, plane_total)
        return other, (z, other // owners, lax.rem(other, owners))

    barrier = pltpu.get_barrier_semaphore()
    for d in range(1, across_total):
        pl.semaphore_signal(barrier, inc=1, device_id=across_peer(d)[1], device_id_type=mesh_id)
    for d in range(1, pols):
        q = lax.rem(p + d, pols)
        for o in range(owners):
            pl.semaphore_signal(barrier, inc=1, device_id=(z, q, o), device_id_type=mesh_id)
    pl.semaphore_wait(barrier, across_total - 1 + (pols - 1) * owners)

    quarter = observed_ref.shape[1]
    place = lax.broadcasted_iota(jnp.int32, (2 * NPOL, slots), 1)
    observed_out[...] = jnp.where(
        (place >= p * quarter) & (place < (p + 1) * quarter),
        jnp.concatenate([observed_ref[...]] * pols, axis=1),
        0.0,
    )
    copies = []
    for d in sorted(range(1, subgrids), key=lambda d: -min(d, subgrids - d)):
        other = lax.rem(z + d, subgrids)
        copies.append(
            remote(contrib_ref.at[other], got.at[z], got_send.at[d], got_recv.at[d], (other, p, t))
        )
    partner = lax.rem(t + 1, owners)
    taper_copies = [
        remote(ref, tapers.at[t, k], taper_send.at[k], taper_recv.at[k], (z, p, partner))
        for k, ref in enumerate((trail_ref, lead_ref))
    ]
    observed_copies = []
    for d in range(1, pols):
        q = lax.rem(p + d, pols)
        observed_copies.append(
            remote(
                observed_out, observed_in.at[p], observed_send.at[d], observed_recv.at[d], (z, q, t)
            )
        )
    for copy in copies + taper_copies + observed_copies:
        copy.start()

    table_re = jnp.concatenate([table_re_ref[i, t] for i in range(FGRID)], axis=0)
    table_im = jnp.concatenate([table_im_ref[i, t] for i in range(FGRID)], axis=0)

    turn = jnp.where(
        lax.broadcasted_iota(jnp.int32, (3 * slots, 2 * MC), 1) < MC, -1.0, 1.0
    )

    def prepare(owner, trail, lead):
        trail3 = chirped_rows(trail, chirp_ref)
        a = jnp.dot(trail3, second_ref[...], preferred_element_type=jnp.float32)
        b = jnp.concatenate(
            [
                turn * pltpu.roll(a[:, j * 2 * MC : (j + 1) * 2 * MC], MC, 1)
                for j in range(a.shape[1] // (2 * MC))
            ],
            axis=1,
        )
        n0, n1, n2 = slice(0, slots), slice(slots, 2 * slots), slice(2 * slots, 3 * slots)
        right[owner, 0:slots, :] = a[n0].astype(jnp.bfloat16)
        right[owner, slots : 2 * slots, :] = (a[n1] - b[n2]).astype(jnp.bfloat16)
        right[owner, 2 * slots : 3 * slots, :] = b[n0].astype(jnp.bfloat16)
        right[owner, 3 * slots : 4 * slots, :] = (b[n1] + a[n2]).astype(jnp.bfloat16)
        lead3 = chirped_rows(lead, chirp_ref)
        u = nt_dot(table_re, lead3)
        v = nt_dot(table_im, lead3)
        left[owner, 0] = u[:, n0]
        left[owner, 1] = v[:, n0]
        left[owner, 2] = u[:, n1] - v[:, n2]
        left[owner, 3] = u[:, n2] + v[:, n1]

    prepare(t, trail_ref[...], lead_ref[...])
    got[z] = contrib_ref[z]
    for copy in taper_copies:
        copy.wait()
    prepare(partner, tapers[partner, 0], tapers[partner, 1])
    for copy in copies:
        copy.wait()
    if width == 2 * SG:
        whole = got[...].reshape(subgrids * groups * rows, width)
    else:
        for f in range(subgrids * groups):
            i, j = f // FGRID, f % FGRID
            lines[i * rows : (i + 1) * rows, j * 2 * MC : (j + 1) * 2 * MC] = got[
                f // groups, f % groups
            ]
        whole = lines[...]
    for o in range(owners):
        spread = nt_dot(whole, right[o])
        for w in range(NW):
            g_re = spread[:, w * slots : (w + 1) * slots]
            g_im = spread[:, (NW + w) * slots : (NW + w + 1) * slots]
            l_re, l_im = left[o, 2 * w], left[o, 2 * w + 1]
            part_out[o, 2 * w : 2 * w + 1, :] = jnp.sum(l_re * g_re - l_im * g_im, axis=0, keepdims=True)
            part_out[o, 2 * w + 1 : 2 * w + 2, :] = jnp.sum(
                l_re * g_im + l_im * g_re, axis=0, keepdims=True
            )
        part_out[o, 2 * NW :, :] = jnp.zeros((8 - 2 * NW, slots), jnp.float32)

    part_copies = []
    for d in range(1, plane_total):
        other, peer = plane_peer(d)
        part_copies.append(
            remote(
                part_out.at[lax.rem(other, owners)],
                part_in.at[plane],
                part_send.at[d],
                part_recv.at[d],
                peer,
            )
        )
    for copy in part_copies:
        copy.start()
    part_in[plane] = part_out[t]
    observed_in[p] = observed_out[...]
    for copy in observed_copies:
        copy.wait()
    observed = observed_in[0]
    for q in range(1, pols):
        observed = observed + observed_in[q]
    depth = depth_ref[...].astype(jnp.float32)
    for copy in part_copies:
        copy.wait()

    pred = []
    per_pol = part_in.shape[0] // NPOL
    for q in range(NPOL):
        block = part_in[q * per_pol]
        for o in range(1, per_pol):
            block = block + part_in[q * per_pol + o]
        pred.append(
            tuple(
                sum(depth[w : w + 1] * block[2 * w + c : 2 * w + c + 1] for w in range(NW))
                for c in range(2)
            )
        )
    gains = gains_ref[...]
    idents = idents_ref[...]
    residual, leading, trailing = model_terms(
        pred,
        [observed[k : k + 1] for k in range(2 * NPOL)],
        [gains[k : k + 1] for k in range(4)],
        [gains[4 + k : 5 + k] for k in range(4)],
        idents[3:4],
    )
    for k in range(3):
        record_out[k : k + 1, :] = idents[k : k + 1]
    for k in range(4):
        record_out[3 + k : 4 + k, :] = leading[k]
        record_out[7 + k : 8 + k, :] = trailing[k]
    record_out[11:, :] = jnp.zeros((5, slots), jnp.float32)
    record_copies = []
    for d in range(1, across_total):
        other, peer = across_peer(d)
        record_copies.append(
            remote(record_out, record_in.at[across], record_send.at[d], record_recv.at[d], peer)
        )
    for copy in record_copies:
        copy.start()
    record_in[across] = record_out[...]
    rest = jnp.concatenate(residual, axis=0)
    own_rest = jnp.zeros((2 * NPOL, quarter), jnp.float32)
    for q in range(pols):
        own_rest = jnp.where(p == q, rest[:, q * quarter : (q + 1) * quarter], own_rest)
    residual_ref[...] = own_rest
    for copy in record_copies:
        copy.wait()

    piece = jnp.concatenate([record_in[d] for d in range(across_total)], axis=1)
    own_count = grad_ref.shape[1]
    index = (z * pols + p) * owners + t
    mine = (index * own_count + lax.broadcasted_iota(jnp.int32, (own_count, 1), 0)).astype(
        jnp.float32
    )
    match_first = mine == piece[0:1]
    match_second = mine == piece[1:2]
    weighted = jnp.concatenate(
        [
            jnp.where(match_first, piece[3 + k : 4 + k], 0.0)
            + jnp.where(match_second, piece[7 + k : 8 + k], 0.0)
            for k in range(4)
        ],
        axis=0,
    )
    high = weighted.astype(jnp.bfloat16)
    low = (weighted - high.astype(jnp.float32)).astype(jnp.bfloat16)
    channel_ids = lax.broadcasted_iota(jnp.int32, (NCH, 1), 0).astype(jnp.float32)
    onehot = jnp.where(channel_ids == piece[2:3], 1.0, 0.0).astype(jnp.bfloat16)
    summed = nt_dot(high, onehot) + nt_dot(low, onehot)
    for k in range(4):
        grad_ref[k] = grad_scale * summed[k * own_count : (k + 1) * own_count]


def predict(sizes, own_count, *operands):
    subgrids, pols, owners = sizes
    contrib, lead = operands[0], operands[1]
    _, groups, rows, width = contrib.shape
    slots = lead.shape[0]
    vmem = pl.BlockSpec(memory_space=pltpu.VMEM)
    dma = lambda n: pltpu.SemaphoreType.DMA((n,))
    across_total, plane_total = subgrids * owners, pols * owners
    return pl.pallas_call(
        functools.partial(predict_kernel, sizes),
        out_shape=(
            jax.ShapeDtypeStruct((2 * NPOL, slots // pols), jnp.float32),
            jax.ShapeDtypeStruct((4, own_count, NCH), jnp.float32),
        ),
        in_specs=[vmem] * len(operands),
        out_specs=(vmem, vmem),
        scratch_shapes=[
            pltpu.VMEM(contrib.shape, jnp.bfloat16),
            pltpu.VMEM((FGRID * rows, 2 * SG), jnp.bfloat16),
            pltpu.VMEM((owners, 2, slots, SG), jnp.bfloat16),
            pltpu.VMEM((owners, 2 * NW * slots, 2 * SG), jnp.bfloat16),
            pltpu.VMEM((owners, 4, FGRID * rows, slots), jnp.float32),
            pltpu.VMEM((owners, 8, slots), jnp.float32),
            pltpu.VMEM((plane_total, 8, slots), jnp.float32),
            pltpu.VMEM((8, slots), jnp.float32),
            pltpu.VMEM((pols, 8, slots), jnp.float32),
            pltpu.VMEM((16, slots), jnp.float32),
            pltpu.VMEM((across_total, 16, slots), jnp.float32),
            dma(subgrids),
            dma(subgrids),
            dma(2),
            dma(2),
            dma(pols),
            dma(pols),
            dma(plane_total),
            dma(plane_total),
            dma(across_total),
            dma(across_total),
        ],
        compiler_params=pltpu.CompilerParams(
            collective_id=0, has_side_effects=True, vmem_limit_bytes=48 << 20
        ),
    )(*operands)


def gather_lookups(block_ref, links_ref, gain_ref, gains_ref, idents_ref):
    blocks = block_ref.shape[2]
    slots = idents_ref.shape[1]
    span = slots + 128
    lane = lax.broadcasted_iota(jnp.int32, (1, slots), 1)
    place = lax.broadcasted_iota(jnp.int32, (span, slots), 0)
    lane_tall = lax.broadcasted_iota(jnp.int32, (span, slots), 1)
    begin = jnp.int32(0)
    member, picks, windows, tables = [], [], [], []
    channel = jnp.zeros((1, slots), jnp.float32)
    alive = jnp.zeros((1, slots), jnp.float32)
    for b in range(blocks):
        chosen, offset, amount = [block_ref[k, 0, b] for k in range(3)]
        row = jnp.minimum(lax.div(offset, 128), links_ref.shape[0] - span // 128)
        first = row * 128
        windows += [links_ref[row + k] for k in range(span // 128)]
        tables.append(gain_ref[chosen])
        inside = jnp.where((lane >= begin) & (lane < begin + amount), 1.0, 0.0)
        member.append(inside)
        alive += inside
        channel += inside * chosen.astype(jnp.float32)
        hit = place == lane_tall + (offset - first - begin)
        picks.append((jnp.where(hit, 1.0, 0.0) * inside).astype(jnp.bfloat16))
        begin = begin + amount
    links = jnp.concatenate(windows, axis=1)
    upper = links // 16
    lower = links - 16 * upper
    pieces = jnp.concatenate([upper, lower], axis=0).astype(jnp.float32).astype(jnp.bfloat16)
    found = jnp.dot(
        pieces, jnp.concatenate(picks, axis=0), preferred_element_type=jnp.float32
    )
    stations = 16.0 * found[0:2] + found[2:4]
    table = jnp.concatenate(tables, axis=0)
    high = table.astype(jnp.bfloat16)
    rest = table - high.astype(jnp.float32)
    middle = rest.astype(jnp.bfloat16)
    low = (rest - middle.astype(jnp.float32)).astype(jnp.bfloat16)
    split = jnp.concatenate([high, middle, low], axis=0)
    size = table.shape[0]
    names = lax.broadcasted_iota(jnp.int32, (table.shape[1], 1), 0).astype(jnp.float32)
    for side in range(2):
        pick = jnp.where(names == stations[side : side + 1], 1.0, 0.0).astype(jnp.bfloat16)
        three = jnp.dot(split, pick, preferred_element_type=jnp.float32)
        rows = three[:size] + three[size : 2 * size] + three[2 * size :]
        chosen = member[0] * rows[0:4]
        for b in range(1, blocks):
            chosen = chosen + member[b] * rows[4 * b : 4 * b + 4]
        gains_ref[4 * side : 4 * side + 4, :] = chosen
    idents_ref[0:2, :] = stations
    idents_ref[2:3, :] = channel
    idents_ref[3:4, :] = alive
    idents_ref[4:8, :] = jnp.zeros((4, slots), jnp.float32)


def fused_kernel(
    sizes,
    block_hbm,
    links_hbm,
    gain_hbm,
    p_hbm,
    q_hbm,
    c_hbm,
    s_hbm,
    x_hbm,
    lead_hbm,
    trail_hbm,
    depth_hbm,
    observed_hbm,
    table_re_hbm,
    table_im_hbm,
    second_hbm,
    chirp_hbm,
    residual_ref,
    grad_ref,
    block_ref,
    links_ref,
    gain_ref,
    p_ref,
    q_ref,
    c_ref,
    s_ref,
    x_ref,
    tapers,
    depths,
    observed_ref,
    table_ref,
    second_ref,
    chirp_ref,
    factors,
    contrib,
    got,
    right,
    left,
    gains_ref,
    idents_ref,
    side,
    part_out,
    part_in,
    observed_out,
    observed_in,
    rests,
    load_sem,
    chunk_sem,
    pair_send,
    pair_recv,
    chip_send,
    chip_recv,
    relay_send,
    relay_recv,
    far_send,
    far_recv,
    near_send,
    near_recv,
    observed_send,
    observed_recv,
    side_send,
    side_recv,
    part_send,
    part_recv,
):
    subgrids, pols, owners = sizes
    z, p, t = lax.axis_index("facet"), lax.axis_index("pol"), lax.axis_index("tm")
    _, _, slots, _ = tapers.shape
    facets, _, rows, length = x_ref.shape
    _, _, groups, _, width = contrib.shape
    side_z, own = lax.rem(z, 2), z // 2
    far = 1 - own
    pair_z = z + 1 - 2 * side_z
    far_z = z + 2 - 4 * own
    partner = lax.rem(t + 1, owners)
    mesh_id = pl.DeviceIdType.MESH

    def remote(src, dst, send, recv, peer):
        return pltpu.make_async_remote_copy(
            src_ref=src,
            dst_ref=dst,
            send_sem=send,
            recv_sem=recv,
            device_id=peer,
            device_id_type=mesh_id,
        )

    across_total = subgrids * owners
    across = z * owners + t

    def across_peer(d):
        other = lax.rem(across + d, across_total)
        return other, (other // owners, p, lax.rem(other, owners))

    barrier = pltpu.get_barrier_semaphore()
    for d in range(1, across_total):
        pl.semaphore_signal(barrier, inc=1, device_id=across_peer(d)[1], device_id_type=mesh_id)
    for d in range(1, pols):
        q = lax.rem(p + d, pols)
        for o in range(owners):
            pl.semaphore_signal(barrier, inc=1, device_id=(z, q, o), device_id_type=mesh_id)

    offsets = [
        (dz, dp, dt)
        for dz in sorted(range(subgrids), key=lambda d: -min(d, subgrids - d))
        for dp in reversed(range(pols))
        for dt in range(owners)
    ]
    offsets.remove((0, 0, 0))
    per_chunk = FGRID // PIECES
    chunks = facets // per_chunk
    x_loads = [
        pltpu.make_async_copy(
            x_hbm.at[pl.ds(c * per_chunk, per_chunk)],
            x_ref.at[pl.ds(c * per_chunk, per_chunk)],
            chunk_sem.at[c],
        )
        for c in range(chunks)
    ]
    pairs = [
        (c_hbm, c_ref),
        (s_hbm, s_ref),
        (p_hbm, p_ref),
        (q_hbm, q_ref),
        (trail_hbm, tapers.at[own, 0]),
        (lead_hbm, tapers.at[own, 1]),
        (depth_hbm, depths.at[own]),
        (observed_hbm, observed_ref),
        (chirp_hbm, chirp_ref),
        (second_hbm, second_ref),
        (table_re_hbm.at[pl.ds(own * 2 * groups, 2 * groups)], table_ref.at[0]),
        (table_im_hbm.at[pl.ds(own * 2 * groups, 2 * groups)], table_ref.at[1]),
        (block_hbm, block_ref),
        (links_hbm, links_ref),
        (gain_hbm, gain_ref),
    ]
    loads = [
        pltpu.make_async_copy(src, dst, load_sem.at[k]) for k, (src, dst) in enumerate(pairs)
    ]
    for copy in loads[:4]:
        copy.start()
    x_loads[0].start()
    for copy in loads[4:9]:
        copy.start()
    for copy in x_loads[1:]:
        copy.start()
    for copy in loads[9:]:
        copy.start()

    for copy in loads[:4]:
        copy.wait()
    spread = c_ref.shape[0]
    cosine, sine = c_ref[...], s_ref[...]
    for part in range(length // spread):
        factors[part * spread : (part + 1) * spread, :] = (
            p_ref[part : part + 1, :] * cosine + q_ref[part : part + 1, :] * sine
        ).astype(jnp.bfloat16)

    for copy in loads[4:9]:
        copy.wait()
    quarter = observed_ref.shape[1]
    place = lax.broadcasted_iota(jnp.int32, (2 * NPOL, slots), 1)
    observed_out[...] = jnp.where(
        (place >= p * quarter) & (place < (p + 1) * quarter),
        jnp.concatenate([observed_ref[...]] * pols, axis=1),
        0.0,
    )
    pl.semaphore_wait(barrier, across_total - 1 + (pols - 1) * owners)
    share = lambda q: pl.ds(pl.multiple_of(q * quarter, quarter), quarter)
    far_copies = [
        remote(
            tapers.at[own, side, share(p)],
            tapers.at[own, side, share(p)],
            far_send.at[side],
            far_recv.at[side],
            (far_z, p, t),
        )
        for side in range(2)
    ]
    far_copies.append(
        remote(depths.at[own], depths.at[own], far_send.at[2], far_recv.at[2], (far_z, p, t))
    )
    observed_copies = []
    for d in range(1, pols):
        q = lax.rem(p + d, pols)
        observed_copies.append(
            remote(
                observed_out, observed_in.at[p], observed_send.at[d], observed_recv.at[d], (z, q, t)
            )
        )
    for copy in far_copies + observed_copies:
        copy.start()
    others = pols - 1
    near_copies = [
        remote(
            tapers.at[far, side, share(p)],
            tapers.at[far, side, share(p)],
            near_send.at[others * side + d - 1],
            near_recv.at[others * side + d - 1],
            (z, lax.rem(p + d, pols), t),
        )
        for side in range(2)
        for d in (2, 1, 3)
    ]

    def forward(side):
        far_copies[side].wait_recv()
        for copy in near_copies[others * side : others * side + others]:
            copy.start()


    lane = lax.broadcasted_iota(jnp.int32, (rows, 2 * MC), 1)
    sign = jnp.where(lane < MC, -1.0, 1.0)
    part_width = width // PIECES
    pair_copies, chip_copies, relay_copies = [], [], []
    for c in range(chunks):
        x_loads[c].wait()
        x = x_ref[c * per_chunk : (c + 1) * per_chunk].reshape(per_chunk * 2 * rows, length)
        total = jnp.dot(x, factors[...], preferred_element_type=jnp.float32)
        group, piece = c // PIECES, c % PIECES
        for s in range(subgrids):
            cut = slice(s * 2 * MC, (s + 1) * 2 * MC)
            for f in range(per_chunk):
                first = total[2 * f * rows : (2 * f + 1) * rows, cut]
                second = total[(2 * f + 1) * rows : (2 * f + 2) * rows, cut]
                j = piece * per_chunk + f
                contrib[s % 2, s // 2, group, :, j * 2 * MC : (j + 1) * 2 * MC] = (
                    first + sign * pltpu.roll(second, MC, 1)
                ).astype(jnp.bfloat16)
        lanes = pl.ds(piece * part_width, part_width)
        pair_copies.append(
            remote(
                contrib.at[1 - side_z, :, group, :, lanes],
                got.at[:, side_z, group, t, :, lanes],
                pair_send.at[c],
                pair_recv.at[c],
                (pair_z, p, t),
            )
        )
        chip_copies.append(
            remote(
                contrib.at[side_z, :, group, :, lanes],
                got.at[:, side_z, group, t, :, lanes],
                chip_send.at[c],
                chip_recv.at[c],
                (z, p, partner),
            )
        )
        relay_copies.append(
            remote(
                got.at[:, 1 - side_z, group, t, :, lanes],
                got.at[:, 1 - side_z, group, t, :, lanes],
                relay_send.at[c],
                relay_recv.at[c],
                (z, p, partner),
            )
        )
        pair_copies[c].start()
        chip_copies[c].start()
        if c == chunks - FORWARD:
            forward(0)

    for k in range(2):
        for group in range(groups):
            got[k, side_z, group, t] = contrib[side_z, k, group]
    for copy in loads[9:]:
        copy.wait()
    gather_lookups(block_ref, links_ref, gain_ref, gains_ref, idents_ref)
    observed_in[p] = observed_out[...]
    for copy in observed_copies:
        copy.wait()
    observed = observed_in[0]
    for q in range(1, pols):
        observed = observed + observed_in[q]
    side[across, 0:8] = gains_ref[...]
    side[across, 8:16] = observed
    side[across, 16:20] = idents_ref[0:4]
    side_copies = []
    for d in range(1, across_total):
        other, peer = across_peer(d)
        side_copies.append(
            remote(side.at[across], side.at[across], side_send.at[d], side_recv.at[d], peer)
        )
    for copy in side_copies:
        copy.start()
    forward(1)

    span = 2 * groups * owners * rows
    table_re = table_ref[0].reshape(span, SG)
    table_im = table_ref[1].reshape(span, SG)
    turn = jnp.where(
        lax.broadcasted_iota(jnp.int32, (3 * slots, 2 * MC), 1) < MC, -1.0, 1.0
    )

    def prepare_right(k):
        trail3 = chirped_rows(tapers[k, 0], chirp_ref)
        a = jnp.dot(trail3, second_ref[...], preferred_element_type=jnp.float32)
        b = jnp.concatenate(
            [
                turn * pltpu.roll(a[:, j * 2 * MC : (j + 1) * 2 * MC], MC, 1)
                for j in range(a.shape[1] // (2 * MC))
            ],
            axis=1,
        )
        n0, n1, n2 = slice(0, slots), slice(slots, 2 * slots), slice(2 * slots, 3 * slots)
        right[k, 0:slots, :] = a[n0].astype(jnp.bfloat16)
        right[k, slots : 2 * slots, :] = (a[n1] - b[n2]).astype(jnp.bfloat16)
        right[k, 2 * slots : 3 * slots, :] = b[n0].astype(jnp.bfloat16)
        right[k, 3 * slots : 4 * slots, :] = (b[n1] + a[n2]).astype(jnp.bfloat16)

    def prepare_left(k):
        n0, n1, n2 = slice(0, slots), slice(slots, 2 * slots), slice(2 * slots, 3 * slots)
        lead3 = chirped_rows(tapers[k, 1], chirp_ref)
        u = nt_dot(table_re, lead3)
        v = nt_dot(table_im, lead3)
        left[k, 0] = u[:, n0]
        left[k, 1] = v[:, n0]
        left[k, 2] = u[:, n1] - v[:, n2]
        left[k, 3] = u[:, n2] + v[:, n1]

    prepare_right(own)
    prepare_left(own)
    for pair, relay in zip(pair_copies[:-1], relay_copies[:-1]):
        pair.wait_recv()
        relay.start()
    for copy in near_copies[:others]:
        copy.wait_recv()
    prepare_right(far)
    pair_copies[-1].wait_recv()
    relay_copies[-1].start()
    for copy in [far_copies[2]] + near_copies[others:]:
        copy.wait_recv()
    prepare_left(far)
    for copy in chip_copies + relay_copies:
        copy.wait()
    for k in range(2):
        spread_v = nt_dot(got[k].reshape(span, width), right[k])
        weights = depths[k].astype(jnp.float32)
        sums = [0.0, 0.0]
        for w in range(NW):
            g_re = spread_v[:, w * slots : (w + 1) * slots]
            g_im = spread_v[:, (NW + w) * slots : (NW + w + 1) * slots]
            l_re, l_im = left[k, 2 * w], left[k, 2 * w + 1]
            weight = weights[w : w + 1]
            sums[0] += weight * jnp.sum(l_re * g_re - l_im * g_im, axis=0, keepdims=True)
            sums[1] += weight * jnp.sum(l_re * g_im + l_im * g_re, axis=0, keepdims=True)
        for c in range(2):
            part_out[2 * c + k : 2 * c + k + 1, :] = sums[c]

    part_copies = []
    for dz, dp, dt in offsets:
        peer = (lax.rem(z + dz, subgrids), lax.rem(p + dp, pols), lax.rem(t + dt, owners))
        k = (dz * pols + dp) * owners + dt
        part_copies.append(
            remote(part_out, part_in.at[z, p, t], part_send.at[k], part_recv.at[k], peer)
        )
    for copy in part_copies:
        copy.start()
    part_in[z, p, t] = part_out[...]
    for copy in pair_copies + far_copies + near_copies:
        copy.wait_send()
    for copy in side_copies:
        copy.wait()

    own_count = grad_ref.shape[0]
    index = (z * pols + p) * owners + t
    mine = (index * own_count + lax.broadcasted_iota(jnp.int32, (own_count, 1), 0)).astype(
        jnp.float32
    )
    channel_ids = lax.broadcasted_iota(jnp.int32, (NCH, 1), 0).astype(jnp.float32)
    first_here = [jnp.where(mine == side[d, 16:17], 1.0, 0.0) for d in range(across_total)]
    second_here = [jnp.where(mine == side[d, 17:18], 1.0, 0.0) for d in range(across_total)]
    onehot = jnp.concatenate(
        [
            jnp.where(channel_ids == side[d, 18:19], 1.0, 0.0).astype(jnp.bfloat16)
            for d in range(across_total)
        ],
        axis=1,
    )
    column = lambda k: jnp.concatenate([side[d, k : k + 1] for d in range(across_total)], axis=0)
    gains = [column(k) for k in range(8)]
    observed = [column(8 + k) for k in range(8)]
    alive = column(19)
    for copy in part_copies:
        copy.wait()

    pred = []
    for q in range(NPOL):
        both = [[part_in[y, q, o] + part_in[y + 2, q, o] for o in range(owners)] for y in range(2)]
        pred.append(
            tuple(
                jnp.concatenate(
                    [
                        both[s % 2][o][2 * c + s // 2 : 2 * c + s // 2 + 1]
                        for s in range(subgrids)
                        for o in range(owners)
                    ],
                    axis=0,
                )
                for c in range(2)
            )
        )
    residual, leading, trailing = model_terms(pred, observed, gains[:4], gains[4:], alive)
    for k in range(2 * NPOL):
        rests[:, k : k + 1, :] = residual[k][:, None, :]
    rest = rests[across]
    own_rest = jnp.zeros((2 * NPOL, quarter), jnp.float32)
    for q in range(pols):
        own_rest = jnp.where(p == q, rest[:, q * quarter : (q + 1) * quarter], own_rest)
    residual_ref[...] = own_rest

    weighted = jnp.concatenate(
        [
            jnp.concatenate(
                [
                    first_here[d] * leading[k][d : d + 1]
                    + second_here[d] * trailing[k][d : d + 1]
                    for d in range(across_total)
                ],
                axis=1,
            )
            for k in range(4)
        ],
        axis=0,
    )
    high = weighted.astype(jnp.bfloat16)
    low = (weighted - high.astype(jnp.float32)).astype(jnp.bfloat16)
    summed = nt_dot(high, onehot) + nt_dot(low, onehot)
    lane_group = lax.broadcasted_iota(jnp.int32, (own_count, 128), 1) // 32
    mixed = []
    for g in range(NCH // 32):
        base = g // 4 * 128
        built = None
        for k in range(4):
            block = summed[k * own_count : (k + 1) * own_count, base : base + 128]
            shift = 32 * (k - g % 4) % 128
            block = pltpu.roll(block, shift, 1) if shift else block
            built = block if built is None else jnp.where(lane_group == k, block, built)
        mixed.append(grad_scale * built)
    mixed = jnp.concatenate(mixed, axis=0)
    high = mixed.astype(jnp.bfloat16)
    low = (mixed - high.astype(jnp.float32)).astype(jnp.bfloat16)
    came = lax.broadcasted_iota(jnp.int32, (128, 128), 0)
    goes = lax.broadcasted_iota(jnp.int32, (128, 128), 1)
    order = jnp.where(goes == came % 32 * 4 + came // 32, 1.0, 0.0).astype(jnp.bfloat16)
    placed = jnp.dot(
        jnp.concatenate([high, low], axis=0), order, preferred_element_type=jnp.float32
    )
    placed = placed[: mixed.shape[0]] + placed[mixed.shape[0] :]
    for g in range(NCH // 32):
        grad_ref[:, g * 128 : (g + 1) * 128] = placed[g * own_count : (g + 1) * own_count]


def emit_kernel(residual_ref, grad_ref, residual_out, grad_out, sems):
    copies = [
        pltpu.make_async_copy(residual_ref, residual_out, sems.at[0]),
        pltpu.make_async_copy(grad_ref, grad_out, sems.at[1]),
    ]
    for copy in copies:
        copy.start()
    for copy in copies:
        copy.wait()


def fused(sizes, own_count, *operands):
    subgrids, pols, owners = sizes
    block_table, links, gains = operands[0:3]
    x, lead, trail, depth, observed = operands[7:12]
    facets, _, rows, length = x.shape
    slots = lead.shape[0]
    width = subgrids * 2 * MC
    spread = FS // MC
    groups = facets // FGRID
    chunks = facets // (FGRID // PIECES)
    hbm = pl.BlockSpec(memory_space=pltpu.HBM)
    vmem = pl.BlockSpec(memory_space=pltpu.VMEM)
    dma = lambda n: pltpu.SemaphoreType.DMA((n,))
    held = lambda a: pltpu.VMEM(a.shape, a.dtype)
    across_total, all_total = subgrids * owners, subgrids * pols * owners
    f32, bf16 = jnp.float32, jnp.bfloat16
    residual, grad = pl.pallas_call(
        functools.partial(fused_kernel, sizes),
        out_shape=(
            jax.ShapeDtypeStruct(observed.shape, f32),
            jax.ShapeDtypeStruct((own_count, 4 * NCH), f32),
        ),
        in_specs=[hbm] * len(operands),
        out_specs=(vmem, vmem),
        scratch_shapes=[
            pltpu.SMEM(block_table.shape, jnp.int32),
            held(links),
            held(gains),
            pltpu.VMEM((length // spread, width), f32),
            pltpu.VMEM((length // spread, width), f32),
            pltpu.VMEM((spread, width), f32),
            pltpu.VMEM((spread, width), f32),
            held(x),
            pltpu.VMEM((2, 2, slots, SG), bf16),
            pltpu.VMEM((2,) + depth.shape, bf16),
            held(observed),
            pltpu.VMEM((2, 2 * groups, owners, rows, SG), bf16),
            pltpu.VMEM((SG, 2 * SG), bf16),
            pltpu.VMEM((2, SG), f32),
            pltpu.VMEM((length, width), bf16),
            pltpu.VMEM((2, 2, groups, rows, 2 * SG), bf16),
            pltpu.VMEM((2, 2, groups, owners, rows, 2 * SG), bf16),
            pltpu.VMEM((2, 2 * NW * slots, 2 * SG), bf16),
            pltpu.VMEM((2, 4, 2 * groups * owners * rows, slots), f32),
            pltpu.VMEM((8, slots), f32),
            pltpu.VMEM((8, slots), f32),
            pltpu.VMEM((across_total, 20, slots), f32),
            pltpu.VMEM((4, slots), f32),
            pltpu.VMEM((subgrids, pols, owners, 4, slots), f32),
            pltpu.VMEM((8, slots), f32),
            pltpu.VMEM((pols, 8, slots), f32),
            pltpu.VMEM((across_total, 8, slots), f32),
            dma(15),
            dma(chunks),
            dma(chunks),
            dma(chunks),
            dma(chunks),
            dma(chunks),
            dma(chunks),
            dma(chunks),
            dma(3),
            dma(3),
            dma(2 * pols - 2),
            dma(2 * pols - 2),
            dma(pols),
            dma(pols),
            dma(across_total),
            dma(across_total),
            dma(all_total),
            dma(all_total),
        ],
        compiler_params=pltpu.CompilerParams(
            collective_id=0, has_side_effects=True, vmem_limit_bytes=36 << 20
        ),
    )(*[pltpu.with_memory_space_constraint(a, pltpu.HBM) for a in operands])
    return pl.pallas_call(
        emit_kernel,
        out_shape=(
            jax.ShapeDtypeStruct(residual.shape, f32),
            jax.ShapeDtypeStruct(grad.shape, f32),
        ),
        in_specs=[vmem] * 2,
        out_specs=[hbm] * 2,
        scratch_shapes=[dma(2)],
        compiler_params=pltpu.CompilerParams(vmem_limit_bytes=1 << 20),
    )(residual, grad)


def on_device(
    tile_spectral_lines,
    taper_leading_axis,
    taper_trailing_axis,
    depth_layer_factors,
    measured_correlations,
    visibility_groups_table,
    antenna_links,
    complex_receiver_factors,
):
    sizes = tuple(lax.axis_size(name) for name in ("facet", "pol", "tm"))
    subgrids, pols, owners = sizes
    slots = taper_leading_axis.shape[2]
    quarter = measured_correlations.shape[3]
    rows = tile_spectral_lines.shape[3]

    block_table = visibility_groups_table.reshape(3, visibility_groups_table.shape[3])
    observed = measured_correlations.reshape(2 * NPOL, quarter)

    if tile_spectral_lines.shape[0] % FGRID == 0 and sizes == (4, NPOL, 2):
        table_re, table_im, second = [jnp.asarray(t) for t in subgrid_tables()]
        own_count = NST // (subgrids * pols * owners)
        residual, gain_grad = fused(
            sizes,
            own_count,
            visibility_groups_table.reshape(3, 1, visibility_groups_table.shape[3]),
            jnp.transpose(antenna_links.reshape(2, -1, 128), (1, 0, 2)),
            complex_receiver_factors,
            *[jnp.asarray(t) for t in fourier_factors(subgrids)],
            tile_spectral_lines[:, 0],
            taper_leading_axis.reshape(slots, SG),
            taper_trailing_axis.reshape(slots, SG),
            depth_layer_factors.reshape(NW, slots),
            observed,
            table_re.reshape(FGRID, owners, rows, SG),
            table_im.reshape(FGRID, owners, rows, SG),
            second,
            jnp.asarray(np.stack(chirp_line())),
        )
        return residual.reshape(1, 2 * NPOL, 1, quarter), gain_grad

    contrib, gains, idents = fourier(
        tile_spectral_lines[:, 0],
        subgrids,
        slots,
        block_table,
        antenna_links,
        complex_receiver_factors,
    )
    table_re, table_im, second = [jnp.asarray(t) for t in subgrid_tables()]
    cosine, sine = chirp_line()
    own_count = NST // (subgrids * pols * owners)
    residual, grad = predict(
        sizes,
        own_count,
        contrib,
        taper_leading_axis.reshape(slots, SG),
        taper_trailing_axis.reshape(slots, SG),
        depth_layer_factors.reshape(NW, slots),
        observed,
        gains,
        idents,
        table_re.reshape(FGRID, owners, rows, SG),
        table_im.reshape(FGRID, owners, rows, SG),
        second,
        jnp.asarray(np.stack([cosine, sine])),
    )
    gain_grad = jnp.transpose(grad, (1, 2, 0)).reshape(own_count, 4 * NCH)
    return residual.reshape(1, 2 * NPOL, 1, quarter), gain_grad


def solution(mesh):
    return jax.shard_map(
        on_device,
        mesh=mesh,
        in_specs=(
            P("facet", "pol", None, "tm", None),
            P("facet", "tm", None, None),
            P("facet", "tm", None, None),
            P("facet", "tm", None, None),
            P("facet", None, "tm", "pol"),
            P("facet", "tm", None, None),
            P(),
            P(),
        ),
        out_specs=(P("facet", None, "tm", "pol"), P(("facet", "pol", "tm"), None)),
        check_vma=False,
    )
```

```python
import functools
import math

import jax
import jax.numpy as jnp
import numpy as np
from jax import lax
from jax.experimental import pallas as pl
from jax.experimental.pallas import tpu as pltpu
from jax.sharding import PartitionSpec as P

FGRID = 8
FS = 4096
MC = 64
SG = 512
NPOL = 4
NW = 2
NCH = 256
NST = 512
CHUNK = 1024
PIECES = 2
FORWARD = 2

w_chirp = 0.37
grad_scale = 0.1


def unit_angles(left, right, length):
    product = np.outer(np.arange(left), np.arange(right)) % length
    return 2.0 * math.pi * product / length


def fourier_factors(subgrids):
    spread = FS // MC
    alpha = unit_angles(FS // spread, MC, MC)
    p = np.concatenate([np.cos(alpha), -np.sin(alpha)], axis=1) / math.sqrt(FS)
    q = np.concatenate([-np.sin(alpha), -np.cos(alpha)], axis=1) / math.sqrt(FS)
    beta = unit_angles(spread, subgrids * MC, FS).reshape(spread, subgrids, 1, MC)
    beta = np.broadcast_to(beta, (spread, subgrids, 2, MC)).reshape(spread, subgrids * 2 * MC)
    tile = lambda t: np.tile(t, (1, subgrids)).astype(np.float32)
    return (
        tile(p),
        tile(q),
        np.cos(beta).astype(np.float32),
        np.sin(beta).astype(np.float32),
    )


def fetch_lookups(block_ref, links_ref, gain_ref, window, channel_gain, window_sem, gain_sem):
    blocks, _, span = window.shape
    copies = []
    for b in range(blocks):
        first = jnp.minimum(block_ref[1, b] // 128 * 128, links_ref.shape[1] - span)
        first = pl.multiple_of(first, 128)
        copies.append(
            pltpu.make_async_copy(
                links_ref.at[:, pl.ds(first, span)], window.at[b], window_sem.at[b]
            )
        )
        copies.append(
            pltpu.make_async_copy(
                gain_ref.at[block_ref[0, b]], channel_gain.at[b], gain_sem.at[b]
            )
        )
    return copies


def use_lookups(block_ref, links_ref, window, channel_gain, gains_ref, idents_ref):
    blocks, _, span = window.shape
    slots = idents_ref.shape[1]
    lane = lax.broadcasted_iota(jnp.int32, (1, slots), 1)
    place = lax.broadcasted_iota(jnp.int32, (span, slots), 0)
    lane_tall = lax.broadcasted_iota(jnp.int32, (span, slots), 1)
    begin = jnp.int32(0)
    member, picks = [], []
    channel = jnp.zeros((1, slots), jnp.float32)
    alive = jnp.zeros((1, slots), jnp.float32)
    for b in range(blocks):
        offset, amount = block_ref[1, b], block_ref[2, b]
        first = jnp.minimum(offset // 128 * 128, links_ref.shape[1] - span)
        inside = jnp.where((lane >= begin) & (lane < begin + amount), 1.0, 0.0)
        member.append(inside)
        alive += inside
        channel += inside * block_ref[0, b].astype(jnp.float32)
        hit = place == lane_tall + (offset - first - begin)
        picks.append((jnp.where(hit, 1.0, 0.0) * inside).astype(jnp.bfloat16))
        begin = begin + amount
    links = jnp.concatenate([window[b] for b in range(blocks)], axis=1)
    upper = links // 16
    lower = links - 16 * upper
    pieces = jnp.concatenate([upper, lower], axis=0).astype(jnp.float32).astype(jnp.bfloat16)
    found = jnp.dot(
        pieces, jnp.concatenate(picks, axis=0), preferred_element_type=jnp.float32
    )
    stations = 16.0 * found[0:2] + found[2:4]
    table = channel_gain[...].reshape(blocks * 4, channel_gain.shape[2])
    high = table.astype(jnp.bfloat16)
    rest = table - high.astype(jnp.float32)
    middle = rest.astype(jnp.bfloat16)
    low = (rest - middle.astype(jnp.float32)).astype(jnp.bfloat16)
    names = lax.broadcasted_iota(jnp.int32, (table.shape[1], 1), 0).astype(jnp.float32)
    for side in range(2):
        pick = jnp.where(names == stations[side : side + 1], 1.0, 0.0).astype(jnp.bfloat16)
        rows = (
            jnp.dot(high, pick, preferred_element_type=jnp.float32)
            + jnp.dot(middle, pick, preferred_element_type=jnp.float32)
            + jnp.dot(low, pick, preferred_element_type=jnp.float32)
        )
        chosen = member[0] * rows[0:4]
        for b in range(1, blocks):
            chosen = chosen + member[b] * rows[4 * b : 4 * b + 4]
        gains_ref[4 * side : 4 * side + 4, :] = chosen
    idents_ref[0:2, :] = stations
    idents_ref[2:3, :] = channel
    idents_ref[3:4, :] = alive
    idents_ref[4:8, :] = jnp.zeros((4, slots), jnp.float32)


def fourier_kernel(
    block_ref,
    links_ref,
    gain_ref,
    p_ref,
    q_ref,
    c_ref,
    s_ref,
    x_ref,
    o_ref,
    gains_ref,
    idents_ref,
    table,
    total,
    window,
    channel_gain,
    window_sem,
    gain_sem,
):
    step = pl.program_id(0)
    copies = fetch_lookups(
        block_ref, links_ref, gain_ref, window, channel_gain, window_sem, gain_sem
    )

    @pl.when(step == 0)
    def _():
        for copy in copies:
            copy.start()

    @pl.when(step == pl.num_programs(0) - 1)
    def _():
        for copy in copies:
            copy.wait()
        use_lookups(block_ref, links_ref, window, channel_gain, gains_ref, idents_ref)

    facets, _, rows, chunk = x_ref.shape
    subgrids = o_ref.shape[0]
    spread = c_ref.shape[0]
    cosine, sine = c_ref[...], s_ref[...]
    for part in range(chunk // spread):
        lead = p_ref[part : part + 1, :]
        other = q_ref[part : part + 1, :]
        table[part * spread : (part + 1) * spread, :] = (lead * cosine + other * sine).astype(
            jnp.bfloat16
        )
    x = x_ref[...].reshape(facets * 2 * rows, chunk)
    product = jnp.dot(x, table[...], preferred_element_type=jnp.float32)

    @pl.when(step == 0)
    def _():
        total[...] = product

    @pl.when(step > 0)
    def _():
        total[...] += product

    @pl.when(step == pl.num_programs(0) - 1)
    def _():
        lane = lax.broadcasted_iota(jnp.int32, (rows, 2 * MC), 1)
        sign = jnp.where(lane < MC, -1.0, 1.0)
        packed = o_ref.shape[3] // (2 * MC)
        for f in range(facets):
            for s in range(subgrids):
                cut = slice(s * 2 * MC, (s + 1) * 2 * MC)
                first = total[2 * f * rows : (2 * f + 1) * rows, cut]
                second = total[(2 * f + 1) * rows : (2 * f + 2) * rows, cut]
                value = first + sign * pltpu.roll(second, MC, 1)
                j = f % packed
                o_ref[s, f // packed, :, j * 2 * MC : (j + 1) * 2 * MC] = value.astype(jnp.bfloat16)


def fourier(x, subgrids, slots, block_table, links, station_gains):
    facets, _, rows, length = x.shape
    width = subgrids * 2 * MC
    spread = FS // MC
    packed = FGRID if facets % FGRID == 0 else 1
    per_step = CHUNK // spread
    blocks = block_table.shape[1]
    span = slots + 128
    in_place = lambda array: pltpu.with_memory_space_constraint(array, pltpu.HBM)
    factors = [in_place(jnp.asarray(t)) for t in fourier_factors(subgrids)]
    out = (subgrids, facets // packed, rows, packed * 2 * MC)
    return pl.pallas_call(
        fourier_kernel,
        out_shape=(
            jax.ShapeDtypeStruct(out, jnp.bfloat16),
            jax.ShapeDtypeStruct((8, slots), jnp.float32),
            jax.ShapeDtypeStruct((8, slots), jnp.float32),
        ),
        grid=(length // CHUNK,),
        in_specs=[
            pl.BlockSpec(memory_space=pltpu.SMEM),
            pl.BlockSpec(memory_space=pltpu.HBM),
            pl.BlockSpec(memory_space=pltpu.HBM),
            pl.BlockSpec((per_step, width), lambda g: (g, 0)),
            pl.BlockSpec((per_step, width), lambda g: (g, 0)),
            pl.BlockSpec((spread, width), lambda g: (0, 0)),
            pl.BlockSpec((spread, width), lambda g: (0, 0)),
            pl.BlockSpec((facets, 2, rows, CHUNK), lambda g: (0, 0, 0, g)),
        ],
        out_specs=(
            pl.BlockSpec(out, lambda g: (0, 0, 0, 0)),
            pl.BlockSpec((8, slots), lambda g: (0, 0)),
            pl.BlockSpec((8, slots), lambda g: (0, 0)),
        ),
        scratch_shapes=[
            pltpu.VMEM((CHUNK, width), jnp.bfloat16),
            pltpu.VMEM((facets * 2 * rows, width), jnp.float32),
            pltpu.VMEM((blocks, 2, span), jnp.int32),
            pltpu.VMEM((blocks, 4, NST), jnp.float32),
            pltpu.SemaphoreType.DMA((blocks,)),
            pltpu.SemaphoreType.DMA((blocks,)),
        ],
        compiler_params=pltpu.CompilerParams(
            dimension_semantics=("arbitrary",), vmem_limit_bytes=48 << 20
        ),
    )(
        block_table,
        in_place(links),
        in_place(station_gains),
        *factors,
        x,
    )


def subgrid_tables():
    angle = unit_angles(SG, SG, SG)
    re = np.cos(angle) / math.sqrt(SG)
    im = np.sin(angle) / math.sqrt(SG)
    blocks = lambda t: t.reshape(SG, FGRID, MC)
    second = np.stack([blocks(re), -blocks(im)], axis=2).reshape(SG, 2 * SG)
    return [t.astype(jnp.bfloat16) for t in (re, im, second)]


def chirp_line():
    offset = np.arange(SG) - SG // 2
    angle = 2.0 * math.pi * w_chirp * (offset * offset) / float(SG * SG)
    return np.cos(angle).astype(np.float32), np.sin(angle).astype(np.float32)


def model_terms(pred, observed, first, second, alive):
    residual, lead, trail = [], [], []
    for p in range(NPOL):
        f1, f2 = p // 2, p % 2
        pred_re, pred_im = pred[p]
        first_re, first_im = first[2 * f1], first[2 * f1 + 1]
        second_re, second_im = second[2 * f2], second[2 * f2 + 1]
        both_re = first_re * second_re + first_im * second_im
        both_im = first_im * second_re - first_re * second_im
        resid_re = alive * (observed[2 * p] - (both_re * pred_re - both_im * pred_im))
        resid_im = alive * (observed[2 * p + 1] - (both_re * pred_im + both_im * pred_re))
        cross_re = second_re * pred_re + second_im * pred_im
        cross_im = second_im * pred_re - second_re * pred_im
        along_re = first_re * pred_re - first_im * pred_im
        along_im = first_re * pred_im + first_im * pred_re
        residual += [resid_re, resid_im]
        lead.append(
            (-(resid_re * cross_re - resid_im * cross_im), -(resid_re * cross_im + resid_im * cross_re))
        )
        trail.append(
            (-(resid_re * along_re + resid_im * along_im), -(resid_re * along_im - resid_im * along_re))
        )
    leading = [lead[2 * f][r] + lead[2 * f + 1][r] for f in range(2) for r in range(2)]
    trailing = [trail[f][r] + trail[f + 2][r] for f in range(2) for r in range(2)]
    return residual, leading, trailing


def nt_dot(left, right, **kw):
    return lax.dot_general(
        left, right, (((1,), (1,)), ((), ())), preferred_element_type=jnp.float32, **kw
    )


def chirped_rows(taper, chirp_ref):
    wide = taper.astype(jnp.float32)
    return jnp.concatenate(
        [
            taper,
            (wide * chirp_ref[0:1, :]).astype(jnp.bfloat16),
            (wide * chirp_ref[1:2, :]).astype(jnp.bfloat16),
        ],
        axis=0,
    )


def predict_kernel(
    sizes,
    contrib_ref,
    lead_ref,
    trail_ref,
    depth_ref,
    observed_ref,
    gains_ref,
    idents_ref,
    table_re_ref,
    table_im_ref,
    second_ref,
    chirp_ref,
    residual_ref,
    grad_ref,
    got,
    lines,
    tapers,
    right,
    left,
    part_out,
    part_in,
    observed_out,
    observed_in,
    record_out,
    record_in,
    got_send,
    got_recv,
    taper_send,
    taper_recv,
    observed_send,
    observed_recv,
    part_send,
    part_recv,
    record_send,
    record_recv,
):
    subgrids, pols, owners = sizes
    z, p, t = lax.axis_index("facet"), lax.axis_index("pol"), lax.axis_index("tm")
    slots = lead_ref.shape[0]
    _, groups, rows, width = contrib_ref.shape
    mesh_id = pl.DeviceIdType.MESH

    def remote(src, dst, send, recv, peer):
        return pltpu.make_async_remote_copy(
            src_ref=src,
            dst_ref=dst,
            send_sem=send,
            recv_sem=recv,
            device_id=peer,
            device_id_type=mesh_id,
        )

    across_total = subgrids * owners
    plane_total = pols * owners
    across = z * owners + t
    plane = p * owners + t

    def across_peer(d):
        other = lax.rem(across + d, across_total)
        return other, (other // owners, p, lax.rem(other, owners))

    def plane_peer(d):
        other = lax.rem(plane + d, plane_total)
        return other, (z, other // owners, lax.rem(other, owners))

    barrier = pltpu.get_barrier_semaphore()
    for d in range(1, across_total):
        pl.semaphore_signal(barrier, inc=1, device_id=across_peer(d)[1], device_id_type=mesh_id)
    for d in range(1, pols):
        q = lax.rem(p + d, pols)
        for o in range(owners):
            pl.semaphore_signal(barrier, inc=1, device_id=(z, q, o), device_id_type=mesh_id)
    pl.semaphore_wait(barrier, across_total - 1 + (pols - 1) * owners)

    quarter = observed_ref.shape[1]
    place = lax.broadcasted_iota(jnp.int32, (2 * NPOL, slots), 1)
    observed_out[...] = jnp.where(
        (place >= p * quarter) & (place < (p + 1) * quarter),
        jnp.concatenate([observed_ref[...]] * pols, axis=1),
        0.0,
    )
    copies = []
    for d in sorted(range(1, subgrids), key=lambda d: -min(d, subgrids - d)):
        other = lax.rem(z + d, subgrids)
        copies.append(
            remote(contrib_ref.at[other], got.at[z], got_send.at[d], got_recv.at[d], (other, p, t))
        )
    partner = lax.rem(t + 1, owners)
    taper_copies = [
        remote(ref, tapers.at[t, k], taper_send.at[k], taper_recv.at[k], (z, p, partner))
        for k, ref in enumerate((trail_ref, lead_ref))
    ]
    observed_copies = []
    for d in range(1, pols):
        q = lax.rem(p + d, pols)
        observed_copies.append(
            remote(
                observed_out, observed_in.at[p], observed_send.at[d], observed_recv.at[d], (z, q, t)
            )
        )
    for copy in copies + taper_copies + observed_copies:
        copy.start()

    table_re = jnp.concatenate([table_re_ref[i, t] for i in range(FGRID)], axis=0)
    table_im = jnp.concatenate([table_im_ref[i, t] for i in range(FGRID)], axis=0)

    turn = jnp.where(
        lax.broadcasted_iota(jnp.int32, (3 * slots, 2 * MC), 1) < MC, -1.0, 1.0
    )

    def prepare(owner, trail, lead):
        trail3 = chirped_rows(trail, chirp_ref)
        a = jnp.dot(trail3, second_ref[...], preferred_element_type=jnp.float32)
        b = jnp.concatenate(
            [
                turn * pltpu.roll(a[:, j * 2 * MC : (j + 1) * 2 * MC], MC, 1)
                for j in range(a.shape[1] // (2 * MC))
            ],
            axis=1,
        )
        n0, n1, n2 = slice(0, slots), slice(slots, 2 * slots), slice(2 * slots, 3 * slots)
        right[owner, 0:slots, :] = a[n0].astype(jnp.bfloat16)
        right[owner, slots : 2 * slots, :] = (a[n1] - b[n2]).astype(jnp.bfloat16)
        right[owner, 2 * slots : 3 * slots, :] = b[n0].astype(jnp.bfloat16)
        right[owner, 3 * slots : 4 * slots, :] = (b[n1] + a[n2]).astype(jnp.bfloat16)
        lead3 = chirped_rows(lead, chirp_ref)
        u = nt_dot(table_re, lead3)
        v = nt_dot(table_im, lead3)
        left[owner, 0] = u[:, n0]
        left[owner, 1] = v[:, n0]
        left[owner, 2] = u[:, n1] - v[:, n2]
        left[owner, 3] = u[:, n2] + v[:, n1]

    prepare(t, trail_ref[...], lead_ref[...])
    got[z] = contrib_ref[z]
    for copy in taper_copies:
        copy.wait()
    prepare(partner, tapers[partner, 0], tapers[partner, 1])
    for copy in copies:
        copy.wait()
    if width == 2 * SG:
        whole = got[...].reshape(subgrids * groups * rows, width)
    else:
        for f in range(subgrids * groups):
            i, j = f // FGRID, f % FGRID
            lines[i * rows : (i + 1) * rows, j * 2 * MC : (j + 1) * 2 * MC] = got[
                f // groups, f % groups
            ]
        whole = lines[...]
    for o in range(owners):
        spread = nt_dot(whole, right[o])
        for w in range(NW):
            g_re = spread[:, w * slots : (w + 1) * slots]
            g_im = spread[:, (NW + w) * slots : (NW + w + 1) * slots]
            l_re, l_im = left[o, 2 * w], left[o, 2 * w + 1]
            part_out[o, 2 * w : 2 * w + 1, :] = jnp.sum(l_re * g_re - l_im * g_im, axis=0, keepdims=True)
            part_out[o, 2 * w + 1 : 2 * w + 2, :] = jnp.sum(
                l_re * g_im + l_im * g_re, axis=0, keepdims=True
            )
        part_out[o, 2 * NW :, :] = jnp.zeros((8 - 2 * NW, slots), jnp.float32)

    part_copies = []
    for d in range(1, plane_total):
        other, peer = plane_peer(d)
        part_copies.append(
            remote(
                part_out.at[lax.rem(other, owners)],
                part_in.at[plane],
                part_send.at[d],
                part_recv.at[d],
                peer,
            )
        )
    for copy in part_copies:
        copy.start()
    part_in[plane] = part_out[t]
    observed_in[p] = observed_out[...]
    for copy in observed_copies:
        copy.wait()
    observed = observed_in[0]
    for q in range(1, pols):
        observed = observed + observed_in[q]
    depth = depth_ref[...].astype(jnp.float32)
    for copy in part_copies:
        copy.wait()

    pred = []
    per_pol = part_in.shape[0] // NPOL
    for q in range(NPOL):
        block = part_in[q * per_pol]
        for o in range(1, per_pol):
            block = block + part_in[q * per_pol + o]
        pred.append(
            tuple(
                sum(depth[w : w + 1] * block[2 * w + c : 2 * w + c + 1] for w in range(NW))
                for c in range(2)
            )
        )
    gains = gains_ref[...]
    idents = idents_ref[...]
    residual, leading, trailing = model_terms(
        pred,
        [observed[k : k + 1] for k in range(2 * NPOL)],
        [gains[k : k + 1] for k in range(4)],
        [gains[4 + k : 5 + k] for k in range(4)],
        idents[3:4],
    )
    for k in range(3):
        record_out[k : k + 1, :] = idents[k : k + 1]
    for k in range(4):
        record_out[3 + k : 4 + k, :] = leading[k]
        record_out[7 + k : 8 + k, :] = trailing[k]
    record_out[11:, :] = jnp.zeros((5, slots), jnp.float32)
    record_copies = []
    for d in range(1, across_total):
        other, peer = across_peer(d)
        record_copies.append(
            remote(record_out, record_in.at[across], record_send.at[d], record_recv.at[d], peer)
        )
    for copy in record_copies:
        copy.start()
    record_in[across] = record_out[...]
    rest = jnp.concatenate(residual, axis=0)
    own_rest = jnp.zeros((2 * NPOL, quarter), jnp.float32)
    for q in range(pols):
        own_rest = jnp.where(p == q, rest[:, q * quarter : (q + 1) * quarter], own_rest)
    residual_ref[...] = own_rest
    for copy in record_copies:
        copy.wait()

    piece = jnp.concatenate([record_in[d] for d in range(across_total)], axis=1)
    own_count = grad_ref.shape[1]
    index = (z * pols + p) * owners + t
    mine = (index * own_count + lax.broadcasted_iota(jnp.int32, (own_count, 1), 0)).astype(
        jnp.float32
    )
    match_first = mine == piece[0:1]
    match_second = mine == piece[1:2]
    weighted = jnp.concatenate(
        [
            jnp.where(match_first, piece[3 + k : 4 + k], 0.0)
            + jnp.where(match_second, piece[7 + k : 8 + k], 0.0)
            for k in range(4)
        ],
        axis=0,
    )
    high = weighted.astype(jnp.bfloat16)
    low = (weighted - high.astype(jnp.float32)).astype(jnp.bfloat16)
    channel_ids = lax.broadcasted_iota(jnp.int32, (NCH, 1), 0).astype(jnp.float32)
    onehot = jnp.where(channel_ids == piece[2:3], 1.0, 0.0).astype(jnp.bfloat16)
    summed = nt_dot(high, onehot) + nt_dot(low, onehot)
    for k in range(4):
        grad_ref[k] = grad_scale * summed[k * own_count : (k + 1) * own_count]


def predict(sizes, own_count, *operands):
    subgrids, pols, owners = sizes
    contrib, lead = operands[0], operands[1]
    _, groups, rows, width = contrib.shape
    slots = lead.shape[0]
    vmem = pl.BlockSpec(memory_space=pltpu.VMEM)
    dma = lambda n: pltpu.SemaphoreType.DMA((n,))
    across_total, plane_total = subgrids * owners, pols * owners
    return pl.pallas_call(
        functools.partial(predict_kernel, sizes),
        out_shape=(
            jax.ShapeDtypeStruct((2 * NPOL, slots // pols), jnp.float32),
            jax.ShapeDtypeStruct((4, own_count, NCH), jnp.float32),
        ),
        in_specs=[vmem] * len(operands),
        out_specs=(vmem, vmem),
        scratch_shapes=[
            pltpu.VMEM(contrib.shape, jnp.bfloat16),
            pltpu.VMEM((FGRID * rows, 2 * SG), jnp.bfloat16),
            pltpu.VMEM((owners, 2, slots, SG), jnp.bfloat16),
            pltpu.VMEM((owners, 2 * NW * slots, 2 * SG), jnp.bfloat16),
            pltpu.VMEM((owners, 4, FGRID * rows, slots), jnp.float32),
            pltpu.VMEM((owners, 8, slots), jnp.float32),
            pltpu.VMEM((plane_total, 8, slots), jnp.float32),
            pltpu.VMEM((8, slots), jnp.float32),
            pltpu.VMEM((pols, 8, slots), jnp.float32),
            pltpu.VMEM((16, slots), jnp.float32),
            pltpu.VMEM((across_total, 16, slots), jnp.float32),
            dma(subgrids),
            dma(subgrids),
            dma(2),
            dma(2),
            dma(pols),
            dma(pols),
            dma(plane_total),
            dma(plane_total),
            dma(across_total),
            dma(across_total),
        ],
        compiler_params=pltpu.CompilerParams(
            collective_id=0, has_side_effects=True, vmem_limit_bytes=48 << 20
        ),
    )(*operands)


def folded_factors(subgrids):
    half = lambda odd, s, c: [s * 2 * MC + c * MC + k for k in range(odd, MC, 2)]
    order = []
    for odd in range(2):
        for first in range(0, subgrids, 2):
            for c in range(2):
                for s in ((first + 1, first) if odd else (first, first + 1)):
                    order += half(odd, s, c)
    p, q, cosine, sine = [t[:, order] for t in fourier_factors(subgrids)]
    return p[: len(p) // 2], q[: len(q) // 2], cosine, sine


def folded_second(second):
    split = second.reshape(SG, 2 * FGRID, MC // 2, 2)
    return np.concatenate([split[..., 0], split[..., 1]], axis=2).reshape(SG, 2 * SG)


def gather_lookups(block_ref, links_ref, gain_ref, gains_ref, idents_ref):
    blocks = block_ref.shape[2]
    slots = idents_ref.shape[1]
    span = slots + 128
    lane = lax.broadcasted_iota(jnp.int32, (1, slots), 1)
    place = lax.broadcasted_iota(jnp.int32, (span, slots), 0)
    lane_tall = lax.broadcasted_iota(jnp.int32, (span, slots), 1)
    begin = jnp.int32(0)
    member, picks, windows, tables = [], [], [], []
    channel = jnp.zeros((1, slots), jnp.float32)
    alive = jnp.zeros((1, slots), jnp.float32)
    for b in range(blocks):
        chosen, offset, amount = [block_ref[k, 0, b] for k in range(3)]
        row = jnp.minimum(lax.div(offset, 128), links_ref.shape[0] - span // 128)
        first = row * 128
        windows += [links_ref[row + k] for k in range(span // 128)]
        tables.append(gain_ref[chosen])
        inside = jnp.where((lane >= begin) & (lane < begin + amount), 1.0, 0.0)
        member.append(inside)
        alive += inside
        channel += inside * chosen.astype(jnp.float32)
        hit = place == lane_tall + (offset - first - begin)
        picks.append((jnp.where(hit, 1.0, 0.0) * inside).astype(jnp.bfloat16))
        begin = begin + amount
    links = jnp.concatenate(windows, axis=1)
    upper = links // 16
    lower = links - 16 * upper
    pieces = jnp.concatenate([upper, lower], axis=0).astype(jnp.float32).astype(jnp.bfloat16)
    found = jnp.dot(
        pieces, jnp.concatenate(picks, axis=0), preferred_element_type=jnp.float32
    )
    stations = 16.0 * found[0:2] + found[2:4]
    table = jnp.concatenate(tables, axis=0)
    high = table.astype(jnp.bfloat16)
    rest = table - high.astype(jnp.float32)
    middle = rest.astype(jnp.bfloat16)
    low = (rest - middle.astype(jnp.float32)).astype(jnp.bfloat16)
    split = jnp.concatenate([high, middle, low], axis=0)
    size = table.shape[0]
    names = lax.broadcasted_iota(jnp.int32, (table.shape[1], 1), 0).astype(jnp.float32)
    for side in range(2):
        pick = jnp.where(names == stations[side : side + 1], 1.0, 0.0).astype(jnp.bfloat16)
        three = jnp.dot(split, pick, preferred_element_type=jnp.float32)
        rows = three[:size] + three[size : 2 * size] + three[2 * size :]
        chosen = member[0] * rows[0:4]
        for b in range(1, blocks):
            chosen = chosen + member[b] * rows[4 * b : 4 * b + 4]
        gains_ref[4 * side : 4 * side + 4, :] = chosen
    idents_ref[0:2, :] = stations
    idents_ref[2:3, :] = channel
    idents_ref[3:4, :] = alive
    idents_ref[4:8, :] = jnp.zeros((4, slots), jnp.float32)


def fused_kernel(
    sizes,
    block_hbm,
    links_hbm,
    gain_hbm,
    p_hbm,
    q_hbm,
    c_hbm,
    s_hbm,
    x_hbm,
    lead_hbm,
    trail_hbm,
    depth_hbm,
    observed_hbm,
    table_re_hbm,
    table_im_hbm,
    second_hbm,
    chirp_hbm,
    residual_ref,
    grad_ref,
    block_ref,
    links_ref,
    gain_ref,
    p_ref,
    q_ref,
    c_ref,
    s_ref,
    x_ref,
    tapers,
    depths,
    observed_ref,
    table_ref,
    second_ref,
    chirp_ref,
    factors,
    contrib,
    got,
    right,
    left,
    gains_ref,
    idents_ref,
    side,
    part_out,
    part_in,
    observed_out,
    observed_in,
    rests,
    load_sem,
    chunk_sem,
    pair_send,
    pair_recv,
    chip_send,
    chip_recv,
    relay_send,
    relay_recv,
    far_send,
    far_recv,
    near_send,
    near_recv,
    observed_send,
    observed_recv,
    side_send,
    side_recv,
    part_send,
    part_recv,
):
    subgrids, pols, owners = sizes
    z, p, t = lax.axis_index("facet"), lax.axis_index("pol"), lax.axis_index("tm")
    _, _, slots, _ = tapers.shape
    facets, _, rows, length = x_ref.shape
    _, _, groups, _, width = contrib.shape
    side_z, own = lax.rem(z, 2), z // 2
    far = 1 - own
    pair_z = z + 1 - 2 * side_z
    far_z = z + 2 - 4 * own
    partner = lax.rem(t + 1, owners)
    mesh_id = pl.DeviceIdType.MESH

    def remote(src, dst, send, recv, peer):
        return pltpu.make_async_remote_copy(
            src_ref=src,
            dst_ref=dst,
            send_sem=send,
            recv_sem=recv,
            device_id=peer,
            device_id_type=mesh_id,
        )

    across_total = subgrids * owners
    across = z * owners + t

    def across_peer(d):
        other = lax.rem(across + d, across_total)
        return other, (other // owners, p, lax.rem(other, owners))

    barrier = pltpu.get_barrier_semaphore()
    for d in range(1, across_total):
        pl.semaphore_signal(barrier, inc=1, device_id=across_peer(d)[1], device_id_type=mesh_id)
    for d in range(1, pols):
        q = lax.rem(p + d, pols)
        for o in range(owners):
            pl.semaphore_signal(barrier, inc=1, device_id=(z, q, o), device_id_type=mesh_id)

    offsets = [
        (dz, dp, dt)
        for dz in sorted(range(subgrids), key=lambda d: -min(d, subgrids - d))
        for dp in reversed(range(pols))
        for dt in range(owners)
    ]
    offsets.remove((0, 0, 0))
    per_chunk = FGRID // PIECES
    chunks = facets // per_chunk
    x_loads = [
        pltpu.make_async_copy(
            x_hbm.at[pl.ds(c * per_chunk, per_chunk)],
            x_ref.at[pl.ds(c * per_chunk, per_chunk)],
            chunk_sem.at[c],
        )
        for c in range(chunks)
    ]
    pairs = [
        (c_hbm, c_ref),
        (s_hbm, s_ref),
        (p_hbm, p_ref),
        (q_hbm, q_ref),
        (trail_hbm, tapers.at[own, 0]),
        (lead_hbm, tapers.at[own, 1]),
        (depth_hbm, depths.at[own]),
        (observed_hbm, observed_ref),
        (chirp_hbm, chirp_ref),
        (second_hbm, second_ref),
        (table_re_hbm.at[pl.ds(own * 2 * groups, 2 * groups)], table_ref.at[0]),
        (table_im_hbm.at[pl.ds(own * 2 * groups, 2 * groups)], table_ref.at[1]),
        (block_hbm, block_ref),
        (links_hbm, links_ref),
        (gain_hbm, gain_ref),
    ]
    loads = [
        pltpu.make_async_copy(src, dst, load_sem.at[k]) for k, (src, dst) in enumerate(pairs)
    ]
    for copy in loads[:4]:
        copy.start()
    x_loads[0].start()
    for copy in loads[4:9]:
        copy.start()
    for copy in x_loads[1:]:
        copy.start()
    for copy in loads[9:]:
        copy.start()

    for copy in loads[:4]:
        copy.wait()
    spread = c_ref.shape[0]
    cosine, sine = c_ref[...], s_ref[...]
    half = length // 2
    for part in range(half // spread):
        factors[part * spread : (part + 1) * spread, :] = (
            p_ref[part : part + 1, :] * cosine + q_ref[part : part + 1, :] * sine
        ).astype(jnp.bfloat16)

    for copy in loads[4:9]:
        copy.wait()
    quarter = observed_ref.shape[1]
    place = lax.broadcasted_iota(jnp.int32, (2 * NPOL, slots), 1)
    observed_out[...] = jnp.where(
        (place >= p * quarter) & (place < (p + 1) * quarter),
        jnp.concatenate([observed_ref[...]] * pols, axis=1),
        0.0,
    )
    pl.semaphore_wait(barrier, across_total - 1 + (pols - 1) * owners)
    share = lambda q: pl.ds(pl.multiple_of(q * quarter, quarter), quarter)
    far_copies = [
        remote(
            tapers.at[own, side, share(p)],
            tapers.at[own, side, share(p)],
            far_send.at[side],
            far_recv.at[side],
            (far_z, p, t),
        )
        for side in range(2)
    ]
    far_copies.append(
        remote(depths.at[own], depths.at[own], far_send.at[2], far_recv.at[2], (far_z, p, t))
    )
    observed_copies = []
    for d in range(1, pols):
        q = lax.rem(p + d, pols)
        observed_copies.append(
            remote(
                observed_out, observed_in.at[p], observed_send.at[d], observed_recv.at[d], (z, q, t)
            )
        )
    for copy in far_copies + observed_copies:
        copy.start()
    others = pols - 1
    near_copies = [
        remote(
            tapers.at[far, side, share(p)],
            tapers.at[far, side, share(p)],
            near_send.at[others * side + d - 1],
            near_recv.at[others * side + d - 1],
            (z, lax.rem(p + d, pols), t),
        )
        for side in range(2)
        for d in (2, 1, 3)
    ]

    def forward(side):
        far_copies[side].wait_recv()
        for copy in near_copies[others * side : others * side + others]:
            copy.start()


    lane = lax.broadcasted_iota(jnp.int32, (rows, 2 * MC), 1)
    sign = jnp.where(lane < MC, -1.0, 1.0)
    front = lane % MC < MC // 2
    folded = factors.shape[1] // 2
    part_width = width // PIECES
    pair_copies, chip_copies, relay_copies = [], [], []
    for c in range(chunks):
        x_loads[c].wait()
        x = x_ref[c * per_chunk : (c + 1) * per_chunk].reshape(per_chunk * 2 * rows, length)
        totals = [
            jnp.dot(
                x[:, :half] + x[:, half:], factors[:, :folded], preferred_element_type=jnp.float32
            ),
            jnp.dot(
                x[:, :half] - x[:, half:], factors[:, folded:], preferred_element_type=jnp.float32
            ),
        ]
        group, piece = c // PIECES, c % PIECES
        for pair in range(subgrids // 2):
            cut = slice(pair * 2 * MC, (pair + 1) * 2 * MC)
            for f in range(per_chunk):
                even, odd = [
                    total[2 * f * rows : (2 * f + 1) * rows, cut]
                    + sign
                    * pltpu.roll(total[(2 * f + 1) * rows : (2 * f + 2) * rows, cut], MC, 1)
                    for total in totals
                ]
                place = slice(
                    (piece * per_chunk + f) * 2 * MC, (piece * per_chunk + f + 1) * 2 * MC
                )
                contrib[0, pair, group, :, place] = jnp.where(front, even, odd).astype(jnp.bfloat16)
                other = jnp.where(front, odd, even)
                other = jnp.where(
                    front,
                    pltpu.roll(other, 2 * MC - MC // 2, 1),
                    pltpu.roll(other, MC // 2, 1),
                )
                contrib[1, pair, group, :, place] = other.astype(jnp.bfloat16)
        lanes = pl.ds(piece * part_width, part_width)
        pair_copies.append(
            remote(
                contrib.at[1 - side_z, :, group, :, lanes],
                got.at[:, side_z, group, t, :, lanes],
                pair_send.at[c],
                pair_recv.at[c],
                (pair_z, p, t),
            )
        )
        chip_copies.append(
            remote(
                contrib.at[side_z, :, group, :, lanes],
                got.at[:, side_z, group, t, :, lanes],
                chip_send.at[c],
                chip_recv.at[c],
                (z, p, partner),
            )
        )
        relay_copies.append(
            remote(
                got.at[:, 1 - side_z, group, t, :, lanes],
                got.at[:, 1 - side_z, group, t, :, lanes],
                relay_send.at[c],
                relay_recv.at[c],
                (z, p, partner),
            )
        )
        pair_copies[c].start()
        chip_copies[c].start()
        if c == chunks - FORWARD:
            forward(0)

    for k in range(2):
        for group in range(groups):
            got[k, side_z, group, t] = contrib[side_z, k, group]
    for copy in loads[9:]:
        copy.wait()
    gather_lookups(block_ref, links_ref, gain_ref, gains_ref, idents_ref)
    observed_in[p] = observed_out[...]
    for copy in observed_copies:
        copy.wait()
    observed = observed_in[0]
    for q in range(1, pols):
        observed = observed + observed_in[q]
    side[across, 0:8] = gains_ref[...]
    side[across, 8:16] = observed
    side[across, 16:20] = idents_ref[0:4]
    side_copies = []
    for d in range(1, across_total):
        other, peer = across_peer(d)
        side_copies.append(
            remote(side.at[across], side.at[across], side_send.at[d], side_recv.at[d], peer)
        )
    for copy in side_copies:
        copy.start()
    forward(1)

    span = 2 * groups * owners * rows
    table_re = table_ref[0].reshape(span, SG)
    table_im = table_ref[1].reshape(span, SG)
    turn = jnp.where(
        lax.broadcasted_iota(jnp.int32, (3 * slots, 2 * MC), 1) < MC, -1.0, 1.0
    )

    def prepare_right(k):
        trail3 = chirped_rows(tapers[k, 0], chirp_ref)
        a = jnp.dot(trail3, second_ref[...], preferred_element_type=jnp.float32)
        b = jnp.concatenate(
            [
                turn * pltpu.roll(a[:, j * 2 * MC : (j + 1) * 2 * MC], MC, 1)
                for j in range(a.shape[1] // (2 * MC))
            ],
            axis=1,
        )
        n0, n1, n2 = slice(0, slots), slice(slots, 2 * slots), slice(2 * slots, 3 * slots)
        right[k, 0:slots, :] = a[n0].astype(jnp.bfloat16)
        right[k, slots : 2 * slots, :] = (a[n1] - b[n2]).astype(jnp.bfloat16)
        right[k, 2 * slots : 3 * slots, :] = b[n0].astype(jnp.bfloat16)
        right[k, 3 * slots : 4 * slots, :] = (b[n1] + a[n2]).astype(jnp.bfloat16)

    def prepare_left(k):
        n0, n1, n2 = slice(0, slots), slice(slots, 2 * slots), slice(2 * slots, 3 * slots)
        lead3 = chirped_rows(tapers[k, 1], chirp_ref)
        u = nt_dot(table_re, lead3)
        v = nt_dot(table_im, lead3)
        left[k, 0] = u[:, n0]
        left[k, 1] = v[:, n0]
        left[k, 2] = u[:, n1] - v[:, n2]
        left[k, 3] = u[:, n2] + v[:, n1]

    prepare_right(own)
    prepare_left(own)
    for pair, relay in zip(pair_copies[:-1], relay_copies[:-1]):
        pair.wait_recv()
        relay.start()
    for copy in near_copies[:others]:
        copy.wait_recv()
    prepare_right(far)
    pair_copies[-1].wait_recv()
    relay_copies[-1].start()
    for copy in [far_copies[2]] + near_copies[others:]:
        copy.wait_recv()
    prepare_left(far)
    for copy in chip_copies + relay_copies:
        copy.wait()
    for k in range(2):
        spread_v = nt_dot(got[k].reshape(span, width), right[k])
        weights = depths[k].astype(jnp.float32)
        sums = [0.0, 0.0]
        for w in range(NW):
            g_re = spread_v[:, w * slots : (w + 1) * slots]
            g_im = spread_v[:, (NW + w) * slots : (NW + w + 1) * slots]
            l_re, l_im = left[k, 2 * w], left[k, 2 * w + 1]
            weight = weights[w : w + 1]
            sums[0] += weight * jnp.sum(l_re * g_re - l_im * g_im, axis=0, keepdims=True)
            sums[1] += weight * jnp.sum(l_re * g_im + l_im * g_re, axis=0, keepdims=True)
        for c in range(2):
            part_out[2 * c + k : 2 * c + k + 1, :] = sums[c]

    part_copies = []
    for dz, dp, dt in offsets:
        peer = (lax.rem(z + dz, subgrids), lax.rem(p + dp, pols), lax.rem(t + dt, owners))
        k = (dz * pols + dp) * owners + dt
        part_copies.append(
            remote(part_out, part_in.at[z, p, t], part_send.at[k], part_recv.at[k], peer)
        )
    for copy in part_copies:
        copy.start()
    part_in[z, p, t] = part_out[...]
    for copy in pair_copies + far_copies + near_copies:
        copy.wait_send()
    for copy in side_copies:
        copy.wait()

    own_count = grad_ref.shape[0]
    index = (z * pols + p) * owners + t
    mine = (index * own_count + lax.broadcasted_iota(jnp.int32, (own_count, 1), 0)).astype(
        jnp.float32
    )
    channel_ids = lax.broadcasted_iota(jnp.int32, (NCH, 1), 0).astype(jnp.float32)
    first_here = [jnp.where(mine == side[d, 16:17], 1.0, 0.0) for d in range(across_total)]
    second_here = [jnp.where(mine == side[d, 17:18], 1.0, 0.0) for d in range(across_total)]
    onehot = jnp.concatenate(
        [
            jnp.where(channel_ids == side[d, 18:19], 1.0, 0.0).astype(jnp.bfloat16)
            for d in range(across_total)
        ],
        axis=1,
    )
    column = lambda k: jnp.concatenate([side[d, k : k + 1] for d in range(across_total)], axis=0)
    gains = [column(k) for k in range(8)]
    observed = [column(8 + k) for k in range(8)]
    alive = column(19)
    for copy in part_copies:
        copy.wait()

    pred = []
    for q in range(NPOL):
        both = [[part_in[y, q, o] + part_in[y + 2, q, o] for o in range(owners)] for y in range(2)]
        pred.append(
            tuple(
                jnp.concatenate(
                    [
                        both[s % 2][o][2 * c + s // 2 : 2 * c + s // 2 + 1]
                        for s in range(subgrids)
                        for o in range(owners)
                    ],
                    axis=0,
                )
                for c in range(2)
            )
        )
    residual, leading, trailing = model_terms(pred, observed, gains[:4], gains[4:], alive)
    for k in range(2 * NPOL):
        rests[:, k : k + 1, :] = residual[k][:, None, :]
    rest = rests[across]
    own_rest = jnp.zeros((2 * NPOL, quarter), jnp.float32)
    for q in range(pols):
        own_rest = jnp.where(p == q, rest[:, q * quarter : (q + 1) * quarter], own_rest)
    residual_ref[...] = own_rest

    weighted = jnp.concatenate(
        [
            jnp.concatenate(
                [
                    first_here[d] * leading[k][d : d + 1]
                    + second_here[d] * trailing[k][d : d + 1]
                    for d in range(across_total)
                ],
                axis=1,
            )
            for k in range(4)
        ],
        axis=0,
    )
    high = weighted.astype(jnp.bfloat16)
    low = (weighted - high.astype(jnp.float32)).astype(jnp.bfloat16)
    summed = nt_dot(jnp.concatenate([high, low], axis=0), onehot)
    summed = summed[: high.shape[0]] + summed[high.shape[0] :]
    lane_group = lax.broadcasted_iota(jnp.int32, (own_count, 128), 1) // 32
    mixed = []
    for g in range(NCH // 32):
        base = g // 4 * 128
        built = None
        for k in range(4):
            block = summed[k * own_count : (k + 1) * own_count, base : base + 128]
            shift = 32 * (k - g % 4) % 128
            block = pltpu.roll(block, shift, 1) if shift else block
            built = block if built is None else jnp.where(lane_group == k, block, built)
        mixed.append(grad_scale * built)
    mixed = jnp.concatenate(mixed, axis=0)
    high = mixed.astype(jnp.bfloat16)
    low = (mixed - high.astype(jnp.float32)).astype(jnp.bfloat16)
    came = lax.broadcasted_iota(jnp.int32, (128, 128), 0)
    goes = lax.broadcasted_iota(jnp.int32, (128, 128), 1)
    order = jnp.where(goes == came % 32 * 4 + came // 32, 1.0, 0.0).astype(jnp.bfloat16)
    placed = jnp.dot(
        jnp.concatenate([high, low], axis=0), order, preferred_element_type=jnp.float32
    )
    placed = placed[: mixed.shape[0]] + placed[mixed.shape[0] :]
    for g in range(NCH // 32):
        grad_ref[:, g * 128 : (g + 1) * 128] = placed[g * own_count : (g + 1) * own_count]


def emit_kernel(residual_ref, grad_ref, residual_out, grad_out, sems):
    copies = [
        pltpu.make_async_copy(residual_ref, residual_out, sems.at[0]),
        pltpu.make_async_copy(grad_ref, grad_out, sems.at[1]),
    ]
    for copy in copies:
        copy.start()
    for copy in copies:
        copy.wait()


def fused(sizes, own_count, *operands):
    subgrids, pols, owners = sizes
    block_table, links, gains = operands[0:3]
    x, lead, trail, depth, observed = operands[7:12]
    facets, _, rows, length = x.shape
    slots = lead.shape[0]
    width = subgrids * 2 * MC
    spread = FS // MC
    groups = facets // FGRID
    chunks = facets // (FGRID // PIECES)
    hbm = pl.BlockSpec(memory_space=pltpu.HBM)
    vmem = pl.BlockSpec(memory_space=pltpu.VMEM)
    dma = lambda n: pltpu.SemaphoreType.DMA((n,))
    held = lambda a: pltpu.VMEM(a.shape, a.dtype)
    across_total, all_total = subgrids * owners, subgrids * pols * owners
    f32, bf16 = jnp.float32, jnp.bfloat16
    residual, grad = pl.pallas_call(
        functools.partial(fused_kernel, sizes),
        out_shape=(
            jax.ShapeDtypeStruct(observed.shape, f32),
            jax.ShapeDtypeStruct((own_count, 4 * NCH), f32),
        ),
        in_specs=[hbm] * len(operands),
        out_specs=(vmem, vmem),
        scratch_shapes=[
            pltpu.SMEM(block_table.shape, jnp.int32),
            held(links),
            held(gains),
            pltpu.VMEM((length // 2 // spread, width), f32),
            pltpu.VMEM((length // 2 // spread, width), f32),
            pltpu.VMEM((spread, width), f32),
            pltpu.VMEM((spread, width), f32),
            held(x),
            pltpu.VMEM((2, 2, slots, SG), bf16),
            pltpu.VMEM((2,) + depth.shape, bf16),
            held(observed),
            pltpu.VMEM((2, 2 * groups, owners, rows, SG), bf16),
            pltpu.VMEM((SG, 2 * SG), bf16),
            pltpu.VMEM((2, SG), f32),
            pltpu.VMEM((length // 2, width), bf16),
            pltpu.VMEM((2, 2, groups, rows, 2 * SG), bf16),
            pltpu.VMEM((2, 2, groups, owners, rows, 2 * SG), bf16),
            pltpu.VMEM((2, 2 * NW * slots, 2 * SG), bf16),
            pltpu.VMEM((2, 4, 2 * groups * owners * rows, slots), f32),
            pltpu.VMEM((8, slots), f32),
            pltpu.VMEM((8, slots), f32),
            pltpu.VMEM((across_total, 20, slots), f32),
            pltpu.VMEM((4, slots), f32),
            pltpu.VMEM((subgrids, pols, owners, 4, slots), f32),
            pltpu.VMEM((8, slots), f32),
            pltpu.VMEM((pols, 8, slots), f32),
            pltpu.VMEM((across_total, 8, slots), f32),
            dma(15),
            dma(chunks),
            dma(chunks),
            dma(chunks),
            dma(chunks),
            dma(chunks),
            dma(chunks),
            dma(chunks),
            dma(3),
            dma(3),
            dma(2 * pols - 2),
            dma(2 * pols - 2),
            dma(pols),
            dma(pols),
            dma(across_total),
            dma(across_total),
            dma(all_total),
            dma(all_total),
        ],
        compiler_params=pltpu.CompilerParams(
            collective_id=0, has_side_effects=True, vmem_limit_bytes=36 << 20
        ),
    )(*[pltpu.with_memory_space_constraint(a, pltpu.HBM) for a in operands])
    return pl.pallas_call(
        emit_kernel,
        out_shape=(
            jax.ShapeDtypeStruct(residual.shape, f32),
            jax.ShapeDtypeStruct(grad.shape, f32),
        ),
        in_specs=[vmem] * 2,
        out_specs=[hbm] * 2,
        scratch_shapes=[dma(2)],
        compiler_params=pltpu.CompilerParams(vmem_limit_bytes=1 << 20),
    )(residual, grad)


def on_device(
    tile_spectral_lines,
    taper_leading_axis,
    taper_trailing_axis,
    depth_layer_factors,
    measured_correlations,
    visibility_groups_table,
    antenna_links,
    complex_receiver_factors,
):
    sizes = tuple(lax.axis_size(name) for name in ("facet", "pol", "tm"))
    subgrids, pols, owners = sizes
    slots = taper_leading_axis.shape[2]
    quarter = measured_correlations.shape[3]
    rows = tile_spectral_lines.shape[3]

    block_table = visibility_groups_table.reshape(3, visibility_groups_table.shape[3])
    observed = measured_correlations.reshape(2 * NPOL, quarter)

    if tile_spectral_lines.shape[0] % FGRID == 0 and sizes == (4, NPOL, 2):
        table_re, table_im = [jnp.asarray(t) for t in subgrid_tables()[:2]]
        own_count = NST // (subgrids * pols * owners)
        residual, gain_grad = fused(
            sizes,
            own_count,
            visibility_groups_table.reshape(3, 1, visibility_groups_table.shape[3]),
            jnp.transpose(antenna_links.reshape(2, -1, 128), (1, 0, 2)),
            complex_receiver_factors,
            *[jnp.asarray(t) for t in folded_factors(subgrids)],
            tile_spectral_lines[:, 0],
            taper_leading_axis.reshape(slots, SG),
            taper_trailing_axis.reshape(slots, SG),
            depth_layer_factors.reshape(NW, slots),
            observed,
            table_re.reshape(FGRID, owners, rows, SG),
            table_im.reshape(FGRID, owners, rows, SG),
            jnp.asarray(folded_second(subgrid_tables()[2])),
            jnp.asarray(np.stack(chirp_line())),
        )
        return residual.reshape(1, 2 * NPOL, 1, quarter), gain_grad

    contrib, gains, idents = fourier(
        tile_spectral_lines[:, 0],
        subgrids,
        slots,
        block_table,
        antenna_links,
        complex_receiver_factors,
    )
    table_re, table_im, second = [jnp.asarray(t) for t in subgrid_tables()]
    cosine, sine = chirp_line()
    own_count = NST // (subgrids * pols * owners)
    residual, grad = predict(
        sizes,
        own_count,
        contrib,
        taper_leading_axis.reshape(slots, SG),
        taper_trailing_axis.reshape(slots, SG),
        depth_layer_factors.reshape(NW, slots),
        observed,
        gains,
        idents,
        table_re.reshape(FGRID, owners, rows, SG),
        table_im.reshape(FGRID, owners, rows, SG),
        second,
        jnp.asarray(np.stack([cosine, sine])),
    )
    gain_grad = jnp.transpose(grad, (1, 2, 0)).reshape(own_count, 4 * NCH)
    return residual.reshape(1, 2 * NPOL, 1, quarter), gain_grad


def solution(mesh):
    return jax.shard_map(
        on_device,
        mesh=mesh,
        in_specs=(
            P("facet", "pol", None, "tm", None),
            P("facet", "tm", None, None),
            P("facet", "tm", None, None),
            P("facet", "tm", None, None),
            P("facet", None, "tm", "pol"),
            P("facet", "tm", None, None),
            P(),
            P(),
        ),
        out_specs=(P("facet", None, "tm", "pol"), P(("facet", "pol", "tm"), None)),
        check_vma=False,
    )
```

```python
import functools
import math

import jax
import jax.numpy as jnp
import numpy as np
from jax import lax
from jax.experimental import pallas as pl
from jax.experimental.pallas import tpu as pltpu
from jax.sharding import PartitionSpec as P

FGRID = 8
FS = 4096
MC = 64
SG = 512
NPOL = 4
NW = 2
NCH = 256
NST = 512
CHUNK = 1024
PIECES = 2
FORWARD = 2

w_chirp = 0.37
grad_scale = 0.1


def unit_angles(left, right, length):
    product = np.outer(np.arange(left), np.arange(right)) % length
    return 2.0 * math.pi * product / length


def fourier_factors(subgrids):
    spread = FS // MC
    alpha = unit_angles(FS // spread, MC, MC)
    p = np.concatenate([np.cos(alpha), -np.sin(alpha)], axis=1) / math.sqrt(FS)
    q = np.concatenate([-np.sin(alpha), -np.cos(alpha)], axis=1) / math.sqrt(FS)
    beta = unit_angles(spread, subgrids * MC, FS).reshape(spread, subgrids, 1, MC)
    beta = np.broadcast_to(beta, (spread, subgrids, 2, MC)).reshape(spread, subgrids * 2 * MC)
    tile = lambda t: np.tile(t, (1, subgrids)).astype(np.float32)
    return (
        tile(p),
        tile(q),
        np.cos(beta).astype(np.float32),
        np.sin(beta).astype(np.float32),
    )


def fetch_lookups(block_ref, links_ref, gain_ref, window, channel_gain, window_sem, gain_sem):
    blocks, _, span = window.shape
    copies = []
    for b in range(blocks):
        first = jnp.minimum(block_ref[1, b] // 128 * 128, links_ref.shape[1] - span)
        first = pl.multiple_of(first, 128)
        copies.append(
            pltpu.make_async_copy(
                links_ref.at[:, pl.ds(first, span)], window.at[b], window_sem.at[b]
            )
        )
        copies.append(
            pltpu.make_async_copy(
                gain_ref.at[block_ref[0, b]], channel_gain.at[b], gain_sem.at[b]
            )
        )
    return copies


def use_lookups(block_ref, links_ref, window, channel_gain, gains_ref, idents_ref):
    blocks, _, span = window.shape
    slots = idents_ref.shape[1]
    lane = lax.broadcasted_iota(jnp.int32, (1, slots), 1)
    place = lax.broadcasted_iota(jnp.int32, (span, slots), 0)
    lane_tall = lax.broadcasted_iota(jnp.int32, (span, slots), 1)
    begin = jnp.int32(0)
    member, picks = [], []
    channel = jnp.zeros((1, slots), jnp.float32)
    alive = jnp.zeros((1, slots), jnp.float32)
    for b in range(blocks):
        offset, amount = block_ref[1, b], block_ref[2, b]
        first = jnp.minimum(offset // 128 * 128, links_ref.shape[1] - span)
        inside = jnp.where((lane >= begin) & (lane < begin + amount), 1.0, 0.0)
        member.append(inside)
        alive += inside
        channel += inside * block_ref[0, b].astype(jnp.float32)
        hit = place == lane_tall + (offset - first - begin)
        picks.append((jnp.where(hit, 1.0, 0.0) * inside).astype(jnp.bfloat16))
        begin = begin + amount
    links = jnp.concatenate([window[b] for b in range(blocks)], axis=1)
    upper = links // 16
    lower = links - 16 * upper
    pieces = jnp.concatenate([upper, lower], axis=0).astype(jnp.float32).astype(jnp.bfloat16)
    found = jnp.dot(
        pieces, jnp.concatenate(picks, axis=0), preferred_element_type=jnp.float32
    )
    stations = 16.0 * found[0:2] + found[2:4]
    table = channel_gain[...].reshape(blocks * 4, channel_gain.shape[2])
    high = table.astype(jnp.bfloat16)
    rest = table - high.astype(jnp.float32)
    middle = rest.astype(jnp.bfloat16)
    low = (rest - middle.astype(jnp.float32)).astype(jnp.bfloat16)
    names = lax.broadcasted_iota(jnp.int32, (table.shape[1], 1), 0).astype(jnp.float32)
    for side in range(2):
        pick = jnp.where(names == stations[side : side + 1], 1.0, 0.0).astype(jnp.bfloat16)
        rows = (
            jnp.dot(high, pick, preferred_element_type=jnp.float32)
            + jnp.dot(middle, pick, preferred_element_type=jnp.float32)
            + jnp.dot(low, pick, preferred_element_type=jnp.float32)
        )
        chosen = member[0] * rows[0:4]
        for b in range(1, blocks):
            chosen = chosen + member[b] * rows[4 * b : 4 * b + 4]
        gains_ref[4 * side : 4 * side + 4, :] = chosen
    idents_ref[0:2, :] = stations
    idents_ref[2:3, :] = channel
    idents_ref[3:4, :] = alive
    idents_ref[4:8, :] = jnp.zeros((4, slots), jnp.float32)


def fourier_kernel(
    block_ref,
    links_ref,
    gain_ref,
    p_ref,
    q_ref,
    c_ref,
    s_ref,
    x_ref,
    o_ref,
    gains_ref,
    idents_ref,
    table,
    total,
    window,
    channel_gain,
    window_sem,
    gain_sem,
):
    step = pl.program_id(0)
    copies = fetch_lookups(
        block_ref, links_ref, gain_ref, window, channel_gain, window_sem, gain_sem
    )

    @pl.when(step == 0)
    def _():
        for copy in copies:
            copy.start()

    @pl.when(step == pl.num_programs(0) - 1)
    def _():
        for copy in copies:
            copy.wait()
        use_lookups(block_ref, links_ref, window, channel_gain, gains_ref, idents_ref)

    facets, _, rows, chunk = x_ref.shape
    subgrids = o_ref.shape[0]
    spread = c_ref.shape[0]
    cosine, sine = c_ref[...], s_ref[...]
    for part in range(chunk // spread):
        lead = p_ref[part : part + 1, :]
        other = q_ref[part : part + 1, :]
        table[part * spread : (part + 1) * spread, :] = (lead * cosine + other * sine).astype(
            jnp.bfloat16
        )
    x = x_ref[...].reshape(facets * 2 * rows, chunk)
    product = jnp.dot(x, table[...], preferred_element_type=jnp.float32)

    @pl.when(step == 0)
    def _():
        total[...] = product

    @pl.when(step > 0)
    def _():
        total[...] += product

    @pl.when(step == pl.num_programs(0) - 1)
    def _():
        lane = lax.broadcasted_iota(jnp.int32, (rows, 2 * MC), 1)
        sign = jnp.where(lane < MC, -1.0, 1.0)
        packed = o_ref.shape[3] // (2 * MC)
        for f in range(facets):
            for s in range(subgrids):
                cut = slice(s * 2 * MC, (s + 1) * 2 * MC)
                first = total[2 * f * rows : (2 * f + 1) * rows, cut]
                second = total[(2 * f + 1) * rows : (2 * f + 2) * rows, cut]
                value = first + sign * pltpu.roll(second, MC, 1)
                j = f % packed
                o_ref[s, f // packed, :, j * 2 * MC : (j + 1) * 2 * MC] = value.astype(jnp.bfloat16)


def fourier(x, subgrids, slots, block_table, links, station_gains):
    facets, _, rows, length = x.shape
    width = subgrids * 2 * MC
    spread = FS // MC
    packed = FGRID if facets % FGRID == 0 else 1
    per_step = CHUNK // spread
    blocks = block_table.shape[1]
    span = slots + 128
    in_place = lambda array: pltpu.with_memory_space_constraint(array, pltpu.HBM)
    factors = [in_place(jnp.asarray(t)) for t in fourier_factors(subgrids)]
    out = (subgrids, facets // packed, rows, packed * 2 * MC)
    return pl.pallas_call(
        fourier_kernel,
        out_shape=(
            jax.ShapeDtypeStruct(out, jnp.bfloat16),
            jax.ShapeDtypeStruct((8, slots), jnp.float32),
            jax.ShapeDtypeStruct((8, slots), jnp.float32),
        ),
        grid=(length // CHUNK,),
        in_specs=[
            pl.BlockSpec(memory_space=pltpu.SMEM),
            pl.BlockSpec(memory_space=pltpu.HBM),
            pl.BlockSpec(memory_space=pltpu.HBM),
            pl.BlockSpec((per_step, width), lambda g: (g, 0)),
            pl.BlockSpec((per_step, width), lambda g: (g, 0)),
            pl.BlockSpec((spread, width), lambda g: (0, 0)),
            pl.BlockSpec((spread, width), lambda g: (0, 0)),
            pl.BlockSpec((facets, 2, rows, CHUNK), lambda g: (0, 0, 0, g)),
        ],
        out_specs=(
            pl.BlockSpec(out, lambda g: (0, 0, 0, 0)),
            pl.BlockSpec((8, slots), lambda g: (0, 0)),
            pl.BlockSpec((8, slots), lambda g: (0, 0)),
        ),
        scratch_shapes=[
            pltpu.VMEM((CHUNK, width), jnp.bfloat16),
            pltpu.VMEM((facets * 2 * rows, width), jnp.float32),
            pltpu.VMEM((blocks, 2, span), jnp.int32),
            pltpu.VMEM((blocks, 4, NST), jnp.float32),
            pltpu.SemaphoreType.DMA((blocks,)),
            pltpu.SemaphoreType.DMA((blocks,)),
        ],
        compiler_params=pltpu.CompilerParams(
            dimension_semantics=("arbitrary",), vmem_limit_bytes=48 << 20
        ),
    )(
        block_table,
        in_place(links),
        in_place(station_gains),
        *factors,
        x,
    )


def subgrid_tables():
    angle = unit_angles(SG, SG, SG)
    re = np.cos(angle) / math.sqrt(SG)
    im = np.sin(angle) / math.sqrt(SG)
    blocks = lambda t: t.reshape(SG, FGRID, MC)
    second = np.stack([blocks(re), -blocks(im)], axis=2).reshape(SG, 2 * SG)
    return [t.astype(jnp.bfloat16) for t in (re, im, second)]


def chirp_line():
    offset = np.arange(SG) - SG // 2
    angle = 2.0 * math.pi * w_chirp * (offset * offset) / float(SG * SG)
    return np.cos(angle).astype(np.float32), np.sin(angle).astype(np.float32)


def model_terms(pred, observed, first, second, alive):
    residual, lead, trail = [], [], []
    for p in range(NPOL):
        f1, f2 = p // 2, p % 2
        pred_re, pred_im = pred[p]
        first_re, first_im = first[2 * f1], first[2 * f1 + 1]
        second_re, second_im = second[2 * f2], second[2 * f2 + 1]
        both_re = first_re * second_re + first_im * second_im
        both_im = first_im * second_re - first_re * second_im
        resid_re = alive * (observed[2 * p] - (both_re * pred_re - both_im * pred_im))
        resid_im = alive * (observed[2 * p + 1] - (both_re * pred_im + both_im * pred_re))
        cross_re = second_re * pred_re + second_im * pred_im
        cross_im = second_im * pred_re - second_re * pred_im
        along_re = first_re * pred_re - first_im * pred_im
        along_im = first_re * pred_im + first_im * pred_re
        residual += [resid_re, resid_im]
        lead.append(
            (-(resid_re * cross_re - resid_im * cross_im), -(resid_re * cross_im + resid_im * cross_re))
        )
        trail.append(
            (-(resid_re * along_re + resid_im * along_im), -(resid_re * along_im - resid_im * along_re))
        )
    leading = [lead[2 * f][r] + lead[2 * f + 1][r] for f in range(2) for r in range(2)]
    trailing = [trail[f][r] + trail[f + 2][r] for f in range(2) for r in range(2)]
    return residual, leading, trailing


def nt_dot(left, right, **kw):
    return lax.dot_general(
        left, right, (((1,), (1,)), ((), ())), preferred_element_type=jnp.float32, **kw
    )


def chirped_rows(taper, chirp_ref):
    wide = taper.astype(jnp.float32)
    return jnp.concatenate(
        [
            taper,
            (wide * chirp_ref[0:1, :]).astype(jnp.bfloat16),
            (wide * chirp_ref[1:2, :]).astype(jnp.bfloat16),
        ],
        axis=0,
    )


def predict_kernel(
    sizes,
    contrib_ref,
    lead_ref,
    trail_ref,
    depth_ref,
    observed_ref,
    gains_ref,
    idents_ref,
    table_re_ref,
    table_im_ref,
    second_ref,
    chirp_ref,
    residual_ref,
    grad_ref,
    got,
    lines,
    tapers,
    right,
    left,
    part_out,
    part_in,
    observed_out,
    observed_in,
    record_out,
    record_in,
    got_send,
    got_recv,
    taper_send,
    taper_recv,
    observed_send,
    observed_recv,
    part_send,
    part_recv,
    record_send,
    record_recv,
):
    subgrids, pols, owners = sizes
    z, p, t = lax.axis_index("facet"), lax.axis_index("pol"), lax.axis_index("tm")
    slots = lead_ref.shape[0]
    _, groups, rows, width = contrib_ref.shape
    mesh_id = pl.DeviceIdType.MESH

    def remote(src, dst, send, recv, peer):
        return pltpu.make_async_remote_copy(
            src_ref=src,
            dst_ref=dst,
            send_sem=send,
            recv_sem=recv,
            device_id=peer,
            device_id_type=mesh_id,
        )

    across_total = subgrids * owners
    plane_total = pols * owners
    across = z * owners + t
    plane = p * owners + t

    def across_peer(d):
        other = lax.rem(across + d, across_total)
        return other, (other // owners, p, lax.rem(other, owners))

    def plane_peer(d):
        other = lax.rem(plane + d, plane_total)
        return other, (z, other // owners, lax.rem(other, owners))

    barrier = pltpu.get_barrier_semaphore()
    for d in range(1, across_total):
        pl.semaphore_signal(barrier, inc=1, device_id=across_peer(d)[1], device_id_type=mesh_id)
    for d in range(1, pols):
        q = lax.rem(p + d, pols)
        for o in range(owners):
            pl.semaphore_signal(barrier, inc=1, device_id=(z, q, o), device_id_type=mesh_id)
    pl.semaphore_wait(barrier, across_total - 1 + (pols - 1) * owners)

    quarter = observed_ref.shape[1]
    place = lax.broadcasted_iota(jnp.int32, (2 * NPOL, slots), 1)
    observed_out[...] = jnp.where(
        (place >= p * quarter) & (place < (p + 1) * quarter),
        jnp.concatenate([observed_ref[...]] * pols, axis=1),
        0.0,
    )
    copies = []
    for d in sorted(range(1, subgrids), key=lambda d: -min(d, subgrids - d)):
        other = lax.rem(z + d, subgrids)
        copies.append(
            remote(contrib_ref.at[other], got.at[z], got_send.at[d], got_recv.at[d], (other, p, t))
        )
    partner = lax.rem(t + 1, owners)
    taper_copies = [
        remote(ref, tapers.at[t, k], taper_send.at[k], taper_recv.at[k], (z, p, partner))
        for k, ref in enumerate((trail_ref, lead_ref))
    ]
    observed_copies = []
    for d in range(1, pols):
        q = lax.rem(p + d, pols)
        observed_copies.append(
            remote(
                observed_out, observed_in.at[p], observed_send.at[d], observed_recv.at[d], (z, q, t)
            )
        )
    for copy in copies + taper_copies + observed_copies:
        copy.start()

    table_re = jnp.concatenate([table_re_ref[i, t] for i in range(FGRID)], axis=0)
    table_im = jnp.concatenate([table_im_ref[i, t] for i in range(FGRID)], axis=0)

    turn = jnp.where(
        lax.broadcasted_iota(jnp.int32, (3 * slots, 2 * MC), 1) < MC, -1.0, 1.0
    )

    def prepare(owner, trail, lead):
        trail3 = chirped_rows(trail, chirp_ref)
        a = jnp.dot(trail3, second_ref[...], preferred_element_type=jnp.float32)
        b = jnp.concatenate(
            [
                turn * pltpu.roll(a[:, j * 2 * MC : (j + 1) * 2 * MC], MC, 1)
                for j in range(a.shape[1] // (2 * MC))
            ],
            axis=1,
        )
        n0, n1, n2 = slice(0, slots), slice(slots, 2 * slots), slice(2 * slots, 3 * slots)
        right[owner, 0:slots, :] = a[n0].astype(jnp.bfloat16)
        right[owner, slots : 2 * slots, :] = (a[n1] - b[n2]).astype(jnp.bfloat16)
        right[owner, 2 * slots : 3 * slots, :] = b[n0].astype(jnp.bfloat16)
        right[owner, 3 * slots : 4 * slots, :] = (b[n1] + a[n2]).astype(jnp.bfloat16)
        lead3 = chirped_rows(lead, chirp_ref)
        u = nt_dot(table_re, lead3)
        v = nt_dot(table_im, lead3)
        left[owner, 0] = u[:, n0]
        left[owner, 1] = v[:, n0]
        left[owner, 2] = u[:, n1] - v[:, n2]
        left[owner, 3] = u[:, n2] + v[:, n1]

    prepare(t, trail_ref[...], lead_ref[...])
    got[z] = contrib_ref[z]
    for copy in taper_copies:
        copy.wait()
    prepare(partner, tapers[partner, 0], tapers[partner, 1])
    for copy in copies:
        copy.wait()
    if width == 2 * SG:
        whole = got[...].reshape(subgrids * groups * rows, width)
    else:
        for f in range(subgrids * groups):
            i, j = f // FGRID, f % FGRID
            lines[i * rows : (i + 1) * rows, j * 2 * MC : (j + 1) * 2 * MC] = got[
                f // groups, f % groups
            ]
        whole = lines[...]
    for o in range(owners):
        spread = nt_dot(whole, right[o])
        for w in range(NW):
            g_re = spread[:, w * slots : (w + 1) * slots]
            g_im = spread[:, (NW + w) * slots : (NW + w + 1) * slots]
            l_re, l_im = left[o, 2 * w], left[o, 2 * w + 1]
            part_out[o, 2 * w : 2 * w + 1, :] = jnp.sum(l_re * g_re - l_im * g_im, axis=0, keepdims=True)
            part_out[o, 2 * w + 1 : 2 * w + 2, :] = jnp.sum(
                l_re * g_im + l_im * g_re, axis=0, keepdims=True
            )
        part_out[o, 2 * NW :, :] = jnp.zeros((8 - 2 * NW, slots), jnp.float32)

    part_copies = []
    for d in range(1, plane_total):
        other, peer = plane_peer(d)
        part_copies.append(
            remote(
                part_out.at[lax.rem(other, owners)],
                part_in.at[plane],
                part_send.at[d],
                part_recv.at[d],
                peer,
            )
        )
    for copy in part_copies:
        copy.start()
    part_in[plane] = part_out[t]
    observed_in[p] = observed_out[...]
    for copy in observed_copies:
        copy.wait()
    observed = observed_in[0]
    for q in range(1, pols):
        observed = observed + observed_in[q]
    depth = depth_ref[...].astype(jnp.float32)
    for copy in part_copies:
        copy.wait()

    pred = []
    per_pol = part_in.shape[0] // NPOL
    for q in range(NPOL):
        block = part_in[q * per_pol]
        for o in range(1, per_pol):
            block = block + part_in[q * per_pol + o]
        pred.append(
            tuple(
                sum(depth[w : w + 1] * block[2 * w + c : 2 * w + c + 1] for w in range(NW))
                for c in range(2)
            )
        )
    gains = gains_ref[...]
    idents = idents_ref[...]
    residual, leading, trailing = model_terms(
        pred,
        [observed[k : k + 1] for k in range(2 * NPOL)],
        [gains[k : k + 1] for k in range(4)],
        [gains[4 + k : 5 + k] for k in range(4)],
        idents[3:4],
    )
    for k in range(3):
        record_out[k : k + 1, :] = idents[k : k + 1]
    for k in range(4):
        record_out[3 + k : 4 + k, :] = leading[k]
        record_out[7 + k : 8 + k, :] = trailing[k]
    record_out[11:, :] = jnp.zeros((5, slots), jnp.float32)
    record_copies = []
    for d in range(1, across_total):
        other, peer = across_peer(d)
        record_copies.append(
            remote(record_out, record_in.at[across], record_send.at[d], record_recv.at[d], peer)
        )
    for copy in record_copies:
        copy.start()
    record_in[across] = record_out[...]
    rest = jnp.concatenate(residual, axis=0)
    own_rest = jnp.zeros((2 * NPOL, quarter), jnp.float32)
    for q in range(pols):
        own_rest = jnp.where(p == q, rest[:, q * quarter : (q + 1) * quarter], own_rest)
    residual_ref[...] = own_rest
    for copy in record_copies:
        copy.wait()

    piece = jnp.concatenate([record_in[d] for d in range(across_total)], axis=1)
    own_count = grad_ref.shape[1]
    index = (z * pols + p) * owners + t
    mine = (index * own_count + lax.broadcasted_iota(jnp.int32, (own_count, 1), 0)).astype(
        jnp.float32
    )
    match_first = mine == piece[0:1]
    match_second = mine == piece[1:2]
    weighted = jnp.concatenate(
        [
            jnp.where(match_first, piece[3 + k : 4 + k], 0.0)
            + jnp.where(match_second, piece[7 + k : 8 + k], 0.0)
            for k in range(4)
        ],
        axis=0,
    )
    high = weighted.astype(jnp.bfloat16)
    low = (weighted - high.astype(jnp.float32)).astype(jnp.bfloat16)
    channel_ids = lax.broadcasted_iota(jnp.int32, (NCH, 1), 0).astype(jnp.float32)
    onehot = jnp.where(channel_ids == piece[2:3], 1.0, 0.0).astype(jnp.bfloat16)
    summed = nt_dot(high, onehot) + nt_dot(low, onehot)
    for k in range(4):
        grad_ref[k] = grad_scale * summed[k * own_count : (k + 1) * own_count]


def predict(sizes, own_count, *operands):
    subgrids, pols, owners = sizes
    contrib, lead = operands[0], operands[1]
    _, groups, rows, width = contrib.shape
    slots = lead.shape[0]
    vmem = pl.BlockSpec(memory_space=pltpu.VMEM)
    dma = lambda n: pltpu.SemaphoreType.DMA((n,))
    across_total, plane_total = subgrids * owners, pols * owners
    return pl.pallas_call(
        functools.partial(predict_kernel, sizes),
        out_shape=(
            jax.ShapeDtypeStruct((2 * NPOL, slots // pols), jnp.float32),
            jax.ShapeDtypeStruct((4, own_count, NCH), jnp.float32),
        ),
        in_specs=[vmem] * len(operands),
        out_specs=(vmem, vmem),
        scratch_shapes=[
            pltpu.VMEM(contrib.shape, jnp.bfloat16),
            pltpu.VMEM((FGRID * rows, 2 * SG), jnp.bfloat16),
            pltpu.VMEM((owners, 2, slots, SG), jnp.bfloat16),
            pltpu.VMEM((owners, 2 * NW * slots, 2 * SG), jnp.bfloat16),
            pltpu.VMEM((owners, 4, FGRID * rows, slots), jnp.float32),
            pltpu.VMEM((owners, 8, slots), jnp.float32),
            pltpu.VMEM((plane_total, 8, slots), jnp.float32),
            pltpu.VMEM((8, slots), jnp.float32),
            pltpu.VMEM((pols, 8, slots), jnp.float32),
            pltpu.VMEM((16, slots), jnp.float32),
            pltpu.VMEM((across_total, 16, slots), jnp.float32),
            dma(subgrids),
            dma(subgrids),
            dma(2),
            dma(2),
            dma(pols),
            dma(pols),
            dma(plane_total),
            dma(plane_total),
            dma(across_total),
            dma(across_total),
        ],
        compiler_params=pltpu.CompilerParams(
            collective_id=0, has_side_effects=True, vmem_limit_bytes=48 << 20
        ),
    )(*operands)


def folded_factors(subgrids):
    half = lambda odd, s, c: [s * 2 * MC + c * MC + k for k in range(odd, MC, 2)]
    order = []
    for odd in range(2):
        for first in range(0, subgrids, 2):
            for c in range(2):
                for s in ((first + 1, first) if odd else (first, first + 1)):
                    order += half(odd, s, c)
    p, q, cosine, sine = [t[:, order] for t in fourier_factors(subgrids)]
    return p[: len(p) // 2], q[: len(q) // 2], cosine, sine


def folded_second(second):
    split = second.reshape(SG, 2 * FGRID, MC // 2, 2)
    return np.concatenate([split[..., 0], split[..., 1]], axis=2).reshape(SG, 2 * SG)


def gather_lookups(block_ref, links_ref, gain_ref, gains_ref, idents_ref):
    blocks = block_ref.shape[2]
    slots = idents_ref.shape[1]
    span = slots + 128
    lane = lax.broadcasted_iota(jnp.int32, (1, slots), 1)
    place = lax.broadcasted_iota(jnp.int32, (span, slots), 0)
    lane_tall = lax.broadcasted_iota(jnp.int32, (span, slots), 1)
    begin = jnp.int32(0)
    member, picks, windows, tables = [], [], [], []
    channel = jnp.zeros((1, slots), jnp.float32)
    alive = jnp.zeros((1, slots), jnp.float32)
    for b in range(blocks):
        chosen, offset, amount = [block_ref[k, 0, b] for k in range(3)]
        row = jnp.minimum(lax.div(offset, 128), links_ref.shape[0] - span // 128)
        first = row * 128
        windows += [links_ref[row + k] for k in range(span // 128)]
        tables.append(gain_ref[chosen])
        inside = jnp.where((lane >= begin) & (lane < begin + amount), 1.0, 0.0)
        member.append(inside)
        alive += inside
        channel += inside * chosen.astype(jnp.float32)
        hit = place == lane_tall + (offset - first - begin)
        picks.append((jnp.where(hit, 1.0, 0.0) * inside).astype(jnp.bfloat16))
        begin = begin + amount
    links = jnp.concatenate(windows, axis=1)
    upper = links // 16
    lower = links - 16 * upper
    pieces = jnp.concatenate([upper, lower], axis=0).astype(jnp.float32).astype(jnp.bfloat16)
    found = jnp.dot(
        pieces, jnp.concatenate(picks, axis=0), preferred_element_type=jnp.float32
    )
    stations = 16.0 * found[0:2] + found[2:4]
    table = jnp.concatenate(tables, axis=0)
    high = table.astype(jnp.bfloat16)
    rest = table - high.astype(jnp.float32)
    middle = rest.astype(jnp.bfloat16)
    low = (rest - middle.astype(jnp.float32)).astype(jnp.bfloat16)
    split = jnp.concatenate([high, middle, low], axis=0)
    size = table.shape[0]
    names = lax.broadcasted_iota(jnp.int32, (table.shape[1], 1), 0).astype(jnp.float32)
    for side in range(2):
        pick = jnp.where(names == stations[side : side + 1], 1.0, 0.0).astype(jnp.bfloat16)
        three = jnp.dot(split, pick, preferred_element_type=jnp.float32)
        rows = three[:size] + three[size : 2 * size] + three[2 * size :]
        chosen = member[0] * rows[0:4]
        for b in range(1, blocks):
            chosen = chosen + member[b] * rows[4 * b : 4 * b + 4]
        gains_ref[4 * side : 4 * side + 4, :] = chosen
    idents_ref[0:2, :] = stations
    idents_ref[2:3, :] = channel
    idents_ref[3:4, :] = alive
    idents_ref[4:8, :] = jnp.zeros((4, slots), jnp.float32)


def fused_kernel(
    sizes,
    block_hbm,
    links_hbm,
    gain_hbm,
    p_hbm,
    q_hbm,
    c_hbm,
    s_hbm,
    x_hbm,
    lead_hbm,
    trail_hbm,
    depth_hbm,
    observed_hbm,
    table_re_hbm,
    table_im_hbm,
    second_hbm,
    chirp_hbm,
    residual_ref,
    grad_ref,
    block_ref,
    links_ref,
    gain_ref,
    p_ref,
    q_ref,
    c_ref,
    s_ref,
    x_ref,
    tapers,
    depths,
    observed_ref,
    table_ref,
    second_ref,
    chirp_ref,
    factors,
    contrib,
    got,
    right,
    left,
    gains_ref,
    idents_ref,
    side,
    part_out,
    part_in,
    observed_out,
    observed_in,
    rests,
    load_sem,
    chunk_sem,
    pair_send,
    pair_recv,
    chip_send,
    chip_recv,
    relay_send,
    relay_recv,
    far_send,
    far_recv,
    near_send,
    near_recv,
    observed_send,
    observed_recv,
    side_send,
    side_recv,
    part_send,
    part_recv,
):
    subgrids, pols, owners = sizes
    z, p, t = lax.axis_index("facet"), lax.axis_index("pol"), lax.axis_index("tm")
    _, _, slots, _ = tapers.shape
    facets, _, rows, length = x_ref.shape
    _, _, groups, _, width = contrib.shape
    side_z, own = lax.rem(z, 2), z // 2
    far = 1 - own
    pair_z = z + 1 - 2 * side_z
    far_z = z + 2 - 4 * own
    partner = lax.rem(t + 1, owners)
    mesh_id = pl.DeviceIdType.MESH

    def remote(src, dst, send, recv, peer):
        return pltpu.make_async_remote_copy(
            src_ref=src,
            dst_ref=dst,
            send_sem=send,
            recv_sem=recv,
            device_id=peer,
            device_id_type=mesh_id,
        )

    across_total = subgrids * owners
    across = z * owners + t

    def across_peer(d):
        other = lax.rem(across + d, across_total)
        return other, (other // owners, p, lax.rem(other, owners))

    barrier = pltpu.get_barrier_semaphore()
    greeted = [(pair_z, p, t), (far_z, p, t), (z, p, partner)]
    greeted += [(z, lax.rem(p + d, pols), t) for d in range(1, pols)]
    for peer in greeted:
        pl.semaphore_signal(barrier, inc=1, device_id=peer, device_id_type=mesh_id)

    offsets = [
        (dz, dp, dt)
        for dz in sorted(range(subgrids), key=lambda d: -min(d, subgrids - d))
        for dp in reversed(range(pols))
        for dt in range(owners)
    ]
    offsets.remove((0, 0, 0))
    per_chunk = FGRID // PIECES
    chunks = facets // per_chunk
    x_loads = [
        pltpu.make_async_copy(
            x_hbm.at[pl.ds(c * per_chunk, per_chunk)],
            x_ref.at[pl.ds(c * per_chunk, per_chunk)],
            chunk_sem.at[c],
        )
        for c in range(chunks)
    ]
    pairs = [
        (c_hbm, c_ref),
        (s_hbm, s_ref),
        (p_hbm, p_ref),
        (q_hbm, q_ref),
        (trail_hbm, tapers.at[own, 0]),
        (lead_hbm, tapers.at[own, 1]),
        (depth_hbm, depths.at[own]),
        (observed_hbm, observed_ref),
        (chirp_hbm, chirp_ref),
        (second_hbm, second_ref),
        (table_re_hbm.at[pl.ds(own * 2 * groups, 2 * groups)], table_ref.at[0]),
        (table_im_hbm.at[pl.ds(own * 2 * groups, 2 * groups)], table_ref.at[1]),
        (block_hbm, block_ref),
        (links_hbm, links_ref),
        (gain_hbm, gain_ref),
    ]
    loads = [
        pltpu.make_async_copy(src, dst, load_sem.at[k]) for k, (src, dst) in enumerate(pairs)
    ]
    for copy in loads[4:9] + loads[:4]:
        copy.start()
    x_loads[0].start()
    for copy in x_loads[1:]:
        copy.start()
    for copy in loads[9:]:
        copy.start()

    for copy in loads[4:9]:
        copy.wait()
    quarter = observed_ref.shape[1]
    place = lax.broadcasted_iota(jnp.int32, (2 * NPOL, slots), 1)
    observed_out[...] = jnp.where(
        (place >= p * quarter) & (place < (p + 1) * quarter),
        jnp.concatenate([observed_ref[...]] * pols, axis=1),
        0.0,
    )
    pl.semaphore_wait(barrier, len(greeted))
    share = lambda q: pl.ds(pl.multiple_of(q * quarter, quarter), quarter)
    far_copies = [
        remote(
            tapers.at[own, side, share(p)],
            tapers.at[own, side, share(p)],
            far_send.at[side],
            far_recv.at[side],
            (far_z, p, t),
        )
        for side in range(2)
    ]
    far_copies.append(
        remote(depths.at[own], depths.at[own], far_send.at[2], far_recv.at[2], (far_z, p, t))
    )
    observed_copies = []
    for d in range(1, pols):
        q = lax.rem(p + d, pols)
        observed_copies.append(
            remote(
                observed_out, observed_in.at[p], observed_send.at[d], observed_recv.at[d], (z, q, t)
            )
        )
    for copy in far_copies + observed_copies:
        copy.start()
    others = pols - 1
    near_copies = [
        remote(
            tapers.at[far, side, share(p)],
            tapers.at[far, side, share(p)],
            near_send.at[others * side + d - 1],
            near_recv.at[others * side + d - 1],
            (z, lax.rem(p + d, pols), t),
        )
        for side in range(2)
        for d in (2, 1, 3)
    ]

    def forward(side):
        far_copies[side].wait_recv()
        for copy in near_copies[others * side : others * side + others]:
            copy.start()


    for copy in loads[:4]:
        copy.wait()
    spread = c_ref.shape[0]
    cosine, sine = c_ref[...], s_ref[...]
    half = length // 2
    for part in range(half // spread):
        factors[part * spread : (part + 1) * spread, :] = (
            p_ref[part : part + 1, :] * cosine + q_ref[part : part + 1, :] * sine
        ).astype(jnp.bfloat16)

    lane = lax.broadcasted_iota(jnp.int32, (rows, 2 * MC), 1)
    sign = jnp.where(lane < MC, -1.0, 1.0)
    front = lane % MC < MC // 2
    folded = factors.shape[1] // 2
    part_width = width // PIECES
    pair_copies, chip_copies, relay_copies = [], [], []
    for c in range(chunks):
        x_loads[c].wait()
        x = x_ref[c * per_chunk : (c + 1) * per_chunk].reshape(per_chunk * 2 * rows, length)
        totals = [
            jnp.dot(
                x[:, :half] + x[:, half:], factors[:, :folded], preferred_element_type=jnp.float32
            ),
            jnp.dot(
                x[:, :half] - x[:, half:], factors[:, folded:], preferred_element_type=jnp.float32
            ),
        ]
        group, piece = c // PIECES, c % PIECES
        for pair in range(subgrids // 2):
            cut = slice(pair * 2 * MC, (pair + 1) * 2 * MC)
            for f in range(per_chunk):
                even, odd = [
                    total[2 * f * rows : (2 * f + 1) * rows, cut]
                    + sign
                    * pltpu.roll(total[(2 * f + 1) * rows : (2 * f + 2) * rows, cut], MC, 1)
                    for total in totals
                ]
                place = slice(
                    (piece * per_chunk + f) * 2 * MC, (piece * per_chunk + f + 1) * 2 * MC
                )
                contrib[0, pair, group, :, place] = jnp.where(front, even, odd).astype(jnp.bfloat16)
                other = jnp.where(front, odd, even)
                other = jnp.where(
                    front,
                    pltpu.roll(other, 2 * MC - MC // 2, 1),
                    pltpu.roll(other, MC // 2, 1),
                )
                contrib[1, pair, group, :, place] = other.astype(jnp.bfloat16)
        lanes = pl.ds(piece * part_width, part_width)
        pair_copies.append(
            remote(
                contrib.at[1 - side_z, :, group, :, lanes],
                got.at[:, side_z, group, t, :, lanes],
                pair_send.at[c],
                pair_recv.at[c],
                (pair_z, p, t),
            )
        )
        chip_copies.append(
            remote(
                contrib.at[side_z, :, group, :, lanes],
                got.at[:, side_z, group, t, :, lanes],
                chip_send.at[c],
                chip_recv.at[c],
                (z, p, partner),
            )
        )
        relay_copies.append(
            remote(
                got.at[:, 1 - side_z, group, t, :, lanes],
                got.at[:, 1 - side_z, group, t, :, lanes],
                relay_send.at[c],
                relay_recv.at[c],
                (z, p, partner),
            )
        )
        pair_copies[c].start()
        chip_copies[c].start()
        if c == chunks - FORWARD:
            forward(0)

    for k in range(2):
        for group in range(groups):
            got[k, side_z, group, t] = contrib[side_z, k, group]
    for copy in loads[9:]:
        copy.wait()
    gather_lookups(block_ref, links_ref, gain_ref, gains_ref, idents_ref)
    observed_in[p] = observed_out[...]
    for copy in observed_copies:
        copy.wait()
    observed = observed_in[0]
    for q in range(1, pols):
        observed = observed + observed_in[q]
    side[across, 0:8] = gains_ref[...]
    side[across, 8:16] = observed
    side[across, 16:20] = idents_ref[0:4]
    side_copies = []
    for d in range(1, across_total):
        other, peer = across_peer(d)
        side_copies.append(
            remote(side.at[across], side.at[across], side_send.at[d], side_recv.at[d], peer)
        )
    forward(1)

    span = 2 * groups * owners * rows
    table_re = table_ref[0].reshape(span, SG)
    table_im = table_ref[1].reshape(span, SG)
    turn = jnp.where(
        lax.broadcasted_iota(jnp.int32, (3 * slots, 2 * MC), 1) < MC, -1.0, 1.0
    )

    def prepare_right(k):
        trail3 = chirped_rows(tapers[k, 0], chirp_ref)
        a = jnp.dot(trail3, second_ref[...], preferred_element_type=jnp.float32)
        b = jnp.concatenate(
            [
                turn * pltpu.roll(a[:, j * 2 * MC : (j + 1) * 2 * MC], MC, 1)
                for j in range(a.shape[1] // (2 * MC))
            ],
            axis=1,
        )
        n0, n1, n2 = slice(0, slots), slice(slots, 2 * slots), slice(2 * slots, 3 * slots)
        right[k, 0:slots, :] = a[n0].astype(jnp.bfloat16)
        right[k, slots : 2 * slots, :] = (a[n1] - b[n2]).astype(jnp.bfloat16)
        right[k, 2 * slots : 3 * slots, :] = b[n0].astype(jnp.bfloat16)
        right[k, 3 * slots : 4 * slots, :] = (b[n1] + a[n2]).astype(jnp.bfloat16)

    def prepare_left(k):
        n0, n1, n2 = slice(0, slots), slice(slots, 2 * slots), slice(2 * slots, 3 * slots)
        lead3 = chirped_rows(tapers[k, 1], chirp_ref)
        u = nt_dot(table_re, lead3)
        v = nt_dot(table_im, lead3)
        left[k, 0] = u[:, n0]
        left[k, 1] = v[:, n0]
        left[k, 2] = u[:, n1] - v[:, n2]
        left[k, 3] = u[:, n2] + v[:, n1]

    prepare_right(own)
    prepare_left(own)
    for pair, relay in zip(pair_copies[:-1], relay_copies[:-1]):
        pair.wait_recv()
        relay.start()
    chip_copies[-1].wait_recv()
    for copy in side_copies:
        copy.start()
    for copy in near_copies[:others]:
        copy.wait_recv()
    prepare_right(far)
    pair_copies[-1].wait_recv()
    relay_copies[-1].start()
    for copy in [far_copies[2]] + near_copies[others:]:
        copy.wait_recv()
    prepare_left(far)
    for copy in chip_copies[:-1] + relay_copies:
        copy.wait()
    chip_copies[-1].wait_send()
    for k in range(2):
        spread_v = nt_dot(got[k].reshape(span, width), right[k])
        weights = depths[k].astype(jnp.float32)
        sums = [0.0, 0.0]
        for w in range(NW):
            g_re = spread_v[:, w * slots : (w + 1) * slots]
            g_im = spread_v[:, (NW + w) * slots : (NW + w + 1) * slots]
            l_re, l_im = left[k, 2 * w], left[k, 2 * w + 1]
            weight = weights[w : w + 1]
            sums[0] += weight * jnp.sum(l_re * g_re - l_im * g_im, axis=0, keepdims=True)
            sums[1] += weight * jnp.sum(l_re * g_im + l_im * g_re, axis=0, keepdims=True)
        for c in range(2):
            part_out[2 * c + k : 2 * c + k + 1, :] = sums[c]

    part_copies = []
    for dz, dp, dt in offsets:
        peer = (lax.rem(z + dz, subgrids), lax.rem(p + dp, pols), lax.rem(t + dt, owners))
        k = (dz * pols + dp) * owners + dt
        part_copies.append(
            remote(part_out, part_in.at[z, p, t], part_send.at[k], part_recv.at[k], peer)
        )
    for copy in part_copies:
        copy.start()
    part_in[z, p, t] = part_out[...]
    for copy in pair_copies + far_copies + near_copies:
        copy.wait_send()
    for copy in side_copies:
        copy.wait()

    own_count = grad_ref.shape[0]
    index = (z * pols + p) * owners + t
    mine = (index * own_count + lax.broadcasted_iota(jnp.int32, (own_count, 1), 0)).astype(
        jnp.float32
    )
    channel_ids = lax.broadcasted_iota(jnp.int32, (NCH, 1), 0).astype(jnp.float32)
    first_here = [jnp.where(mine == side[d, 16:17], 1.0, 0.0) for d in range(across_total)]
    second_here = [jnp.where(mine == side[d, 17:18], 1.0, 0.0) for d in range(across_total)]
    onehot = jnp.concatenate(
        [
            jnp.where(channel_ids == side[d, 18:19], 1.0, 0.0).astype(jnp.bfloat16)
            for d in range(across_total)
        ],
        axis=1,
    )
    column = lambda k: jnp.concatenate([side[d, k : k + 1] for d in range(across_total)], axis=0)
    gains = [column(k) for k in range(8)]
    observed = [column(8 + k) for k in range(8)]
    alive = column(19)
    for copy in part_copies:
        copy.wait()

    pred = []
    for q in range(NPOL):
        both = [[part_in[y, q, o] + part_in[y + 2, q, o] for o in range(owners)] for y in range(2)]
        pred.append(
            tuple(
                jnp.concatenate(
                    [
                        both[s % 2][o][2 * c + s // 2 : 2 * c + s // 2 + 1]
                        for s in range(subgrids)
                        for o in range(owners)
                    ],
                    axis=0,
                )
                for c in range(2)
            )
        )
    residual, leading, trailing = model_terms(pred, observed, gains[:4], gains[4:], alive)
    for k in range(2 * NPOL):
        rests[:, k : k + 1, :] = residual[k][:, None, :]
    rest = rests[across]
    own_rest = jnp.zeros((2 * NPOL, quarter), jnp.float32)
    for q in range(pols):
        own_rest = jnp.where(p == q, rest[:, q * quarter : (q + 1) * quarter], own_rest)
    residual_ref[...] = own_rest

    weighted = jnp.concatenate(
        [
            jnp.concatenate(
                [
                    first_here[d] * leading[k][d : d + 1]
                    + second_here[d] * trailing[k][d : d + 1]
                    for d in range(across_total)
                ],
                axis=1,
            )
            for k in range(4)
        ],
        axis=0,
    )
    high = weighted.astype(jnp.bfloat16)
    low = (weighted - high.astype(jnp.float32)).astype(jnp.bfloat16)
    summed = nt_dot(jnp.concatenate([high, low], axis=0), onehot)
    summed = summed[: high.shape[0]] + summed[high.shape[0] :]
    lane_group = lax.broadcasted_iota(jnp.int32, (own_count, 128), 1) // 32
    mixed = []
    for g in range(NCH // 32):
        base = g // 4 * 128
        built = None
        for k in range(4):
            block = summed[k * own_count : (k + 1) * own_count, base : base + 128]
            shift = 32 * (k - g % 4) % 128
            block = pltpu.roll(block, shift, 1) if shift else block
            built = block if built is None else jnp.where(lane_group == k, block, built)
        mixed.append(grad_scale * built)
    mixed = jnp.concatenate(mixed, axis=0)
    high = mixed.astype(jnp.bfloat16)
    low = (mixed - high.astype(jnp.float32)).astype(jnp.bfloat16)
    came = lax.broadcasted_iota(jnp.int32, (128, 128), 0)
    goes = lax.broadcasted_iota(jnp.int32, (128, 128), 1)
    order = jnp.where(goes == came % 32 * 4 + came // 32, 1.0, 0.0).astype(jnp.bfloat16)
    placed = jnp.dot(
        jnp.concatenate([high, low], axis=0), order, preferred_element_type=jnp.float32
    )
    placed = placed[: mixed.shape[0]] + placed[mixed.shape[0] :]
    for g in range(NCH // 32):
        grad_ref[:, g * 128 : (g + 1) * 128] = placed[g * own_count : (g + 1) * own_count]


def emit_kernel(residual_ref, grad_ref, residual_out, grad_out, sems):
    copies = [
        pltpu.make_async_copy(residual_ref, residual_out, sems.at[0]),
        pltpu.make_async_copy(grad_ref, grad_out, sems.at[1]),
    ]
    for copy in copies:
        copy.start()
    for copy in copies:
        copy.wait()


def fused(sizes, own_count, *operands):
    subgrids, pols, owners = sizes
    block_table, links, gains = operands[0:3]
    x, lead, trail, depth, observed = operands[7:12]
    facets, _, rows, length = x.shape
    slots = lead.shape[0]
    width = subgrids * 2 * MC
    spread = FS // MC
    groups = facets // FGRID
    chunks = facets // (FGRID // PIECES)
    hbm = pl.BlockSpec(memory_space=pltpu.HBM)
    vmem = pl.BlockSpec(memory_space=pltpu.VMEM)
    dma = lambda n: pltpu.SemaphoreType.DMA((n,))
    held = lambda a: pltpu.VMEM(a.shape, a.dtype)
    across_total, all_total = subgrids * owners, subgrids * pols * owners
    f32, bf16 = jnp.float32, jnp.bfloat16
    residual, grad = pl.pallas_call(
        functools.partial(fused_kernel, sizes),
        out_shape=(
            jax.ShapeDtypeStruct(observed.shape, f32),
            jax.ShapeDtypeStruct((own_count, 4 * NCH), f32),
        ),
        in_specs=[hbm] * len(operands),
        out_specs=(vmem, vmem),
        scratch_shapes=[
            pltpu.SMEM(block_table.shape, jnp.int32),
            held(links),
            held(gains),
            pltpu.VMEM((length // 2 // spread, width), f32),
            pltpu.VMEM((length // 2 // spread, width), f32),
            pltpu.VMEM((spread, width), f32),
            pltpu.VMEM((spread, width), f32),
            held(x),
            pltpu.VMEM((2, 2, slots, SG), bf16),
            pltpu.VMEM((2,) + depth.shape, bf16),
            held(observed),
            pltpu.VMEM((2, 2 * groups, owners, rows, SG), bf16),
            pltpu.VMEM((SG, 2 * SG), bf16),
            pltpu.VMEM((2, SG), f32),
            pltpu.VMEM((length // 2, width), bf16),
            pltpu.VMEM((2, 2, groups, rows, 2 * SG), bf16),
            pltpu.VMEM((2, 2, groups, owners, rows, 2 * SG), bf16),
            pltpu.VMEM((2, 2 * NW * slots, 2 * SG), bf16),
            pltpu.VMEM((2, 4, 2 * groups * owners * rows, slots), f32),
            pltpu.VMEM((8, slots), f32),
            pltpu.VMEM((8, slots), f32),
            pltpu.VMEM((across_total, 20, slots), f32),
            pltpu.VMEM((4, slots), f32),
            pltpu.VMEM((subgrids, pols, owners, 4, slots), f32),
            pltpu.VMEM((8, slots), f32),
            pltpu.VMEM((pols, 8, slots), f32),
            pltpu.VMEM((across_total, 8, slots), f32),
            dma(15),
            dma(chunks),
            dma(chunks),
            dma(chunks),
            dma(chunks),
            dma(chunks),
            dma(chunks),
            dma(chunks),
            dma(3),
            dma(3),
            dma(2 * pols - 2),
            dma(2 * pols - 2),
            dma(pols),
            dma(pols),
            dma(across_total),
            dma(across_total),
            dma(all_total),
            dma(all_total),
        ],
        compiler_params=pltpu.CompilerParams(
            collective_id=0, has_side_effects=True, vmem_limit_bytes=36 << 20
        ),
    )(*[pltpu.with_memory_space_constraint(a, pltpu.HBM) for a in operands])
    return pl.pallas_call(
        emit_kernel,
        out_shape=(
            jax.ShapeDtypeStruct(residual.shape, f32),
            jax.ShapeDtypeStruct(grad.shape, f32),
        ),
        in_specs=[vmem] * 2,
        out_specs=[hbm] * 2,
        scratch_shapes=[dma(2)],
        compiler_params=pltpu.CompilerParams(vmem_limit_bytes=1 << 20),
    )(residual, grad)


def on_device(
    tile_spectral_lines,
    taper_leading_axis,
    taper_trailing_axis,
    depth_layer_factors,
    measured_correlations,
    visibility_groups_table,
    antenna_links,
    complex_receiver_factors,
):
    sizes = tuple(lax.axis_size(name) for name in ("facet", "pol", "tm"))
    subgrids, pols, owners = sizes
    slots = taper_leading_axis.shape[2]
    quarter = measured_correlations.shape[3]
    rows = tile_spectral_lines.shape[3]

    block_table = visibility_groups_table.reshape(3, visibility_groups_table.shape[3])
    observed = measured_correlations.reshape(2 * NPOL, quarter)

    if tile_spectral_lines.shape[0] % FGRID == 0 and sizes == (4, NPOL, 2):
        table_re, table_im = [jnp.asarray(t) for t in subgrid_tables()[:2]]
        own_count = NST // (subgrids * pols * owners)
        residual, gain_grad = fused(
            sizes,
            own_count,
            visibility_groups_table.reshape(3, 1, visibility_groups_table.shape[3]),
            jnp.transpose(antenna_links.reshape(2, -1, 128), (1, 0, 2)),
            complex_receiver_factors,
            *[jnp.asarray(t) for t in folded_factors(subgrids)],
            tile_spectral_lines[:, 0],
            taper_leading_axis.reshape(slots, SG),
            taper_trailing_axis.reshape(slots, SG),
            depth_layer_factors.reshape(NW, slots),
            observed,
            table_re.reshape(FGRID, owners, rows, SG),
            table_im.reshape(FGRID, owners, rows, SG),
            jnp.asarray(folded_second(subgrid_tables()[2])),
            jnp.asarray(np.stack(chirp_line())),
        )
        return residual.reshape(1, 2 * NPOL, 1, quarter), gain_grad

    contrib, gains, idents = fourier(
        tile_spectral_lines[:, 0],
        subgrids,
        slots,
        block_table,
        antenna_links,
        complex_receiver_factors,
    )
    table_re, table_im, second = [jnp.asarray(t) for t in subgrid_tables()]
    cosine, sine = chirp_line()
    own_count = NST // (subgrids * pols * owners)
    residual, grad = predict(
        sizes,
        own_count,
        contrib,
        taper_leading_axis.reshape(slots, SG),
        taper_trailing_axis.reshape(slots, SG),
        depth_layer_factors.reshape(NW, slots),
        observed,
        gains,
        idents,
        table_re.reshape(FGRID, owners, rows, SG),
        table_im.reshape(FGRID, owners, rows, SG),
        second,
        jnp.asarray(np.stack([cosine, sine])),
    )
    gain_grad = jnp.transpose(grad, (1, 2, 0)).reshape(own_count, 4 * NCH)
    return residual.reshape(1, 2 * NPOL, 1, quarter), gain_grad


def solution(mesh):
    return jax.shard_map(
        on_device,
        mesh=mesh,
        in_specs=(
            P("facet", "pol", None, "tm", None),
            P("facet", "tm", None, None),
            P("facet", "tm", None, None),
            P("facet", "tm", None, None),
            P("facet", None, "tm", "pol"),
            P("facet", "tm", None, None),
            P(),
            P(),
        ),
        out_specs=(P("facet", None, "tm", "pol"), P(("facet", "pol", "tm"), None)),
        check_vma=False,
    )
```

```python
import functools
import math

import jax
import jax.numpy as jnp
import numpy as np
from jax import lax
from jax.experimental import pallas as pl
from jax.experimental.pallas import tpu as pltpu
from jax.sharding import PartitionSpec as P

FGRID = 8
FS = 4096
MC = 64
SG = 512
NPOL = 4
NW = 2
NCH = 256
NST = 512
CHUNK = 1024
PIECES = 2
FORWARD = 2

w_chirp = 0.37
grad_scale = 0.1


def unit_angles(left, right, length):
    product = np.outer(np.arange(left), np.arange(right)) % length
    return 2.0 * math.pi * product / length


def fourier_factors(subgrids):
    spread = FS // MC
    alpha = unit_angles(FS // spread, MC, MC)
    p = np.concatenate([np.cos(alpha), -np.sin(alpha)], axis=1) / math.sqrt(FS)
    q = np.concatenate([-np.sin(alpha), -np.cos(alpha)], axis=1) / math.sqrt(FS)
    beta = unit_angles(spread, subgrids * MC, FS).reshape(spread, subgrids, 1, MC)
    beta = np.broadcast_to(beta, (spread, subgrids, 2, MC)).reshape(spread, subgrids * 2 * MC)
    tile = lambda t: np.tile(t, (1, subgrids)).astype(np.float32)
    return (
        tile(p),
        tile(q),
        np.cos(beta).astype(np.float32),
        np.sin(beta).astype(np.float32),
    )


def fetch_lookups(block_ref, links_ref, gain_ref, window, channel_gain, window_sem, gain_sem):
    blocks, _, span = window.shape
    copies = []
    for b in range(blocks):
        first = jnp.minimum(block_ref[1, b] // 128 * 128, links_ref.shape[1] - span)
        first = pl.multiple_of(first, 128)
        copies.append(
            pltpu.make_async_copy(
                links_ref.at[:, pl.ds(first, span)], window.at[b], window_sem.at[b]
            )
        )
        copies.append(
            pltpu.make_async_copy(
                gain_ref.at[block_ref[0, b]], channel_gain.at[b], gain_sem.at[b]
            )
        )
    return copies


def use_lookups(block_ref, links_ref, window, channel_gain, gains_ref, idents_ref):
    blocks, _, span = window.shape
    slots = idents_ref.shape[1]
    lane = lax.broadcasted_iota(jnp.int32, (1, slots), 1)
    place = lax.broadcasted_iota(jnp.int32, (span, slots), 0)
    lane_tall = lax.broadcasted_iota(jnp.int32, (span, slots), 1)
    begin = jnp.int32(0)
    member, picks = [], []
    channel = jnp.zeros((1, slots), jnp.float32)
    alive = jnp.zeros((1, slots), jnp.float32)
    for b in range(blocks):
        offset, amount = block_ref[1, b], block_ref[2, b]
        first = jnp.minimum(offset // 128 * 128, links_ref.shape[1] - span)
        inside = jnp.where((lane >= begin) & (lane < begin + amount), 1.0, 0.0)
        member.append(inside)
        alive += inside
        channel += inside * block_ref[0, b].astype(jnp.float32)
        hit = place == lane_tall + (offset - first - begin)
        picks.append((jnp.where(hit, 1.0, 0.0) * inside).astype(jnp.bfloat16))
        begin = begin + amount
    links = jnp.concatenate([window[b] for b in range(blocks)], axis=1)
    upper = links // 16
    lower = links - 16 * upper
    pieces = jnp.concatenate([upper, lower], axis=0).astype(jnp.float32).astype(jnp.bfloat16)
    found = jnp.dot(
        pieces, jnp.concatenate(picks, axis=0), preferred_element_type=jnp.float32
    )
    stations = 16.0 * found[0:2] + found[2:4]
    table = channel_gain[...].reshape(blocks * 4, channel_gain.shape[2])
    high = table.astype(jnp.bfloat16)
    rest = table - high.astype(jnp.float32)
    middle = rest.astype(jnp.bfloat16)
    low = (rest - middle.astype(jnp.float32)).astype(jnp.bfloat16)
    names = lax.broadcasted_iota(jnp.int32, (table.shape[1], 1), 0).astype(jnp.float32)
    for side in range(2):
        pick = jnp.where(names == stations[side : side + 1], 1.0, 0.0).astype(jnp.bfloat16)
        rows = (
            jnp.dot(high, pick, preferred_element_type=jnp.float32)
            + jnp.dot(middle, pick, preferred_element_type=jnp.float32)
            + jnp.dot(low, pick, preferred_element_type=jnp.float32)
        )
        chosen = member[0] * rows[0:4]
        for b in range(1, blocks):
            chosen = chosen + member[b] * rows[4 * b : 4 * b + 4]
        gains_ref[4 * side : 4 * side + 4, :] = chosen
    idents_ref[0:2, :] = stations
    idents_ref[2:3, :] = channel
    idents_ref[3:4, :] = alive
    idents_ref[4:8, :] = jnp.zeros((4, slots), jnp.float32)


def fourier_kernel(
    block_ref,
    links_ref,
    gain_ref,
    p_ref,
    q_ref,
    c_ref,
    s_ref,
    x_ref,
    o_ref,
    gains_ref,
    idents_ref,
    table,
    total,
    window,
    channel_gain,
    window_sem,
    gain_sem,
):
    step = pl.program_id(0)
    copies = fetch_lookups(
        block_ref, links_ref, gain_ref, window, channel_gain, window_sem, gain_sem
    )

    @pl.when(step == 0)
    def _():
        for copy in copies:
            copy.start()

    @pl.when(step == pl.num_programs(0) - 1)
    def _():
        for copy in copies:
            copy.wait()
        use_lookups(block_ref, links_ref, window, channel_gain, gains_ref, idents_ref)

    facets, _, rows, chunk = x_ref.shape
    subgrids = o_ref.shape[0]
    spread = c_ref.shape[0]
    cosine, sine = c_ref[...], s_ref[...]
    for part in range(chunk // spread):
        lead = p_ref[part : part + 1, :]
        other = q_ref[part : part + 1, :]
        table[part * spread : (part + 1) * spread, :] = (lead * cosine + other * sine).astype(
            jnp.bfloat16
        )
    x = x_ref[...].reshape(facets * 2 * rows, chunk)
    product = jnp.dot(x, table[...], preferred_element_type=jnp.float32)

    @pl.when(step == 0)
    def _():
        total[...] = product

    @pl.when(step > 0)
    def _():
        total[...] += product

    @pl.when(step == pl.num_programs(0) - 1)
    def _():
        lane = lax.broadcasted_iota(jnp.int32, (rows, 2 * MC), 1)
        sign = jnp.where(lane < MC, -1.0, 1.0)
        packed = o_ref.shape[3] // (2 * MC)
        for f in range(facets):
            for s in range(subgrids):
                cut = slice(s * 2 * MC, (s + 1) * 2 * MC)
                first = total[2 * f * rows : (2 * f + 1) * rows, cut]
                second = total[(2 * f + 1) * rows : (2 * f + 2) * rows, cut]
                value = first + sign * pltpu.roll(second, MC, 1)
                j = f % packed
                o_ref[s, f // packed, :, j * 2 * MC : (j + 1) * 2 * MC] = value.astype(jnp.bfloat16)


def fourier(x, subgrids, slots, block_table, links, station_gains):
    facets, _, rows, length = x.shape
    width = subgrids * 2 * MC
    spread = FS // MC
    packed = FGRID if facets % FGRID == 0 else 1
    per_step = CHUNK // spread
    blocks = block_table.shape[1]
    span = slots + 128
    in_place = lambda array: pltpu.with_memory_space_constraint(array, pltpu.HBM)
    factors = [in_place(jnp.asarray(t)) for t in fourier_factors(subgrids)]
    out = (subgrids, facets // packed, rows, packed * 2 * MC)
    return pl.pallas_call(
        fourier_kernel,
        out_shape=(
            jax.ShapeDtypeStruct(out, jnp.bfloat16),
            jax.ShapeDtypeStruct((8, slots), jnp.float32),
            jax.ShapeDtypeStruct((8, slots), jnp.float32),
        ),
        grid=(length // CHUNK,),
        in_specs=[
            pl.BlockSpec(memory_space=pltpu.SMEM),
            pl.BlockSpec(memory_space=pltpu.HBM),
            pl.BlockSpec(memory_space=pltpu.HBM),
            pl.BlockSpec((per_step, width), lambda g: (g, 0)),
            pl.BlockSpec((per_step, width), lambda g: (g, 0)),
            pl.BlockSpec((spread, width), lambda g: (0, 0)),
            pl.BlockSpec((spread, width), lambda g: (0, 0)),
            pl.BlockSpec((facets, 2, rows, CHUNK), lambda g: (0, 0, 0, g)),
        ],
        out_specs=(
            pl.BlockSpec(out, lambda g: (0, 0, 0, 0)),
            pl.BlockSpec((8, slots), lambda g: (0, 0)),
            pl.BlockSpec((8, slots), lambda g: (0, 0)),
        ),
        scratch_shapes=[
            pltpu.VMEM((CHUNK, width), jnp.bfloat16),
            pltpu.VMEM((facets * 2 * rows, width), jnp.float32),
            pltpu.VMEM((blocks, 2, span), jnp.int32),
            pltpu.VMEM((blocks, 4, NST), jnp.float32),
            pltpu.SemaphoreType.DMA((blocks,)),
            pltpu.SemaphoreType.DMA((blocks,)),
        ],
        compiler_params=pltpu.CompilerParams(
            dimension_semantics=("arbitrary",), vmem_limit_bytes=48 << 20
        ),
    )(
        block_table,
        in_place(links),
        in_place(station_gains),
        *factors,
        x,
    )


def subgrid_tables():
    angle = unit_angles(SG, SG, SG)
    re = np.cos(angle) / math.sqrt(SG)
    im = np.sin(angle) / math.sqrt(SG)
    blocks = lambda t: t.reshape(SG, FGRID, MC)
    second = np.stack([blocks(re), -blocks(im)], axis=2).reshape(SG, 2 * SG)
    return [t.astype(jnp.bfloat16) for t in (re, im, second)]


def chirp_line():
    offset = np.arange(SG) - SG // 2
    angle = 2.0 * math.pi * w_chirp * (offset * offset) / float(SG * SG)
    return np.cos(angle).astype(np.float32), np.sin(angle).astype(np.float32)


def model_terms(pred, observed, first, second, alive):
    residual, lead, trail = [], [], []
    for p in range(NPOL):
        f1, f2 = p // 2, p % 2
        pred_re, pred_im = pred[p]
        first_re, first_im = first[2 * f1], first[2 * f1 + 1]
        second_re, second_im = second[2 * f2], second[2 * f2 + 1]
        both_re = first_re * second_re + first_im * second_im
        both_im = first_im * second_re - first_re * second_im
        resid_re = alive * (observed[2 * p] - (both_re * pred_re - both_im * pred_im))
        resid_im = alive * (observed[2 * p + 1] - (both_re * pred_im + both_im * pred_re))
        cross_re = second_re * pred_re + second_im * pred_im
        cross_im = second_im * pred_re - second_re * pred_im
        along_re = first_re * pred_re - first_im * pred_im
        along_im = first_re * pred_im + first_im * pred_re
        residual += [resid_re, resid_im]
        lead.append(
            (-(resid_re * cross_re - resid_im * cross_im), -(resid_re * cross_im + resid_im * cross_re))
        )
        trail.append(
            (-(resid_re * along_re + resid_im * along_im), -(resid_re * along_im - resid_im * along_re))
        )
    leading = [lead[2 * f][r] + lead[2 * f + 1][r] for f in range(2) for r in range(2)]
    trailing = [trail[f][r] + trail[f + 2][r] for f in range(2) for r in range(2)]
    return residual, leading, trailing


def nt_dot(left, right, **kw):
    return lax.dot_general(
        left, right, (((1,), (1,)), ((), ())), preferred_element_type=jnp.float32, **kw
    )


def chirped_rows(taper, chirp_ref):
    wide = taper.astype(jnp.float32)
    return jnp.concatenate(
        [
            taper,
            (wide * chirp_ref[0:1, :]).astype(jnp.bfloat16),
            (wide * chirp_ref[1:2, :]).astype(jnp.bfloat16),
        ],
        axis=0,
    )


def predict_kernel(
    sizes,
    contrib_ref,
    lead_ref,
    trail_ref,
    depth_ref,
    observed_ref,
    gains_ref,
    idents_ref,
    table_re_ref,
    table_im_ref,
    second_ref,
    chirp_ref,
    residual_ref,
    grad_ref,
    got,
    lines,
    tapers,
    right,
    left,
    part_out,
    part_in,
    observed_out,
    observed_in,
    record_out,
    record_in,
    got_send,
    got_recv,
    taper_send,
    taper_recv,
    observed_send,
    observed_recv,
    part_send,
    part_recv,
    record_send,
    record_recv,
):
    subgrids, pols, owners = sizes
    z, p, t = lax.axis_index("facet"), lax.axis_index("pol"), lax.axis_index("tm")
    slots = lead_ref.shape[0]
    _, groups, rows, width = contrib_ref.shape
    mesh_id = pl.DeviceIdType.MESH

    def remote(src, dst, send, recv, peer):
        return pltpu.make_async_remote_copy(
            src_ref=src,
            dst_ref=dst,
            send_sem=send,
            recv_sem=recv,
            device_id=peer,
            device_id_type=mesh_id,
        )

    across_total = subgrids * owners
    plane_total = pols * owners
    across = z * owners + t
    plane = p * owners + t

    def across_peer(d):
        other = lax.rem(across + d, across_total)
        return other, (other // owners, p, lax.rem(other, owners))

    def plane_peer(d):
        other = lax.rem(plane + d, plane_total)
        return other, (z, other // owners, lax.rem(other, owners))

    barrier = pltpu.get_barrier_semaphore()
    for d in range(1, across_total):
        pl.semaphore_signal(barrier, inc=1, device_id=across_peer(d)[1], device_id_type=mesh_id)
    for d in range(1, pols):
        q = lax.rem(p + d, pols)
        for o in range(owners):
            pl.semaphore_signal(barrier, inc=1, device_id=(z, q, o), device_id_type=mesh_id)
    pl.semaphore_wait(barrier, across_total - 1 + (pols - 1) * owners)

    quarter = observed_ref.shape[1]
    place = lax.broadcasted_iota(jnp.int32, (2 * NPOL, slots), 1)
    observed_out[...] = jnp.where(
        (place >= p * quarter) & (place < (p + 1) * quarter),
        jnp.concatenate([observed_ref[...]] * pols, axis=1),
        0.0,
    )
    copies = []
    for d in sorted(range(1, subgrids), key=lambda d: -min(d, subgrids - d)):
        other = lax.rem(z + d, subgrids)
        copies.append(
            remote(contrib_ref.at[other], got.at[z], got_send.at[d], got_recv.at[d], (other, p, t))
        )
    partner = lax.rem(t + 1, owners)
    taper_copies = [
        remote(ref, tapers.at[t, k], taper_send.at[k], taper_recv.at[k], (z, p, partner))
        for k, ref in enumerate((trail_ref, lead_ref))
    ]
    observed_copies = []
    for d in range(1, pols):
        q = lax.rem(p + d, pols)
        observed_copies.append(
            remote(
                observed_out, observed_in.at[p], observed_send.at[d], observed_recv.at[d], (z, q, t)
            )
        )
    for copy in copies + taper_copies + observed_copies:
        copy.start()

    table_re = jnp.concatenate([table_re_ref[i, t] for i in range(FGRID)], axis=0)
    table_im = jnp.concatenate([table_im_ref[i, t] for i in range(FGRID)], axis=0)

    turn = jnp.where(
        lax.broadcasted_iota(jnp.int32, (3 * slots, 2 * MC), 1) < MC, -1.0, 1.0
    )

    def prepare(owner, trail, lead):
        trail3 = chirped_rows(trail, chirp_ref)
        a = jnp.dot(trail3, second_ref[...], preferred_element_type=jnp.float32)
        b = jnp.concatenate(
            [
                turn * pltpu.roll(a[:, j * 2 * MC : (j + 1) * 2 * MC], MC, 1)
                for j in range(a.shape[1] // (2 * MC))
            ],
            axis=1,
        )
        n0, n1, n2 = slice(0, slots), slice(slots, 2 * slots), slice(2 * slots, 3 * slots)
        right[owner, 0:slots, :] = a[n0].astype(jnp.bfloat16)
        right[owner, slots : 2 * slots, :] = (a[n1] - b[n2]).astype(jnp.bfloat16)
        right[owner, 2 * slots : 3 * slots, :] = b[n0].astype(jnp.bfloat16)
        right[owner, 3 * slots : 4 * slots, :] = (b[n1] + a[n2]).astype(jnp.bfloat16)
        lead3 = chirped_rows(lead, chirp_ref)
        u = nt_dot(table_re, lead3)
        v = nt_dot(table_im, lead3)
        left[owner, 0] = u[:, n0]
        left[owner, 1] = v[:, n0]
        left[owner, 2] = u[:, n1] - v[:, n2]
        left[owner, 3] = u[:, n2] + v[:, n1]

    prepare(t, trail_ref[...], lead_ref[...])
    got[z] = contrib_ref[z]
    for copy in taper_copies:
        copy.wait()
    prepare(partner, tapers[partner, 0], tapers[partner, 1])
    for copy in copies:
        copy.wait()
    if width == 2 * SG:
        whole = got[...].reshape(subgrids * groups * rows, width)
    else:
        for f in range(subgrids * groups):
            i, j = f // FGRID, f % FGRID
            lines[i * rows : (i + 1) * rows, j * 2 * MC : (j + 1) * 2 * MC] = got[
                f // groups, f % groups
            ]
        whole = lines[...]
    for o in range(owners):
        spread = nt_dot(whole, right[o])
        for w in range(NW):
            g_re = spread[:, w * slots : (w + 1) * slots]
            g_im = spread[:, (NW + w) * slots : (NW + w + 1) * slots]
            l_re, l_im = left[o, 2 * w], left[o, 2 * w + 1]
            part_out[o, 2 * w : 2 * w + 1, :] = jnp.sum(l_re * g_re - l_im * g_im, axis=0, keepdims=True)
            part_out[o, 2 * w + 1 : 2 * w + 2, :] = jnp.sum(
                l_re * g_im + l_im * g_re, axis=0, keepdims=True
            )
        part_out[o, 2 * NW :, :] = jnp.zeros((8 - 2 * NW, slots), jnp.float32)

    part_copies = []
    for d in range(1, plane_total):
        other, peer = plane_peer(d)
        part_copies.append(
            remote(
                part_out.at[lax.rem(other, owners)],
                part_in.at[plane],
                part_send.at[d],
                part_recv.at[d],
                peer,
            )
        )
    for copy in part_copies:
        copy.start()
    part_in[plane] = part_out[t]
    observed_in[p] = observed_out[...]
    for copy in observed_copies:
        copy.wait()
    observed = observed_in[0]
    for q in range(1, pols):
        observed = observed + observed_in[q]
    depth = depth_ref[...].astype(jnp.float32)
    for copy in part_copies:
        copy.wait()

    pred = []
    per_pol = part_in.shape[0] // NPOL
    for q in range(NPOL):
        block = part_in[q * per_pol]
        for o in range(1, per_pol):
            block = block + part_in[q * per_pol + o]
        pred.append(
            tuple(
                sum(depth[w : w + 1] * block[2 * w + c : 2 * w + c + 1] for w in range(NW))
                for c in range(2)
            )
        )
    gains = gains_ref[...]
    idents = idents_ref[...]
    residual, leading, trailing = model_terms(
        pred,
        [observed[k : k + 1] for k in range(2 * NPOL)],
        [gains[k : k + 1] for k in range(4)],
        [gains[4 + k : 5 + k] for k in range(4)],
        idents[3:4],
    )
    for k in range(3):
        record_out[k : k + 1, :] = idents[k : k + 1]
    for k in range(4):
        record_out[3 + k : 4 + k, :] = leading[k]
        record_out[7 + k : 8 + k, :] = trailing[k]
    record_out[11:, :] = jnp.zeros((5, slots), jnp.float32)
    record_copies = []
    for d in range(1, across_total):
        other, peer = across_peer(d)
        record_copies.append(
            remote(record_out, record_in.at[across], record_send.at[d], record_recv.at[d], peer)
        )
    for copy in record_copies:
        copy.start()
    record_in[across] = record_out[...]
    rest = jnp.concatenate(residual, axis=0)
    own_rest = jnp.zeros((2 * NPOL, quarter), jnp.float32)
    for q in range(pols):
        own_rest = jnp.where(p == q, rest[:, q * quarter : (q + 1) * quarter], own_rest)
    residual_ref[...] = own_rest
    for copy in record_copies:
        copy.wait()

    piece = jnp.concatenate([record_in[d] for d in range(across_total)], axis=1)
    own_count = grad_ref.shape[1]
    index = (z * pols + p) * owners + t
    mine = (index * own_count + lax.broadcasted_iota(jnp.int32, (own_count, 1), 0)).astype(
        jnp.float32
    )
    match_first = mine == piece[0:1]
    match_second = mine == piece[1:2]
    weighted = jnp.concatenate(
        [
            jnp.where(match_first, piece[3 + k : 4 + k], 0.0)
            + jnp.where(match_second, piece[7 + k : 8 + k], 0.0)
            for k in range(4)
        ],
        axis=0,
    )
    high = weighted.astype(jnp.bfloat16)
    low = (weighted - high.astype(jnp.float32)).astype(jnp.bfloat16)
    channel_ids = lax.broadcasted_iota(jnp.int32, (NCH, 1), 0).astype(jnp.float32)
    onehot = jnp.where(channel_ids == piece[2:3], 1.0, 0.0).astype(jnp.bfloat16)
    summed = nt_dot(high, onehot) + nt_dot(low, onehot)
    for k in range(4):
        grad_ref[k] = grad_scale * summed[k * own_count : (k + 1) * own_count]


def predict(sizes, own_count, *operands):
    subgrids, pols, owners = sizes
    contrib, lead = operands[0], operands[1]
    _, groups, rows, width = contrib.shape
    slots = lead.shape[0]
    vmem = pl.BlockSpec(memory_space=pltpu.VMEM)
    dma = lambda n: pltpu.SemaphoreType.DMA((n,))
    across_total, plane_total = subgrids * owners, pols * owners
    return pl.pallas_call(
        functools.partial(predict_kernel, sizes),
        out_shape=(
            jax.ShapeDtypeStruct((2 * NPOL, slots // pols), jnp.float32),
            jax.ShapeDtypeStruct((4, own_count, NCH), jnp.float32),
        ),
        in_specs=[vmem] * len(operands),
        out_specs=(vmem, vmem),
        scratch_shapes=[
            pltpu.VMEM(contrib.shape, jnp.bfloat16),
            pltpu.VMEM((FGRID * rows, 2 * SG), jnp.bfloat16),
            pltpu.VMEM((owners, 2, slots, SG), jnp.bfloat16),
            pltpu.VMEM((owners, 2 * NW * slots, 2 * SG), jnp.bfloat16),
            pltpu.VMEM((owners, 4, FGRID * rows, slots), jnp.float32),
            pltpu.VMEM((owners, 8, slots), jnp.float32),
            pltpu.VMEM((plane_total, 8, slots), jnp.float32),
            pltpu.VMEM((8, slots), jnp.float32),
            pltpu.VMEM((pols, 8, slots), jnp.float32),
            pltpu.VMEM((16, slots), jnp.float32),
            pltpu.VMEM((across_total, 16, slots), jnp.float32),
            dma(subgrids),
            dma(subgrids),
            dma(2),
            dma(2),
            dma(pols),
            dma(pols),
            dma(plane_total),
            dma(plane_total),
            dma(across_total),
            dma(across_total),
        ],
        compiler_params=pltpu.CompilerParams(
            collective_id=0, has_side_effects=True, vmem_limit_bytes=48 << 20
        ),
    )(*operands)


def folded_factors(subgrids):
    half = lambda odd, s, c: [s * 2 * MC + c * MC + k for k in range(odd, MC, 2)]
    order = []
    for odd in range(2):
        for first in range(0, subgrids, 2):
            for c in range(2):
                for s in ((first + 1, first) if odd else (first, first + 1)):
                    order += half(odd, s, c)
    p, q, cosine, sine = [t[:, order] for t in fourier_factors(subgrids)]
    return p[: len(p) // 2], q[: len(q) // 2], cosine, sine


def folded_second(second):
    split = second.reshape(SG, 2 * FGRID, MC // 2, 2)
    return np.concatenate([split[..., 0], split[..., 1]], axis=2).reshape(SG, 2 * SG)


def gather_lookups(block_ref, links_ref, gain_ref, gains_ref, idents_ref):
    blocks = block_ref.shape[2]
    slots = idents_ref.shape[1]
    span = slots + 128
    lane = lax.broadcasted_iota(jnp.int32, (1, slots), 1)
    place = lax.broadcasted_iota(jnp.int32, (span, slots), 0)
    lane_tall = lax.broadcasted_iota(jnp.int32, (span, slots), 1)
    begin = jnp.int32(0)
    member, picks, windows, tables = [], [], [], []
    channel = jnp.zeros((1, slots), jnp.float32)
    alive = jnp.zeros((1, slots), jnp.float32)
    for b in range(blocks):
        chosen, offset, amount = [block_ref[k, 0, b] for k in range(3)]
        row = jnp.minimum(lax.div(offset, 128), links_ref.shape[0] - span // 128)
        first = row * 128
        windows += [links_ref[row + k] for k in range(span // 128)]
        tables.append(gain_ref[chosen])
        inside = jnp.where((lane >= begin) & (lane < begin + amount), 1.0, 0.0)
        member.append(inside)
        alive += inside
        channel += inside * chosen.astype(jnp.float32)
        hit = place == lane_tall + (offset - first - begin)
        picks.append((jnp.where(hit, 1.0, 0.0) * inside).astype(jnp.bfloat16))
        begin = begin + amount
    links = jnp.concatenate(windows, axis=1)
    upper = links // 16
    lower = links - 16 * upper
    pieces = jnp.concatenate([upper, lower], axis=0).astype(jnp.float32).astype(jnp.bfloat16)
    found = jnp.dot(
        pieces, jnp.concatenate(picks, axis=0), preferred_element_type=jnp.float32
    )
    stations = 16.0 * found[0:2] + found[2:4]
    table = jnp.concatenate(tables, axis=0)
    high = table.astype(jnp.bfloat16)
    rest = table - high.astype(jnp.float32)
    middle = rest.astype(jnp.bfloat16)
    low = (rest - middle.astype(jnp.float32)).astype(jnp.bfloat16)
    split = jnp.concatenate([high, middle, low], axis=0)
    size = table.shape[0]
    names = lax.broadcasted_iota(jnp.int32, (table.shape[1], 1), 0).astype(jnp.float32)
    for side in range(2):
        pick = jnp.where(names == stations[side : side + 1], 1.0, 0.0).astype(jnp.bfloat16)
        three = jnp.dot(split, pick, preferred_element_type=jnp.float32)
        rows = three[:size] + three[size : 2 * size] + three[2 * size :]
        chosen = member[0] * rows[0:4]
        for b in range(1, blocks):
            chosen = chosen + member[b] * rows[4 * b : 4 * b + 4]
        gains_ref[4 * side : 4 * side + 4, :] = chosen
    idents_ref[0:2, :] = stations
    idents_ref[2:3, :] = channel
    idents_ref[3:4, :] = alive
    idents_ref[4:8, :] = jnp.zeros((4, slots), jnp.float32)


def fused_kernel(
    sizes,
    block_hbm,
    links_hbm,
    gain_hbm,
    p_hbm,
    q_hbm,
    c_hbm,
    s_hbm,
    x_hbm,
    lead_hbm,
    trail_hbm,
    depth_hbm,
    observed_hbm,
    table_re_hbm,
    table_im_hbm,
    second_hbm,
    chirp_hbm,
    residual_ref,
    grad_ref,
    block_ref,
    links_ref,
    gain_ref,
    p_ref,
    q_ref,
    c_ref,
    s_ref,
    x_ref,
    tapers,
    depths,
    observed_ref,
    table_ref,
    second_ref,
    chirp_ref,
    factors,
    contrib,
    got,
    right,
    left,
    gains_ref,
    idents_ref,
    side,
    part_out,
    part_in,
    observed_out,
    observed_in,
    rests,
    load_sem,
    chunk_sem,
    pair_send,
    pair_recv,
    chip_send,
    chip_recv,
    relay_send,
    relay_recv,
    far_send,
    far_recv,
    near_send,
    near_recv,
    observed_send,
    observed_recv,
    side_send,
    side_recv,
    part_send,
    part_recv,
):
    subgrids, pols, owners = sizes
    z, p, t = lax.axis_index("facet"), lax.axis_index("pol"), lax.axis_index("tm")
    _, _, slots, _ = tapers.shape
    facets, _, rows, length = x_ref.shape
    _, _, groups, _, width = contrib.shape
    side_z, own = lax.rem(z, 2), z // 2
    far = 1 - own
    pair_z = z + 1 - 2 * side_z
    far_z = z + 2 - 4 * own
    partner = lax.rem(t + 1, owners)
    mesh_id = pl.DeviceIdType.MESH

    def remote(src, dst, send, recv, peer):
        return pltpu.make_async_remote_copy(
            src_ref=src,
            dst_ref=dst,
            send_sem=send,
            recv_sem=recv,
            device_id=peer,
            device_id_type=mesh_id,
        )

    across_total = subgrids * owners
    across = z * owners + t

    def across_peer(d):
        other = lax.rem(across + d, across_total)
        return other, (other // owners, p, lax.rem(other, owners))

    barrier = pltpu.get_barrier_semaphore()
    greeted = [(pair_z, p, t), (far_z, p, t), (z, p, partner)]
    greeted += [(z, lax.rem(p + d, pols), t) for d in range(1, pols)]
    for peer in greeted:
        pl.semaphore_signal(barrier, inc=1, device_id=peer, device_id_type=mesh_id)

    offsets = [
        (dz, dp, dt)
        for dz in reversed(range(subgrids))
        for dp in reversed(range(pols))
        for dt in range(owners)
    ]
    offsets.remove((0, 0, 0))
    per_chunk = FGRID // PIECES
    chunks = facets // per_chunk
    x_loads = [
        pltpu.make_async_copy(
            x_hbm.at[pl.ds(c * per_chunk, per_chunk)],
            x_ref.at[pl.ds(c * per_chunk, per_chunk)],
            chunk_sem.at[c],
        )
        for c in range(chunks)
    ]
    pairs = [
        (c_hbm, c_ref),
        (s_hbm, s_ref),
        (p_hbm, p_ref),
        (q_hbm, q_ref),
        (trail_hbm, tapers.at[own, 0]),
        (lead_hbm, tapers.at[own, 1]),
        (depth_hbm, depths.at[own]),
        (observed_hbm, observed_ref),
        (chirp_hbm, chirp_ref),
        (second_hbm, second_ref),
        (table_re_hbm.at[pl.ds(own * 2 * groups, 2 * groups)], table_ref.at[0]),
        (table_im_hbm.at[pl.ds(own * 2 * groups, 2 * groups)], table_ref.at[1]),
        (block_hbm, block_ref),
        (links_hbm, links_ref),
        (gain_hbm, gain_ref),
    ]
    loads = [
        pltpu.make_async_copy(src, dst, load_sem.at[k]) for k, (src, dst) in enumerate(pairs)
    ]
    for copy in loads[4:9] + loads[:4]:
        copy.start()
    x_loads[0].start()
    for copy in x_loads[1:]:
        copy.start()
    for copy in loads[9:]:
        copy.start()

    for copy in loads[4:9]:
        copy.wait()
    quarter = observed_ref.shape[1]
    place = lax.broadcasted_iota(jnp.int32, (2 * NPOL, slots), 1)
    observed_out[...] = jnp.where(
        (place >= p * quarter) & (place < (p + 1) * quarter),
        jnp.concatenate([observed_ref[...]] * pols, axis=1),
        0.0,
    )
    pl.semaphore_wait(barrier, len(greeted))
    share = lambda q: pl.ds(pl.multiple_of(q * quarter, quarter), quarter)
    far_copies = [
        remote(
            tapers.at[own, side, share(p)],
            tapers.at[own, side, share(p)],
            far_send.at[side],
            far_recv.at[side],
            (far_z, p, t),
        )
        for side in range(2)
    ]
    far_copies.append(
        remote(depths.at[own], depths.at[own], far_send.at[2], far_recv.at[2], (far_z, p, t))
    )
    observed_copies = []
    for d in range(1, pols):
        q = lax.rem(p + d, pols)
        observed_copies.append(
            remote(
                observed_out, observed_in.at[p], observed_send.at[d], observed_recv.at[d], (z, q, t)
            )
        )
    for copy in far_copies + observed_copies:
        copy.start()
    others = pols - 1
    near_copies = [
        remote(
            tapers.at[far, side, share(p)],
            tapers.at[far, side, share(p)],
            near_send.at[others * side + d - 1],
            near_recv.at[others * side + d - 1],
            (z, lax.rem(p + d, pols), t),
        )
        for side in range(2)
        for d in (2, 1, 3)
    ]

    def forward(side):
        far_copies[side].wait_recv()
        for copy in near_copies[others * side : others * side + others]:
            copy.start()


    for copy in loads[:4]:
        copy.wait()
    spread = c_ref.shape[0]
    cosine, sine = c_ref[...], s_ref[...]
    half = length // 2
    for part in range(half // spread):
        factors[part * spread : (part + 1) * spread, :] = (
            p_ref[part : part + 1, :] * cosine + q_ref[part : part + 1, :] * sine
        ).astype(jnp.bfloat16)

    lane = lax.broadcasted_iota(jnp.int32, (rows, 2 * MC), 1)
    sign = jnp.where(lane < MC, -1.0, 1.0)
    front = lane % MC < MC // 2
    folded = factors.shape[1] // 2
    part_width = width // PIECES
    pair_copies, chip_copies, relay_copies = [], [], []
    for c in range(chunks):
        x_loads[c].wait()
        x = x_ref[c * per_chunk : (c + 1) * per_chunk].reshape(per_chunk * 2 * rows, length)
        totals = [
            jnp.dot(
                x[:, :half] + x[:, half:], factors[:, :folded], preferred_element_type=jnp.float32
            ),
            jnp.dot(
                x[:, :half] - x[:, half:], factors[:, folded:], preferred_element_type=jnp.float32
            ),
        ]
        group, piece = c // PIECES, c % PIECES
        for pair in range(subgrids // 2):
            cut = slice(pair * 2 * MC, (pair + 1) * 2 * MC)
            for f in range(per_chunk):
                even, odd = [
                    total[2 * f * rows : (2 * f + 1) * rows, cut]
                    + sign
                    * pltpu.roll(total[(2 * f + 1) * rows : (2 * f + 2) * rows, cut], MC, 1)
                    for total in totals
                ]
                place = slice(
                    (piece * per_chunk + f) * 2 * MC, (piece * per_chunk + f + 1) * 2 * MC
                )
                contrib[0, pair, group, :, place] = jnp.where(front, even, odd).astype(jnp.bfloat16)
                other = jnp.where(front, odd, even)
                other = jnp.where(
                    front,
                    pltpu.roll(other, 2 * MC - MC // 2, 1),
                    pltpu.roll(other, MC // 2, 1),
                )
                contrib[1, pair, group, :, place] = other.astype(jnp.bfloat16)
        lanes = pl.ds(piece * part_width, part_width)
        pair_copies.append(
            remote(
                contrib.at[1 - side_z, :, group, :, lanes],
                got.at[:, side_z, group, t, :, lanes],
                pair_send.at[c],
                pair_recv.at[c],
                (pair_z, p, t),
            )
        )
        chip_copies.append(
            remote(
                contrib.at[side_z, :, group, :, lanes],
                got.at[:, side_z, group, t, :, lanes],
                chip_send.at[c],
                chip_recv.at[c],
                (z, p, partner),
            )
        )
        relay_copies.append(
            remote(
                got.at[:, 1 - side_z, group, t, :, lanes],
                got.at[:, 1 - side_z, group, t, :, lanes],
                relay_send.at[c],
                relay_recv.at[c],
                (z, p, partner),
            )
        )
        pair_copies[c].start()
        chip_copies[c].start()
        if c == chunks - FORWARD:
            forward(0)

    for k in range(2):
        for group in range(groups):
            got[k, side_z, group, t] = contrib[side_z, k, group]
    for copy in loads[9:]:
        copy.wait()
    gather_lookups(block_ref, links_ref, gain_ref, gains_ref, idents_ref)
    observed_in[p] = observed_out[...]
    for copy in observed_copies:
        copy.wait()
    observed = observed_in[0]
    for q in range(1, pols):
        observed = observed + observed_in[q]
    side[across, 0:8] = gains_ref[...]
    side[across, 8:16] = observed
    side[across, 16:20] = idents_ref[0:4]
    side_copies = []
    for d in range(1, across_total):
        other, peer = across_peer(d)
        side_copies.append(
            remote(side.at[across], side.at[across], side_send.at[d], side_recv.at[d], peer)
        )
    forward(1)

    span = 2 * groups * owners * rows
    table_re = table_ref[0].reshape(span, SG)
    table_im = table_ref[1].reshape(span, SG)
    turn = jnp.where(
        lax.broadcasted_iota(jnp.int32, (3 * slots, 2 * MC), 1) < MC, -1.0, 1.0
    )

    def prepare_right(k):
        trail3 = chirped_rows(tapers[k, 0], chirp_ref)
        a = jnp.dot(trail3, second_ref[...], preferred_element_type=jnp.float32)
        b = jnp.concatenate(
            [
                turn * pltpu.roll(a[:, j * 2 * MC : (j + 1) * 2 * MC], MC, 1)
                for j in range(a.shape[1] // (2 * MC))
            ],
            axis=1,
        )
        n0, n1, n2 = slice(0, slots), slice(slots, 2 * slots), slice(2 * slots, 3 * slots)
        right[k, 0:slots, :] = a[n0].astype(jnp.bfloat16)
        right[k, slots : 2 * slots, :] = (a[n1] - b[n2]).astype(jnp.bfloat16)
        right[k, 2 * slots : 3 * slots, :] = b[n0].astype(jnp.bfloat16)
        right[k, 3 * slots : 4 * slots, :] = (b[n1] + a[n2]).astype(jnp.bfloat16)

    def prepare_left(k):
        n0, n1, n2 = slice(0, slots), slice(slots, 2 * slots), slice(2 * slots, 3 * slots)
        lead3 = chirped_rows(tapers[k, 1], chirp_ref)
        u = nt_dot(table_re, lead3)
        v = nt_dot(table_im, lead3)
        left[k, 0] = u[:, n0]
        left[k, 1] = v[:, n0]
        left[k, 2] = u[:, n1] - v[:, n2]
        left[k, 3] = u[:, n2] + v[:, n1]

    prepare_right(own)
    prepare_left(own)
    for pair, relay in zip(pair_copies[:-1], relay_copies[:-1]):
        pair.wait_recv()
        relay.start()
    chip_copies[-1].wait_recv()
    for copy in side_copies:
        copy.start()
    for copy in near_copies[:others]:
        copy.wait_recv()
    prepare_right(far)
    pair_copies[-1].wait_recv()
    relay_copies[-1].start()
    for copy in [far_copies[2]] + near_copies[others:]:
        copy.wait_recv()
    prepare_left(far)
    for copy in chip_copies[:-1] + relay_copies:
        copy.wait()
    chip_copies[-1].wait_send()
    for k in range(2):
        spread_v = nt_dot(got[k].reshape(span, width), right[k])
        weights = depths[k].astype(jnp.float32)
        sums = [0.0, 0.0]
        for w in range(NW):
            g_re = spread_v[:, w * slots : (w + 1) * slots]
            g_im = spread_v[:, (NW + w) * slots : (NW + w + 1) * slots]
            l_re, l_im = left[k, 2 * w], left[k, 2 * w + 1]
            weight = weights[w : w + 1]
            sums[0] += weight * jnp.sum(l_re * g_re - l_im * g_im, axis=0, keepdims=True)
            sums[1] += weight * jnp.sum(l_re * g_im + l_im * g_re, axis=0, keepdims=True)
        for c in range(2):
            part_out[2 * c + k : 2 * c + k + 1, :] = sums[c]

    part_copies = []
    for dz, dp, dt in offsets:
        peer_z = (z, pair_z, far_z, subgrids - 1 - z)[dz]
        peer = (peer_z, lax.rem(p + dp, pols), lax.rem(t + dt, owners))
        k = (dz * pols + dp) * owners + dt
        part_copies.append(
            remote(part_out, part_in.at[z, p, t], part_send.at[k], part_recv.at[k], peer)
        )
    for copy in part_copies:
        copy.start()
    part_in[z, p, t] = part_out[...]
    for copy in pair_copies + far_copies + near_copies:
        copy.wait_send()
    for copy in side_copies:
        copy.wait()

    own_count = grad_ref.shape[0]
    index = (z * pols + p) * owners + t
    mine = (index * own_count + lax.broadcasted_iota(jnp.int32, (own_count, 1), 0)).astype(
        jnp.float32
    )
    channel_ids = lax.broadcasted_iota(jnp.int32, (NCH, 1), 0).astype(jnp.float32)
    first_here = [jnp.where(mine == side[d, 16:17], 1.0, 0.0) for d in range(across_total)]
    second_here = [jnp.where(mine == side[d, 17:18], 1.0, 0.0) for d in range(across_total)]
    onehot = jnp.concatenate(
        [
            jnp.where(channel_ids == side[d, 18:19], 1.0, 0.0).astype(jnp.bfloat16)
            for d in range(across_total)
        ],
        axis=1,
    )
    column = lambda k: jnp.concatenate([side[d, k : k + 1] for d in range(across_total)], axis=0)
    gains = [column(k) for k in range(8)]
    observed = [column(8 + k) for k in range(8)]
    alive = column(19)
    for copy in part_copies:
        copy.wait()

    pred = []
    for q in range(NPOL):
        both = [[part_in[y, q, o] + part_in[y + 2, q, o] for o in range(owners)] for y in range(2)]
        pred.append(
            tuple(
                jnp.concatenate(
                    [
                        both[s % 2][o][2 * c + s // 2 : 2 * c + s // 2 + 1]
                        for s in range(subgrids)
                        for o in range(owners)
                    ],
                    axis=0,
                )
                for c in range(2)
            )
        )
    residual, leading, trailing = model_terms(pred, observed, gains[:4], gains[4:], alive)
    for k in range(2 * NPOL):
        rests[:, k : k + 1, :] = residual[k][:, None, :]
    rest = rests[across]
    own_rest = jnp.zeros((2 * NPOL, quarter), jnp.float32)
    for q in range(pols):
        own_rest = jnp.where(p == q, rest[:, q * quarter : (q + 1) * quarter], own_rest)
    residual_ref[...] = own_rest

    weighted = jnp.concatenate(
        [
            jnp.concatenate(
                [
                    first_here[d] * leading[k][d : d + 1]
                    + second_here[d] * trailing[k][d : d + 1]
                    for d in range(across_total)
                ],
                axis=1,
            )
            for k in range(4)
        ],
        axis=0,
    )
    high = weighted.astype(jnp.bfloat16)
    low = (weighted - high.astype(jnp.float32)).astype(jnp.bfloat16)
    summed = nt_dot(jnp.concatenate([high, low], axis=0), onehot)
    summed = summed[: high.shape[0]] + summed[high.shape[0] :]
    lane_group = lax.broadcasted_iota(jnp.int32, (own_count, 128), 1) // 32
    mixed = []
    for g in range(NCH // 32):
        base = g // 4 * 128
        built = None
        for k in range(4):
            block = summed[k * own_count : (k + 1) * own_count, base : base + 128]
            shift = 32 * (k - g % 4) % 128
            block = pltpu.roll(block, shift, 1) if shift else block
            built = block if built is None else jnp.where(lane_group == k, block, built)
        mixed.append(grad_scale * built)
    mixed = jnp.concatenate(mixed, axis=0)
    high = mixed.astype(jnp.bfloat16)
    low = (mixed - high.astype(jnp.float32)).astype(jnp.bfloat16)
    came = lax.broadcasted_iota(jnp.int32, (128, 128), 0)
    goes = lax.broadcasted_iota(jnp.int32, (128, 128), 1)
    order = jnp.where(goes == came % 32 * 4 + came // 32, 1.0, 0.0).astype(jnp.bfloat16)
    placed = jnp.dot(
        jnp.concatenate([high, low], axis=0), order, preferred_element_type=jnp.float32
    )
    placed = placed[: mixed.shape[0]] + placed[mixed.shape[0] :]
    for g in range(NCH // 32):
        grad_ref[:, g * 128 : (g + 1) * 128] = placed[g * own_count : (g + 1) * own_count]


def emit_kernel(residual_ref, grad_ref, residual_out, grad_out, sems):
    copies = [
        pltpu.make_async_copy(residual_ref, residual_out, sems.at[0]),
        pltpu.make_async_copy(grad_ref, grad_out, sems.at[1]),
    ]
    for copy in copies:
        copy.start()
    for copy in copies:
        copy.wait()


def fused(sizes, own_count, *operands):
    subgrids, pols, owners = sizes
    block_table, links, gains = operands[0:3]
    x, lead, trail, depth, observed = operands[7:12]
    facets, _, rows, length = x.shape
    slots = lead.shape[0]
    width = subgrids * 2 * MC
    spread = FS // MC
    groups = facets // FGRID
    chunks = facets // (FGRID // PIECES)
    hbm = pl.BlockSpec(memory_space=pltpu.HBM)
    vmem = pl.BlockSpec(memory_space=pltpu.VMEM)
    dma = lambda n: pltpu.SemaphoreType.DMA((n,))
    held = lambda a: pltpu.VMEM(a.shape, a.dtype)
    across_total, all_total = subgrids * owners, subgrids * pols * owners
    f32, bf16 = jnp.float32, jnp.bfloat16
    residual, grad = pl.pallas_call(
        functools.partial(fused_kernel, sizes),
        out_shape=(
            jax.ShapeDtypeStruct(observed.shape, f32),
            jax.ShapeDtypeStruct((own_count, 4 * NCH), f32),
        ),
        in_specs=[hbm] * len(operands),
        out_specs=(vmem, vmem),
        scratch_shapes=[
            pltpu.SMEM(block_table.shape, jnp.int32),
            held(links),
            held(gains),
            pltpu.VMEM((length // 2 // spread, width), f32),
            pltpu.VMEM((length // 2 // spread, width), f32),
            pltpu.VMEM((spread, width), f32),
            pltpu.VMEM((spread, width), f32),
            held(x),
            pltpu.VMEM((2, 2, slots, SG), bf16),
            pltpu.VMEM((2,) + depth.shape, bf16),
            held(observed),
            pltpu.VMEM((2, 2 * groups, owners, rows, SG), bf16),
            pltpu.VMEM((SG, 2 * SG), bf16),
            pltpu.VMEM((2, SG), f32),
            pltpu.VMEM((length // 2, width), bf16),
            pltpu.VMEM((2, 2, groups, rows, 2 * SG), bf16),
            pltpu.VMEM((2, 2, groups, owners, rows, 2 * SG), bf16),
            pltpu.VMEM((2, 2 * NW * slots, 2 * SG), bf16),
            pltpu.VMEM((2, 4, 2 * groups * owners * rows, slots), f32),
            pltpu.VMEM((8, slots), f32),
            pltpu.VMEM((8, slots), f32),
            pltpu.VMEM((across_total, 20, slots), f32),
            pltpu.VMEM((4, slots), f32),
            pltpu.VMEM((subgrids, pols, owners, 4, slots), f32),
            pltpu.VMEM((8, slots), f32),
            pltpu.VMEM((pols, 8, slots), f32),
            pltpu.VMEM((across_total, 8, slots), f32),
            dma(15),
            dma(chunks),
            dma(chunks),
            dma(chunks),
            dma(chunks),
            dma(chunks),
            dma(chunks),
            dma(chunks),
            dma(3),
            dma(3),
            dma(2 * pols - 2),
            dma(2 * pols - 2),
            dma(pols),
            dma(pols),
            dma(across_total),
            dma(across_total),
            dma(all_total),
            dma(all_total),
        ],
        compiler_params=pltpu.CompilerParams(
            collective_id=0, has_side_effects=True, vmem_limit_bytes=36 << 20
        ),
    )(*[pltpu.with_memory_space_constraint(a, pltpu.HBM) for a in operands])
    return pl.pallas_call(
        emit_kernel,
        out_shape=(
            jax.ShapeDtypeStruct(residual.shape, f32),
            jax.ShapeDtypeStruct(grad.shape, f32),
        ),
        in_specs=[vmem] * 2,
        out_specs=[hbm] * 2,
        scratch_shapes=[dma(2)],
        compiler_params=pltpu.CompilerParams(vmem_limit_bytes=1 << 20),
    )(residual, grad)


def on_device(
    tile_spectral_lines,
    taper_leading_axis,
    taper_trailing_axis,
    depth_layer_factors,
    measured_correlations,
    visibility_groups_table,
    antenna_links,
    complex_receiver_factors,
):
    sizes = tuple(lax.axis_size(name) for name in ("facet", "pol", "tm"))
    subgrids, pols, owners = sizes
    slots = taper_leading_axis.shape[2]
    quarter = measured_correlations.shape[3]
    rows = tile_spectral_lines.shape[3]

    block_table = visibility_groups_table.reshape(3, visibility_groups_table.shape[3])
    observed = measured_correlations.reshape(2 * NPOL, quarter)

    if tile_spectral_lines.shape[0] % FGRID == 0 and sizes == (4, NPOL, 2):
        table_re, table_im = [jnp.asarray(t) for t in subgrid_tables()[:2]]
        own_count = NST // (subgrids * pols * owners)
        residual, gain_grad = fused(
            sizes,
            own_count,
            visibility_groups_table.reshape(3, 1, visibility_groups_table.shape[3]),
            jnp.transpose(antenna_links.reshape(2, -1, 128), (1, 0, 2)),
            complex_receiver_factors,
            *[jnp.asarray(t) for t in folded_factors(subgrids)],
            tile_spectral_lines[:, 0],
            taper_leading_axis.reshape(slots, SG),
            taper_trailing_axis.reshape(slots, SG),
            depth_layer_factors.reshape(NW, slots),
            observed,
            table_re.reshape(FGRID, owners, rows, SG),
            table_im.reshape(FGRID, owners, rows, SG),
            jnp.asarray(folded_second(subgrid_tables()[2])),
            jnp.asarray(np.stack(chirp_line())),
        )
        return residual.reshape(1, 2 * NPOL, 1, quarter), gain_grad

    contrib, gains, idents = fourier(
        tile_spectral_lines[:, 0],
        subgrids,
        slots,
        block_table,
        antenna_links,
        complex_receiver_factors,
    )
    table_re, table_im, second = [jnp.asarray(t) for t in subgrid_tables()]
    cosine, sine = chirp_line()
    own_count = NST // (subgrids * pols * owners)
    residual, grad = predict(
        sizes,
        own_count,
        contrib,
        taper_leading_axis.reshape(slots, SG),
        taper_trailing_axis.reshape(slots, SG),
        depth_layer_factors.reshape(NW, slots),
        observed,
        gains,
        idents,
        table_re.reshape(FGRID, owners, rows, SG),
        table_im.reshape(FGRID, owners, rows, SG),
        second,
        jnp.asarray(np.stack([cosine, sine])),
    )
    gain_grad = jnp.transpose(grad, (1, 2, 0)).reshape(own_count, 4 * NCH)
    return residual.reshape(1, 2 * NPOL, 1, quarter), gain_grad


def solution(mesh):
    return jax.shard_map(
        on_device,
        mesh=mesh,
        in_specs=(
            P("facet", "pol", None, "tm", None),
            P("facet", "tm", None, None),
            P("facet", "tm", None, None),
            P("facet", "tm", None, None),
            P("facet", None, "tm", "pol"),
            P("facet", "tm", None, None),
            P(),
            P(),
        ),
        out_specs=(P("facet", None, "tm", "pol"), P(("facet", "pol", "tm"), None)),
        check_vma=False,
    )
```
